32 devices in a mesh: row: 4 (over z), col: 8 (over y, x, core).
Axes of the slice: x: 2, y: 2, z: 4, core: 2. Of those that a mesh axis runs over, the one named last changes fastest.
Arguments:
- activations: bfloat16 [256, 256, 384], P('row', 'col'), may hold values from -6 to 6
- cotangent: bfloat16 [256, 256, 384], P('row', 'col'), may hold values from -6 to 6
- first_gain: float32 [384], replicated, may hold values from 0.1 to 1.9
- joint_weight: bfloat16 [384, 1152], replicated, may hold values from -4 to 4, as said below
- output_weight: bfloat16 [384, 384], replicated, may hold values from -0.3125 to 0.3125
- second_gain: float32 [384], replicated, may hold values from 0.1 to 1.9
- expand_weight: bfloat16 [384, 1536], replicated, may hold values from -0.3125 to 0.3125
- reduce_weight: bfloat16 [1536, 384], replicated, may hold values from -0.15625 to 0.15625
Outputs:
- block_out: bfloat16 [256, 256, 384], P('row', 'col')
- grad_input: bfloat16 [256, 256, 384], P('row', 'col')
- grad_joint: float32 [384, 1152], replicated
- grad_project: float32 [384, 384], replicated
- grad_expand: float32 [384, 1536], replicated
- grad_reduce: float32 [1536, 384], replicated
- grad_first_gain: float32 [384], replicated
- grad_second_gain: float32 [384], replicated
The draws below stay inside these ranges and needn't reach their ends.
Inputs may be any that keep to these rules, and one draw needn't show every extreme that they name: `joint_weight`: Queries, keys and values side by side along the columns, each 384 wide, heads of 32 consecutive columns.
All inputs are finite; a program needn't handle non-finite values.
Results may differ from the reference program's by a relative error of at most 0.014.
The reference program's roundings to bfloat16 on the way count: a program that leaves them out, or rounds other values in their place, can miss the bound.
Values may be sent and summed in bfloat16 or wider, within the bound.
No kernel may reach another device: no remote copies, remote signals or barrier semaphores. Data moves between devices by JAX's collectives and lax.ppermute only.
A program may use at most 192 MiB of HBM per device.

```python
import math
import jax
import jax.numpy as jnp
from jax import lax

D = 384
HEADS = 12
FF = 1536
GRID = 16
IMG_H = 256
IMG_W = 256
STRIDE_H = 16
STRIDE_W = 16
POSITIONS = 65536


def draw_joint_weight(key, part):
    subkeys = jax.random.split(jax.random.fold_in(key, 7), 3)
    key_part = jnp.clip(jax.random.normal(subkeys[1], (D, D), jnp.float32), -4.0, 4.0) * D ** (-0.5)
    value_part = jnp.clip(jax.random.normal(subkeys[2], (D, D), jnp.float32), -4.0, 4.0) * D ** (-0.5)
    query_part = jnp.clip(jax.random.normal(subkeys[0], (D, D), jnp.float32), -4.0, 4.0) * D ** (-0.5)
    return jnp.concatenate([query_part, key_part, value_part], axis=1).astype(jnp.bfloat16)


def block_scale(own_key, extent, cuts, low, top_value):
    def one(position, shards_of):
        steps = jax.random.uniform(jax.random.fold_in(jax.random.fold_in(own_key, 6), position), (shards_of,), jnp.float32, low / len(cuts), top_value / len(cuts))
        return jnp.repeat(jnp.exp(steps), extent[position] // shards_of).reshape((-1,) + (1,) * (len(extent) - position - 1))

    loudness = one(*cuts[0])
    for cut in cuts[1:]:
        loudness = loudness * one(*cut)
    return loudness


def gaussian(key, extent, width, reach, cuts=(), dtype=jnp.bfloat16):
    values = width * jax.random.normal(key, extent, jnp.float32)
    if cuts:
        values = values * block_scale(key, extent, cuts, -0.22, 0.18)
    return jnp.clip(values, -reach, reach).astype(dtype)


def setup_inputs(seed: int = 0) -> dict:
    keys = jax.random.split(jax.random.key(seed), 9)
    activations = gaussian(keys[0], (IMG_H, IMG_W, D), 1.0, 6.0, ((0, 4), (1, 8)))
    cotangent = gaussian(keys[1], (IMG_H, IMG_W, D), 1.0, 6.0, ((0, 4), (1, 8)))
    first_gain = jnp.clip(1.0 + 0.18 * jax.random.normal(keys[2], (D,), jnp.float32), 0.1, 1.9)
    joint_weight = draw_joint_weight(jax.random.fold_in(keys[8], 71), 0)
    output_weight = gaussian(keys[4], (D, D), D ** -0.5, 0.3125)
    second_gain = jnp.clip(1.0 + 0.18 * jax.random.normal(keys[5], (D,), jnp.float32), 0.1, 1.9)
    expand_weight = gaussian(keys[6], (D, FF), D ** -0.5, 0.3125)
    reduce_weight = gaussian(keys[7], (FF, D), FF ** -0.5, 0.15625)
    return dict(activations=activations, cotangent=cotangent, first_gain=first_gain, joint_weight=joint_weight, output_weight=output_weight, second_gain=second_gain, expand_weight=expand_weight, reduce_weight=reduce_weight)


EPSILON = 1e-05
SQRT_HALF = 0.7071067811865476
INV_ROOT_TAU = 0.3989422804014327

def normalize(values):
    center = values - lax.optimization_barrier(jnp.mean(values, axis=-1, keepdims=True))
    inv_std = lax.rsqrt(lax.optimization_barrier(jnp.mean(center * center, axis=-1, keepdims=True)) + EPSILON)
    return (center * inv_std, inv_std)

def norm_back(grad_norm, gain_vec, normed, inv_std):
    scaled = grad_norm * gain_vec
    return inv_std * (scaled - lax.optimization_barrier(jnp.mean(scaled, axis=-1, keepdims=True)) - normed * lax.optimization_barrier(jnp.mean(scaled * normed, axis=-1, keepdims=True)))

def gelu_value(pre_act):
    return 0.5 * pre_act * (1.0 + jax.scipy.special.erf(pre_act * SQRT_HALF))

def gelu_slope(pre_act):
    return 0.5 * (1.0 + jax.scipy.special.erf(pre_act * SQRT_HALF)) + pre_act * jnp.exp(-0.5 * pre_act * pre_act) * INV_ROOT_TAU

def project_rows(inputs, gain_vec, weight):
    normed, inv_std = normalize(inputs)
    scaled = (normed * gain_vec).astype(jnp.bfloat16)
    triple = jnp.dot(scaled, weight, preferred_element_type=jnp.float32).astype(jnp.bfloat16)
    return (triple, scaled, normed, inv_std)

def split_heads(rows, feature_dim):
    return rows.reshape(rows.shape[0], rows.shape[1], HEADS, feature_dim // HEADS).astype(jnp.float32)

def attend(triple):
    feature_dim = triple.shape[-1] // 3
    queries = split_heads(triple[..., :feature_dim], feature_dim)
    key_rows = split_heads(triple[..., feature_dim:2 * feature_dim], feature_dim)
    value_rows = split_heads(triple[..., 2 * feature_dim:], feature_dim)
    score_scale = (feature_dim // HEADS) ** (-0.5)
    scores = jnp.einsum('bqhe,bkhe->bhqk', queries, key_rows) * score_scale
    row_max = lax.optimization_barrier(jnp.max(scores, axis=-1, keepdims=True))
    weights = jnp.exp(scores - row_max)
    weights = weights / lax.optimization_barrier(jnp.sum(weights, axis=-1, keepdims=True))
    return (weights, queries, key_rows, value_rows, score_scale)

def attend_forward(triple):
    weights, queries, key_rows, value_rows, score_scale = attend(triple)
    weights_b = weights.astype(jnp.bfloat16).astype(jnp.float32)
    mixed_rows = jnp.einsum('bhqk,bkhe->bqhe', weights_b, value_rows).astype(jnp.bfloat16)
    return mixed_rows.reshape(triple.shape[0], triple.shape[1], -1)

def attend_backward(triple, grad_mixed):
    weights, queries, key_rows, value_rows, score_scale = attend(triple)
    feature_dim = triple.shape[-1] // 3
    grad_heads = split_heads(grad_mixed, feature_dim)
    grad_weights = jnp.einsum('bqhe,bkhe->bhqk', grad_heads, value_rows)
    inner_sum = lax.optimization_barrier(jnp.sum(weights * grad_weights, axis=-1, keepdims=True))
    grad_scores = (weights * (grad_weights - inner_sum) * score_scale).astype(jnp.bfloat16).astype(jnp.float32)
    weights_b = weights.astype(jnp.bfloat16).astype(jnp.float32)
    grad_query = jnp.einsum('bhqk,bkhe->bqhe', grad_scores, key_rows).astype(jnp.bfloat16)
    grad_key = jnp.einsum('bhqk,bqhe->bkhe', grad_scores, queries).astype(jnp.bfloat16)
    grad_value = jnp.einsum('bhqk,bqhe->bkhe', weights_b, grad_heads).astype(jnp.bfloat16)
    shape_out = (triple.shape[0], triple.shape[1], feature_dim)
    return jnp.concatenate([grad_query.reshape(shape_out), grad_key.reshape(shape_out), grad_value.reshape(shape_out)], axis=-1)

def tail_back(inputs, mixed_rows, out_weight, gain_vec, up_weight, down_weight, cot_rows):
    attended = inputs + jnp.dot(mixed_rows, out_weight, preferred_element_type=jnp.float32)
    normed, inv_std = normalize(attended)
    scaled = (normed * gain_vec).astype(jnp.bfloat16)
    pre_act = jnp.dot(scaled, up_weight, preferred_element_type=jnp.float32)
    hidden = gelu_value(pre_act).astype(jnp.bfloat16)
    result = (attended + jnp.dot(hidden, down_weight, preferred_element_type=jnp.float32)).astype(jnp.bfloat16)
    grad_down = jnp.dot(hidden.T, cot_rows, preferred_element_type=jnp.float32)
    grad_hidden = jnp.dot(cot_rows, down_weight.T, preferred_element_type=jnp.float32).astype(jnp.bfloat16)
    grad_pre = (grad_hidden.astype(jnp.float32) * gelu_slope(pre_act)).astype(jnp.bfloat16)
    grad_up = jnp.dot(scaled.T, grad_pre, preferred_element_type=jnp.float32)
    grad_scaled = jnp.dot(grad_pre, up_weight.T, preferred_element_type=jnp.float32)
    grad_gain = lax.optimization_barrier(jnp.sum(grad_scaled * normed, axis=0))
    grad_attended = cot_rows.astype(jnp.float32) + norm_back(grad_scaled, gain_vec, normed, inv_std)
    grad_attended_b = grad_attended.astype(jnp.bfloat16)
    grad_out = jnp.dot(mixed_rows.T, grad_attended_b, preferred_element_type=jnp.float32)
    grad_mixed = jnp.dot(grad_attended_b, out_weight.T, preferred_element_type=jnp.float32).astype(jnp.bfloat16)
    return (result, grad_attended, grad_mixed, (grad_out, grad_gain, grad_up, grad_down))

def head_back(normed, inv_std, scaled, gain_vec, weight, grad_triple, grad_attended):
    grad_joint = jnp.dot(scaled.T, grad_triple, preferred_element_type=jnp.float32)
    grad_scaled = jnp.dot(grad_triple, weight.T, preferred_element_type=jnp.float32)
    grad_gain = lax.optimization_barrier(jnp.sum(grad_scaled * normed, axis=0))
    grad_input = (grad_attended + norm_back(grad_scaled, gain_vec, normed, inv_std)).astype(jnp.bfloat16)
    return (grad_input, (grad_joint, grad_gain))

def reference(activations, cotangent, first_gain, joint_weight, output_weight, second_gain, expand_weight, reduce_weight):
    group_count = STRIDE_H * STRIDE_W
    tokens = GRID * GRID
    per_step = math.gcd(group_count, 8)

    def regroup(tile):
        return tile.reshape(GRID, STRIDE_H, GRID, STRIDE_W, D).transpose(1, 3, 0, 2, 4).reshape(group_count // per_step, per_step * tokens, D)

    def restore(rows):
        return rows.reshape(STRIDE_H, STRIDE_W, GRID, GRID, D).transpose(2, 0, 3, 1, 4).reshape(IMG_H, IMG_W, D)

    def step_fn(running, pieces):
        act_rows, cot_rows = pieces
        inputs = act_rows.astype(jnp.float32)
        triple, scaled_first, normed_first, inv_first = project_rows(inputs, first_gain, joint_weight)
        triple_grp = triple.reshape(per_step, tokens, 3 * D)
        mixed_rows = attend_forward(triple_grp).reshape(-1, D)
        result, grad_attended, grad_mixed, tail_grads = tail_back(inputs, mixed_rows, output_weight, second_gain, expand_weight, reduce_weight, cot_rows)
        grad_triple = attend_backward(triple_grp, grad_mixed.reshape(per_step, tokens, D)).reshape(-1, 3 * D)
        grad_input, head_grads = head_back(normed_first, inv_first, scaled_first, first_gain, joint_weight, grad_triple, grad_attended)
        partials = head_grads + tail_grads
        running = tuple((old + new for old, new in zip(running, partials)))
        return (running, (result, grad_input))
    initial = (jnp.zeros((D, 3 * D), jnp.float32), jnp.zeros((D,), jnp.float32), jnp.zeros((D, D), jnp.float32), jnp.zeros((D,), jnp.float32), jnp.zeros((D, FF), jnp.float32), jnp.zeros((FF, D), jnp.float32))
    running, outputs = lax.scan(step_fn, initial, (regroup(activations), regroup(cotangent)))
    factor = POSITIONS ** (-0.5)
    grad_joint, grad_first, grad_project, grad_second, grad_expand, grad_reduce = running
    return (restore(outputs[0]), restore(outputs[1]), grad_joint * factor, grad_project * factor, grad_expand * factor, grad_reduce * factor, grad_first * factor, grad_second * factor)
```

```python
import functools

import jax
import jax.numpy as jnp
from jax import lax
from jax.experimental import pallas as pl
from jax.experimental.pallas import tpu as pltpu
from jax.sharding import PartitionSpec as P

HEADS = 12
GRID = 16
SUB = 8
EPSILON = 1e-05
INV_ROOT_TAU = 0.3989422804014327
SQRT_HALF = 0.7071067811865476
LOG2E = 1.4426950408889634
BF = jnp.bfloat16
F32 = jnp.float32

ERFC_P = 0.4
ERFC_C = (
    0.2256758624069583,
    0.22566957331484927,
    0.20784305752189558,
    0.16853970978283367,
    0.1414388899580775,
    -0.005621196233437842,
    0.16909944767289115,
    -0.18290897174728507,
    0.05026375199644912,
)


def nn(a, b):
    return lax.dot_general(a, b, (((1,), (0,)), ((), ())), preferred_element_type=F32)


def nt(a, b):
    return lax.dot_general(a, b, (((1,), (1,)), ((), ())), preferred_element_type=F32)


def tn(a, b):
    return lax.dot_general(a, b, (((0,), (0,)), ((), ())), preferred_element_type=F32)


def gelu_parts(pre):
    gauss = jnp.exp2(pre * pre * (-0.5 * LOG2E))
    t = 1.0 / (1.0 + (ERFC_P * SQRT_HALF) * jnp.abs(pre))
    poly = jnp.full_like(t, 0.5 * ERFC_C[-1])
    for coef in ERFC_C[-2::-1]:
        poly = poly * t + 0.5 * coef
    half_erfc = gauss * (t * poly)
    phi = jnp.where(pre < 0.0, half_erfc, 1.0 - half_erfc)
    return phi, gauss


def normalize(values):
    center = values - jnp.mean(values, axis=0, keepdims=True)
    inv_std = lax.rsqrt(jnp.mean(center * center, axis=0, keepdims=True) + EPSILON)
    return center * inv_std, inv_std


def norm_back(scaled, normed, inv_std):
    return inv_std * (
        scaled
        - jnp.mean(scaled, axis=0, keepdims=True)
        - normed * jnp.mean(scaled * normed, axis=0, keepdims=True)
    )


def load_rows(ref):
    pieces, _, sub, width = ref.shape
    return ref[...].reshape(pieces, sub, width).astype(F32).reshape(pieces * sub, width)


def store_rows(ref, rows):
    pieces, _, sub, width = ref.shape
    ref[...] = rows.reshape(pieces, 1, sub, width).astype(ref.dtype)


def fold_lanes(values):
    total = values[:, :128]
    for start in range(128, values.shape[1], 128):
        total = total + values[:, start : start + 128]
    return total


def attend_kernel(act_ref, gain_ref, joint_ref, flat_ref, triple_ref, mixed_ref):
    width = gain_ref.shape[0]
    head = width // HEADS
    factor = head ** (-0.5) * LOG2E
    flat = load_rows(act_ref).T
    flat_ref[0] = flat.astype(BF)
    normed, _ = normalize(flat)
    scaled = (normed * gain_ref[...]).astype(BF)
    triple_ref[0] = nn(joint_ref[...], scaled).astype(BF)
    for h in range(HEADS):
        rows = slice(h * head, (h + 1) * head)
        queries = triple_ref[0, h * head : (h + 1) * head]
        keys = triple_ref[0, width + h * head : width + (h + 1) * head]
        values = triple_ref[0, 2 * width + h * head : 2 * width + (h + 1) * head]
        scores = tn(keys, queries)
        weights = jnp.exp2((scores - jnp.max(scores, axis=0, keepdims=True)) * factor)
        weights = weights * (1.0 / jnp.sum(weights, axis=0, keepdims=True))
        mixed_ref[0, rows] = nn(values, weights.astype(BF)).astype(BF)


def mlp_kernel(
    flat_ref, mixed_ref, cot_ref, gain_ref, out_t_ref, up_t_ref, down_t_ref, down_ref, up_ref, out_w_ref,
    result_ref, grad_att_ref, grad_mixed_ref, grads_ref, grad_gain_ref,
    acc_ref,
):
    step = pl.program_id(0)
    width = gain_ref.shape[0]
    hidden_dim = up_ref.shape[1]

    @pl.when(step == 0)
    def _():
        acc_ref[...] = jnp.zeros_like(acc_ref)
        grad_gain_ref[...] = jnp.zeros_like(grad_gain_ref)

    cot_rows = load_rows(cot_ref)
    cot_b = cot_rows.astype(BF)
    cot_t = cot_rows.T
    cot_tb = cot_t.astype(BF)
    mixed = mixed_ref[0]
    attended = flat_ref[0].astype(F32) + nn(out_t_ref[...], mixed)
    normed, inv_std = normalize(attended)
    gain = gain_ref[...]
    scaled = (normed * gain).astype(BF)
    result = attended
    grad_scaled = jnp.zeros_like(attended)
    piece = width
    for start in range(0, hidden_dim, piece):
        part = slice(start, start + piece)
        pre = nn(up_t_ref[part], scaled)
        phi, gauss = gelu_parts(pre)
        hidden = (pre * phi).astype(BF)
        result = result + nn(down_t_ref[:, part], hidden)
        acc_ref[part] += nn(hidden, cot_b)
        grad_hidden = nn(down_ref[part], cot_tb).astype(BF).astype(F32)
        grad_pre = (grad_hidden * (phi + pre * gauss * INV_ROOT_TAU)).astype(BF)
        grad_scaled = grad_scaled + nn(up_ref[:, part], grad_pre)
        acc_ref[hidden_dim + start : hidden_dim + start + piece] += nt(grad_pre, scaled)
    store_rows(result_ref, result.T)
    grad_gain_ref[...] += fold_lanes(grad_scaled * normed)
    grad_att = cot_t + norm_back(grad_scaled * gain, normed, inv_std)
    grad_att_ref[0] = grad_att
    grad_att_b = grad_att.astype(BF)
    acc_ref[2 * hidden_dim :] += nt(mixed, grad_att_b)
    grad_mixed_ref[0] = nn(out_w_ref[...], grad_att_b).astype(BF)

    @pl.when(step == pl.num_programs(0) - 1)
    def _():
        grads_ref[...] = acc_ref[...].astype(BF)


def back_kernel(
    flat_ref, triple_ref, grad_mixed_ref, grad_att_ref, gain_ref, joint_ref,
    grad_in_ref, grads_ref, grad_gain_ref,
    acc_ref, grad_triple_ref,
):
    step = pl.program_id(0)
    width = gain_ref.shape[0]
    head = width // HEADS
    scale = head ** (-0.5)

    @pl.when(step == 0)
    def _():
        acc_ref[...] = jnp.zeros_like(acc_ref)
        grad_gain_ref[...] = jnp.zeros_like(grad_gain_ref)

    for h in range(HEADS):
        queries = triple_ref[0, h * head : (h + 1) * head]
        keys = triple_ref[0, width + h * head : width + (h + 1) * head]
        values = triple_ref[0, 2 * width + h * head : 2 * width + (h + 1) * head]
        grad_heads = grad_mixed_ref[0, h * head : (h + 1) * head]
        scores = tn(keys, queries)
        weights = jnp.exp2((scores - jnp.max(scores, axis=0, keepdims=True)) * (scale * LOG2E))
        weights = weights * (1.0 / jnp.sum(weights, axis=0, keepdims=True))
        grad_weights = tn(values, grad_heads)
        inner = jnp.sum(weights * grad_weights, axis=0, keepdims=True)
        grad_scores = (weights * (grad_weights - inner) * scale).astype(BF)
        grad_triple_ref[h * head : (h + 1) * head] = nn(keys, grad_scores).astype(BF)
        grad_triple_ref[width + h * head : width + (h + 1) * head] = nt(queries, grad_scores).astype(BF)
        grad_triple_ref[2 * width + h * head : 2 * width + (h + 1) * head] = nt(
            grad_heads, weights.astype(BF)
        ).astype(BF)
    normed, inv_std = normalize(flat_ref[0].astype(F32))
    gain = gain_ref[...]
    scaled = (normed * gain).astype(BF)
    acc_ref[...] += nt(grad_triple_ref[...], scaled)
    grad_scaled = nn(joint_ref[...], grad_triple_ref[...])
    grad_gain_ref[...] += fold_lanes(grad_scaled * normed)
    grad_in = grad_att_ref[0] + norm_back(grad_scaled * gain, normed, inv_std)
    store_rows(grad_in_ref, grad_in.T)

    @pl.when(step == pl.num_programs(0) - 1)
    def _():
        grads_ref[...] = acc_ref[...].astype(BF)


def whole(array):
    return pl.BlockSpec(array.shape, lambda g: (0,) * array.ndim)


def per_group(shape):
    return pl.BlockSpec((1,) + shape, lambda g: (g, 0, 0))


def pieces_spec(array):
    pieces, _, sub, width = array.shape
    return pl.BlockSpec((pieces, 1, sub, width), lambda g: (0, g, 0, 0))


def params():
    return pltpu.CompilerParams(dimension_semantics=("arbitrary",), vmem_limit_bytes=60 << 20)


def cost(flops, bytes_moved, exps):
    return pl.CostEstimate(flops=int(flops), bytes_accessed=int(bytes_moved), transcendentals=int(exps))


def attend_call(act, gain, joint_t):
    pieces, groups, sub, width = act.shape
    tokens = pieces * sub
    return pl.pallas_call(
        attend_kernel,
        grid=(groups,),
        in_specs=[pieces_spec(act), whole(gain), whole(joint_t)],
        out_specs=[per_group((width, tokens)), per_group((3 * width, tokens)), per_group((width, tokens))],
        out_shape=[
            jax.ShapeDtypeStruct((groups, width, tokens), BF),
            jax.ShapeDtypeStruct((groups, 3 * width, tokens), BF),
            jax.ShapeDtypeStruct((groups, width, tokens), BF),
        ],
        compiler_params=params(),
        cost_estimate=cost(3e9 * groups, 12 * groups * tokens * width, 0),
    )(act, gain, joint_t)


def mlp_call(flat, mixed, cot, gain, weights):
    pieces, groups, sub, width = cot.shape
    tokens = pieces * sub
    hidden_dim = weights[1].shape[0]
    rows = 2 * hidden_dim + width
    return pl.pallas_call(
        mlp_kernel,
        grid=(groups,),
        in_specs=[per_group((width, tokens)), per_group((width, tokens)), pieces_spec(cot), whole(gain)]
        + [whole(w) for w in weights],
        out_specs=[
            pieces_spec(cot),
            per_group((width, tokens)),
            per_group((width, tokens)),
            pl.BlockSpec((rows, width), lambda g: (0, 0)),
            pl.BlockSpec((width, 128), lambda g: (0, 0)),
        ],
        out_shape=[
            jax.ShapeDtypeStruct(cot.shape, BF),
            jax.ShapeDtypeStruct((groups, width, tokens), F32),
            jax.ShapeDtypeStruct((groups, width, tokens), BF),
            jax.ShapeDtypeStruct((rows, width), BF),
            jax.ShapeDtypeStruct((width, 128), F32),
        ],
        scratch_shapes=[pltpu.VMEM((rows, width), F32)],
        compiler_params=params(),
        cost_estimate=cost(4e9 * groups, 14 * groups * tokens * width, 0),
    )(flat, mixed, cot, gain, *weights)


def back_call(flat, triple, grad_mixed, grad_att, gain, joint, like):
    pieces, groups, sub, width = like.shape
    tokens = pieces * sub
    return pl.pallas_call(
        back_kernel,
        grid=(groups,),
        in_specs=[
            per_group((width, tokens)),
            per_group((3 * width, tokens)),
            per_group((width, tokens)),
            per_group((width, tokens)),
            whole(gain),
            whole(joint),
        ],
        out_specs=[
            pieces_spec(like),
            pl.BlockSpec((3 * width, width), lambda g: (0, 0)),
            pl.BlockSpec((width, 128), lambda g: (0, 0)),
        ],
        out_shape=[
            jax.ShapeDtypeStruct(like.shape, BF),
            jax.ShapeDtypeStruct((3 * width, width), BF),
            jax.ShapeDtypeStruct((width, 128), F32),
        ],
        scratch_shapes=[pltpu.VMEM((3 * width, width), F32), pltpu.VMEM((3 * width, tokens), BF)],
        compiler_params=params(),
        cost_estimate=cost(6e9 * groups, 18 * groups * tokens * width, 0),
    )(flat, triple, grad_mixed, grad_att, gain, joint)


def shards(
    activations,
    cotangent,
    first_gain,
    joint_weight,
    output_weight,
    second_gain,
    expand_weight,
    reduce_weight,
):
    row_devs = lax.axis_size("row")
    col_devs = lax.axis_size("col")
    devices = row_devs * col_devs
    both = ("row", "col")
    tile_rows, tile_cols, channels = activations.shape
    local_rows = GRID // row_devs
    local_cols = GRID // col_devs
    stride_rows = tile_rows // local_rows
    stride_cols = tile_cols // local_cols
    part_rows = stride_rows // row_devs
    part_cols = stride_cols // col_devs
    groups = part_rows * part_cols
    share = local_rows * local_cols
    tokens = GRID * GRID
    factor = float(tile_rows * tile_cols * devices) ** (-0.5)

    def scatter(tile):
        sends = tile.reshape(
            local_rows, row_devs, part_rows, local_cols, col_devs, part_cols, channels
        ).transpose(1, 4, 2, 5, 0, 3, 6).reshape(devices, groups, share, channels)
        got = lax.all_to_all(sends, both, split_axis=0, concat_axis=0, tiled=True)
        if share % SUB:
            got = got.transpose(0, 2, 1, 3).reshape(tokens // SUB, SUB, groups, channels).transpose(0, 2, 1, 3)
        return got.reshape(tokens // SUB, groups, SUB, channels)

    def gather(pieces):
        if share % SUB:
            pieces = pieces.transpose(0, 2, 1, 3).reshape(devices, share, groups, channels).transpose(0, 2, 1, 3)
        got = lax.all_to_all(
            pieces.reshape(devices, groups, share, channels), both, split_axis=0, concat_axis=0, tiled=True
        )
        return got.reshape(
            row_devs, col_devs, part_rows, part_cols, local_rows, local_cols, channels
        ).transpose(4, 0, 2, 5, 1, 3, 6).reshape(tile_rows, tile_cols, channels)

    def total(partial):
        rows, width = partial.shape
        by_col = rows // col_devs
        by_row = by_col // row_devs
        got = lax.all_to_all(partial.reshape(col_devs, by_col, width), "col", 0, 0, tiled=True)
        mine = jnp.sum(got.astype(F32), axis=0).astype(BF)
        got = lax.all_to_all(mine.reshape(row_devs, by_row, width), "row", 0, 0, tiled=True)
        mine = jnp.sum(got.astype(F32), axis=0).astype(BF)
        got = lax.all_to_all(
            jnp.broadcast_to(mine[None], (row_devs, by_row, width)), "row", 0, 0, tiled=True
        ).reshape(by_col, width)
        got = lax.all_to_all(
            jnp.broadcast_to(got[None], (col_devs, by_col, width)), "col", 0, 0, tiled=True
        )
        return got.reshape(rows, width).astype(F32) * factor

    def spread(gain):
        return jnp.broadcast_to(gain[:, None], (channels, tokens))

    act = scatter(activations)
    cot = scatter(cotangent)
    gain_one, gain_two = spread(first_gain), spread(second_gain)
    flat, triple, mixed = attend_call(act, gain_one, joint_weight.T)
    result, grad_att, grad_mixed, tail_grads, grad_second = mlp_call(
        flat,
        mixed,
        cot,
        gain_two,
        (output_weight.T, expand_weight.T, reduce_weight.T, reduce_weight, expand_weight, output_weight),
    )
    block_out = gather(result)
    tail_sum = total(tail_grads)
    grad_in, head_grads, grad_first = back_call(
        flat, triple, grad_mixed, grad_att, gain_one, joint_weight, cot
    )
    grad_input = gather(grad_in)
    head_sum = total(head_grads)
    gains = jnp.stack([jnp.sum(grad_first, axis=1), jnp.sum(grad_second, axis=1)])
    gains = lax.all_to_all(
        jnp.broadcast_to(gains[None], (devices,) + gains.shape), both, 0, 0, tiled=True
    )
    gains = jnp.sum(gains, axis=0) * factor
    hidden_dim = expand_weight.shape[1]
    return (
        block_out,
        grad_input,
        head_sum.T,
        tail_sum[2 * hidden_dim :],
        tail_sum[hidden_dim : 2 * hidden_dim].T,
        tail_sum[:hidden_dim],
        gains[0],
        gains[1],
    )


def solution(mesh):
    placed = (P("row", "col", None), P("row", "col", None), P(), P(), P(), P(), P(), P())
    return jax.shard_map(
        shards,
        mesh=mesh,
        in_specs=placed,
        out_specs=placed,
        check_vma=False,
    )
```

```python
import jax
import jax.numpy as jnp
from jax import lax
from jax.experimental import pallas as pl
from jax.experimental.pallas import tpu as pltpu
from jax.sharding import PartitionSpec as P


HEADS = 12
GRID = 16
SUB = 8
EPSILON = 1e-05
INV_ROOT_TAU = 0.3989422804014327
SQRT_HALF = 0.7071067811865476
LOG2E = 1.4426950408889634
BF = jnp.bfloat16
F32 = jnp.float32

ERFC_P = 0.4
ERFC_C = (
    0.2256758624069583,
    0.22566957331484927,
    0.20784305752189558,
    0.16853970978283367,
    0.1414388899580775,
    -0.005621196233437842,
    0.16909944767289115,
    -0.18290897174728507,
    0.05026375199644912,
)


def nn(a, b):
    return lax.dot_general(a, b, (((1,), (0,)), ((), ())), preferred_element_type=F32)


def nt(a, b):
    return lax.dot_general(a, b, (((1,), (1,)), ((), ())), preferred_element_type=F32)


def tn(a, b):
    return lax.dot_general(a, b, (((0,), (0,)), ((), ())), preferred_element_type=F32)


def gelu_parts(pre):
    gauss = jnp.exp2(pre * pre * (-0.5 * LOG2E))
    t = 1.0 / (1.0 + (ERFC_P * SQRT_HALF) * jnp.abs(pre))
    poly = jnp.full_like(t, 0.5 * ERFC_C[-1])
    for coef in ERFC_C[-2::-1]:
        poly = poly * t + 0.5 * coef
    half_erfc = gauss * (t * poly)
    phi = jnp.where(pre < 0.0, half_erfc, 1.0 - half_erfc)
    return phi, gauss


def normalize(values):
    center = values - jnp.mean(values, axis=0, keepdims=True)
    inv_std = lax.rsqrt(jnp.mean(center * center, axis=0, keepdims=True) + EPSILON)
    return center * inv_std, inv_std


def norm_back(scaled, normed, inv_std):
    return inv_std * (
        scaled
        - jnp.mean(scaled, axis=0, keepdims=True)
        - normed * jnp.mean(scaled * normed, axis=0, keepdims=True)
    )


def load_rows(ref):
    pieces, _, sub, width = ref.shape
    return ref[...].reshape(pieces, sub, width).astype(F32).reshape(pieces * sub, width)


def store_rows(ref, rows):
    pieces, _, sub, width = ref.shape
    ref[...] = rows.reshape(pieces, 1, sub, width).astype(ref.dtype)


def fold_lanes(values):
    total = values[:, :128]
    for start in range(128, values.shape[1], 128):
        total = total + values[:, start : start + 128]
    return total


def begin(carried, acc_ref, grad_gain_ref):
    if carried:
        acc_ref[...] = carried[0][...]
        grad_gain_ref[...] = carried[1][...]
    else:
        acc_ref[...] = jnp.zeros_like(acc_ref)
        grad_gain_ref[...] = jnp.zeros_like(grad_gain_ref)


def finish(acc_ref, grads_ref, grad_gain_ref):
    rows = acc_ref.shape[0]
    grads_ref[:rows] = acc_ref[...].astype(grads_ref.dtype)
    if grads_ref.shape[0] > rows:
        gains = jnp.sum(grad_gain_ref[...].T, axis=0, keepdims=True)
        spare = grads_ref.shape[0] - rows
        first = lax.broadcasted_iota(jnp.int32, (spare, gains.shape[1]), 0) == 0
        grads_ref[rows:] = jnp.where(first, gains, 0.0).astype(grads_ref.dtype)


def attend_kernel(act_ref, gain_ref, joint_ref, flat_ref, triple_ref, mixed_ref):
    width = gain_ref.shape[0]
    head = width // HEADS
    factor = head ** (-0.5) * LOG2E
    flat = load_rows(act_ref).T
    flat_ref[0] = flat.astype(BF)
    normed, _ = normalize(flat)
    scaled = (normed * gain_ref[...]).astype(BF)
    triple_ref[0] = nn(joint_ref[...], scaled).astype(BF)
    for h in range(HEADS):
        rows = slice(h * head, (h + 1) * head)
        queries = triple_ref[0, h * head : (h + 1) * head]
        keys = triple_ref[0, width + h * head : width + (h + 1) * head]
        values = triple_ref[0, 2 * width + h * head : 2 * width + (h + 1) * head]
        scores = tn(keys, queries)
        weights = jnp.exp2((scores - jnp.max(scores, axis=0, keepdims=True)) * factor)
        weights = weights * (1.0 / jnp.sum(weights, axis=0, keepdims=True))
        mixed_ref[0, rows] = nn(values, weights.astype(BF)).astype(BF)


def mlp_kernel(
    flat_ref, mixed_ref, cot_ref, gain_ref, out_t_ref, up_t_ref, down_t_ref, down_ref, up_ref, out_w_ref,
    *rest,
):
    carried = rest[:-6]
    result_ref, grad_att_ref, grad_mixed_ref, grads_ref, grad_gain_ref, acc_ref = rest[-6:]
    step = pl.program_id(0)
    width = gain_ref.shape[0]
    hidden_dim = up_ref.shape[1]

    @pl.when(step == 0)
    def _():
        begin(carried, acc_ref, grad_gain_ref)

    cot_rows = load_rows(cot_ref)
    cot_b = cot_rows.astype(BF)
    cot_t = cot_rows.T
    cot_tb = cot_t.astype(BF)
    mixed = mixed_ref[0]
    attended = flat_ref[0].astype(F32) + nn(out_t_ref[...], mixed)
    normed, inv_std = normalize(attended)
    gain = gain_ref[...]
    scaled = (normed * gain).astype(BF)
    result = attended
    grad_scaled = jnp.zeros_like(attended)
    piece = width
    for start in range(0, hidden_dim, piece):
        part = slice(start, start + piece)
        pre = nn(up_t_ref[part], scaled)
        phi, gauss = gelu_parts(pre)
        hidden = (pre * phi).astype(BF)
        result = result + nn(down_t_ref[:, part], hidden)
        acc_ref[part] += nn(hidden, cot_b)
        grad_hidden = nn(down_ref[part], cot_tb).astype(BF).astype(F32)
        grad_pre = (grad_hidden * (phi + pre * gauss * INV_ROOT_TAU)).astype(BF)
        grad_scaled = grad_scaled + nn(up_ref[:, part], grad_pre)
        acc_ref[hidden_dim + start : hidden_dim + start + piece] += nt(grad_pre, scaled)
    store_rows(result_ref, result.T)
    grad_gain_ref[...] += fold_lanes(grad_scaled * normed)
    grad_att = cot_t + norm_back(grad_scaled * gain, normed, inv_std)
    grad_att_ref[0] = grad_att
    grad_att_b = grad_att.astype(BF)
    acc_ref[2 * hidden_dim :] += nt(mixed, grad_att_b)
    grad_mixed_ref[0] = nn(out_w_ref[...], grad_att_b).astype(BF)

    @pl.when(step == pl.num_programs(0) - 1)
    def _():
        finish(acc_ref, grads_ref, grad_gain_ref)


def back_kernel(
    flat_ref, triple_ref, grad_mixed_ref, grad_att_ref, gain_ref, joint_ref,
    *rest,
):
    carried = rest[:-5]
    grad_in_ref, grads_ref, grad_gain_ref, acc_ref, grad_triple_ref = rest[-5:]
    step = pl.program_id(0)
    width = gain_ref.shape[0]
    head = width // HEADS
    scale = head ** (-0.5)

    @pl.when(step == 0)
    def _():
        begin(carried, acc_ref, grad_gain_ref)

    for h in range(HEADS):
        queries = triple_ref[0, h * head : (h + 1) * head]
        keys = triple_ref[0, width + h * head : width + (h + 1) * head]
        values = triple_ref[0, 2 * width + h * head : 2 * width + (h + 1) * head]
        grad_heads = grad_mixed_ref[0, h * head : (h + 1) * head]
        scores = tn(keys, queries)
        weights = jnp.exp2((scores - jnp.max(scores, axis=0, keepdims=True)) * (scale * LOG2E))
        weights = weights * (1.0 / jnp.sum(weights, axis=0, keepdims=True))
        grad_weights = tn(values, grad_heads)
        inner = jnp.sum(weights * grad_weights, axis=0, keepdims=True)
        grad_scores = (weights * (grad_weights - inner) * scale).astype(BF)
        grad_triple_ref[h * head : (h + 1) * head] = nn(keys, grad_scores).astype(BF)
        grad_triple_ref[width + h * head : width + (h + 1) * head] = nt(queries, grad_scores).astype(BF)
        grad_triple_ref[2 * width + h * head : 2 * width + (h + 1) * head] = nt(
            grad_heads, weights.astype(BF)
        ).astype(BF)
    normed, inv_std = normalize(flat_ref[0].astype(F32))
    gain = gain_ref[...]
    scaled = (normed * gain).astype(BF)
    acc_ref[...] += nt(grad_triple_ref[...], scaled)
    grad_scaled = nn(joint_ref[...], grad_triple_ref[...])
    grad_gain_ref[...] += fold_lanes(grad_scaled * normed)
    grad_in = grad_att_ref[0] + norm_back(grad_scaled * gain, normed, inv_std)
    store_rows(grad_in_ref, grad_in.T)

    @pl.when(step == pl.num_programs(0) - 1)
    def _():
        finish(acc_ref, grads_ref, grad_gain_ref)


def whole(array):
    return pl.BlockSpec(array.shape, lambda g: (0,) * array.ndim)


def per_group(shape):
    return pl.BlockSpec((1,) + shape, lambda g: (g, 0, 0))


def pieces_spec(array):
    pieces, _, sub, width = array.shape
    return pl.BlockSpec((pieces, 1, sub, width), lambda g: (0, g, 0, 0))


def params():
    return pltpu.CompilerParams(dimension_semantics=("arbitrary",), vmem_limit_bytes=60 << 20)


def cost(flops, bytes_moved, exps):
    return pl.CostEstimate(flops=int(flops), bytes_accessed=int(bytes_moved), transcendentals=int(exps))


def attend_call(act, gain, joint_t):
    pieces, groups, sub, width = act.shape
    tokens = pieces * sub
    return pl.pallas_call(
        attend_kernel,
        grid=(groups,),
        in_specs=[pieces_spec(act), whole(gain), whole(joint_t)],
        out_specs=[per_group((width, tokens)), per_group((3 * width, tokens)), per_group((width, tokens))],
        out_shape=[
            jax.ShapeDtypeStruct((groups, width, tokens), BF),
            jax.ShapeDtypeStruct((groups, 3 * width, tokens), BF),
            jax.ShapeDtypeStruct((groups, width, tokens), BF),
        ],
        compiler_params=params(),
        cost_estimate=cost(3e9 * groups, 12 * groups * tokens * width, 0),
    )(act, gain, joint_t)


def mlp_call(flat, mixed, cot, gain, weights, carried, spare):
    pieces, groups, sub, width = cot.shape
    tokens = pieces * sub
    hidden_dim = weights[1].shape[0]
    rows = 2 * hidden_dim + width
    return pl.pallas_call(
        mlp_kernel,
        grid=(groups,),
        in_specs=[per_group((width, tokens)), per_group((width, tokens)), pieces_spec(cot), whole(gain)]
        + [whole(w) for w in weights + carried],
        out_specs=[
            pieces_spec(cot),
            per_group((width, tokens)),
            per_group((width, tokens)),
            pl.BlockSpec((rows + spare, width), lambda g: (0, 0)),
            pl.BlockSpec((width, 128), lambda g: (0, 0)),
        ],
        out_shape=[
            jax.ShapeDtypeStruct(cot.shape, BF),
            jax.ShapeDtypeStruct((groups, width, tokens), F32),
            jax.ShapeDtypeStruct((groups, width, tokens), BF),
            jax.ShapeDtypeStruct((rows + spare, width), BF if spare else F32),
            jax.ShapeDtypeStruct((width, 128), F32),
        ],
        scratch_shapes=[pltpu.VMEM((rows, width), F32)],
        compiler_params=params(),
        cost_estimate=cost(4e9 * groups, 14 * groups * tokens * width, 0),
    )(flat, mixed, cot, gain, *weights, *carried)


def back_call(flat, triple, grad_mixed, grad_att, gain, joint, like, carried, spare):
    rows = joint.shape[1]
    pieces, groups, sub, width = like.shape
    tokens = pieces * sub
    return pl.pallas_call(
        back_kernel,
        grid=(groups,),
        in_specs=[
            per_group((width, tokens)),
            per_group((3 * width, tokens)),
            per_group((width, tokens)),
            per_group((width, tokens)),
            whole(gain),
            whole(joint),
        ]
        + [whole(w) for w in carried],
        out_specs=[
            pieces_spec(like),
            pl.BlockSpec((rows + spare, width), lambda g: (0, 0)),
            pl.BlockSpec((width, 128), lambda g: (0, 0)),
        ],
        out_shape=[
            jax.ShapeDtypeStruct(like.shape, BF),
            jax.ShapeDtypeStruct((rows + spare, width), BF if spare else F32),
            jax.ShapeDtypeStruct((width, 128), F32),
        ],
        scratch_shapes=[pltpu.VMEM((3 * width, width), F32), pltpu.VMEM((3 * width, tokens), BF)],
        compiler_params=params(),
        cost_estimate=cost(6e9 * groups, 18 * groups * tokens * width, 0),
    )(flat, triple, grad_mixed, grad_att, gain, joint, *carried)


def tie(value, *after):
    return lax.optimization_barrier((value,) + after)[0]


def peers(axis, low, high):
    return lax.axis_index(axis) // (1 << low) % (1 << (high - low)), 1 << (high - low)


def swap(values, axis, offset):
    return lax.ppermute(values, axis, [(i, i ^ offset) for i in range(lax.axis_size(axis))])


def scatter_sum(values, axis, low, high):
    mine, count = peers(axis, low, high)
    parts = values.reshape((count, values.shape[0] // count) + values.shape[1:])
    total = lax.dynamic_index_in_dim(parts, mine, 0, keepdims=False).astype(F32)
    for other in range(1, count):
        part = lax.dynamic_index_in_dim(parts, mine ^ other, 0, keepdims=False)
        total = total + swap(part, axis, other << low).astype(F32)
    return total.astype(BF)


def collect(values, axis, low, high):
    mine, count = peers(axis, low, high)
    got = jnp.stack([values] + [swap(values, axis, other << low) for other in range(1, count)])
    return jnp.concatenate(
        [lax.dynamic_index_in_dim(got, slot ^ mine, 0, keepdims=False) for slot in range(count)]
    )


def stages():
    row_bits = lax.axis_size("row").bit_length() - 1
    col_bits = lax.axis_size("col").bit_length() - 1
    return (("col", 0, 1), ("col", 1, col_bits), ("row", 0, row_bits))


def shards(
    activations,
    cotangent,
    first_gain,
    joint_weight,
    output_weight,
    second_gain,
    expand_weight,
    reduce_weight,
):
    row_devs = lax.axis_size("row")
    col_devs = lax.axis_size("col")
    devices = row_devs * col_devs
    both = ("row", "col")
    tile_rows, tile_cols, channels = activations.shape
    local_rows = GRID // row_devs
    local_cols = GRID // col_devs
    stride_rows = tile_rows // local_rows
    stride_cols = tile_cols // local_cols
    part_rows = stride_rows // row_devs
    part_cols = stride_cols // col_devs
    share = local_rows * local_cols
    tokens = GRID * GRID
    factor = float(tile_rows * tile_cols * devices) ** (-0.5)

    chunks = 2
    chunk_rows = part_rows // chunks
    chunk_groups = chunk_rows * part_cols

    def scatter(tile, chunk, *after):
        sends = tile.reshape(
            local_rows, row_devs, part_rows, local_cols, col_devs, part_cols, channels
        )[:, :, chunk * chunk_rows : (chunk + 1) * chunk_rows]
        sends = sends.transpose(1, 4, 2, 5, 0, 3, 6).reshape(devices, chunk_groups, share, channels)
        got = lax.all_to_all(tie(sends, *after), both, split_axis=0, concat_axis=0, tiled=True)
        if share % SUB:
            got = got.transpose(0, 2, 1, 3).reshape(tokens // SUB, SUB, chunk_groups, channels)
            got = got.transpose(0, 2, 1, 3)
        return got.reshape(tokens // SUB, chunk_groups, SUB, channels)

    def give_back(pieces, *after):
        if share % SUB:
            pieces = pieces.transpose(0, 2, 1, 3).reshape(devices, share, chunk_groups, channels)
            pieces = pieces.transpose(0, 2, 1, 3)
        pieces = tie(pieces.reshape(devices, chunk_groups, share, channels), *after)
        return lax.all_to_all(pieces, both, split_axis=0, concat_axis=0, tiled=True)

    def to_tile(arrived):
        arrived = [
            part.reshape(row_devs, col_devs, chunk_rows, part_cols, local_rows, local_cols, channels)
            for part in arrived
        ]
        return jnp.concatenate(arrived, axis=2).transpose(4, 0, 2, 5, 1, 3, 6).reshape(
            tile_rows, tile_cols, channels
        )

    def spread(gain):
        return jnp.broadcast_to(gain[:, None], (channels, tokens))

    act, cot = [], []
    for kind, tile in ((act, activations), (cot, cotangent)):
        for k in range(chunks):
            before = (act + cot)[-1:]
            kind.append(scatter(tile, k, *before))
    gain_one, gain_two = spread(first_gain), spread(second_gain)
    joint_t = joint_weight.T
    weights = (
        output_weight.T, expand_weight.T, reduce_weight.T, reduce_weight, expand_weight, output_weight
    )
    hidden_dim = expand_weight.shape[1]
    tail_rows, head_rows = 2 * hidden_dim + channels, 3 * channels
    unit = SUB * devices
    fronts = []
    for k in range(chunks):
        fronts.append(attend_call(act[k], gain_one, joint_t))
    tails, out_parts, carried = [], [], ()
    before = cot[-1:]
    for k in range(chunks):
        flat, _, mixed = fronts[k]
        spare = unit - tail_rows % unit if k == chunks - 1 else 0
        tails.append(mlp_call(flat, mixed, cot[k], gain_two, weights, carried, spare))
        carried = tails[-1][3:]
        out_parts.append(give_back(tails[-1][0], *before))
        before = out_parts[-1:]
    steps = stages()
    tail_sum = carried[0]
    heads, in_parts, carried = [], [], ()
    for k in range(chunks):
        flat, triple, _ = fronts[k]
        _, grad_att, grad_mixed = tails[k][:3]
        spare = unit - head_rows % unit if k == chunks - 1 else 0
        grad_mixed = tie(grad_mixed, out_parts[k], *((tail_sum,) if k else ()))
        heads.append(
            back_call(flat, triple, grad_mixed, grad_att, gain_one, joint_weight, cot[k], carried, spare)
        )
        carried = heads[-1][1:]
        in_parts.append(give_back(heads[-1][0], *before))
        before = in_parts[-1:]
        if k < len(steps):
            tail_sum = scatter_sum(tail_sum, *steps[k])
    head_sum = tie(carried[0], tail_sum)
    for k, stage in enumerate(steps):
        head_sum = scatter_sum(head_sum, *stage)
        if k >= chunks:
            tail_sum = scatter_sum(tail_sum, *stage)
    for stage in steps[::-1]:
        head_sum = collect(head_sum, *stage)
        tail_sum = collect(tail_sum, *stage)
    block_out, grad_input = to_tile(out_parts), to_tile(in_parts)
    head_sum = head_sum.astype(F32) * factor
    tail_sum = tail_sum.astype(F32) * factor
    return (
        block_out,
        grad_input,
        head_sum[:head_rows].T,
        tail_sum[2 * hidden_dim : tail_rows],
        tail_sum[hidden_dim : 2 * hidden_dim].T,
        tail_sum[:hidden_dim],
        head_sum[head_rows],
        tail_sum[tail_rows],
    )


def solution(mesh):
    placed = (P("row", "col", None), P("row", "col", None), P(), P(), P(), P(), P(), P())
    return jax.shard_map(shards, mesh=mesh, in_specs=placed, out_specs=placed, check_vma=False)
```

```python
import jax
import jax.numpy as jnp
from jax import lax
from jax.experimental import pallas as pl
from jax.experimental.pallas import tpu as pltpu
from jax.sharding import PartitionSpec as P


HEADS = 12
GRID = 16
SUB = 8
EPSILON = 1e-05
INV_ROOT_TAU = 0.3989422804014327
SQRT_HALF = 0.7071067811865476
LOG2E = 1.4426950408889634
BF = jnp.bfloat16
F32 = jnp.float32

ERFC_P = 0.4
ERFC_C = (
    0.2256758624069583,
    0.22566957331484927,
    0.20784305752189558,
    0.16853970978283367,
    0.1414388899580775,
    -0.005621196233437842,
    0.16909944767289115,
    -0.18290897174728507,
    0.05026375199644912,
)


def nn(a, b):
    return lax.dot_general(a, b, (((1,), (0,)), ((), ())), preferred_element_type=F32)


def nt(a, b):
    return lax.dot_general(a, b, (((1,), (1,)), ((), ())), preferred_element_type=F32)


def tn(a, b):
    return lax.dot_general(a, b, (((0,), (0,)), ((), ())), preferred_element_type=F32)


def gelu_parts(pre):
    gauss = jnp.exp2(pre * pre * (-0.5 * LOG2E))
    t = 1.0 / (1.0 + (ERFC_P * SQRT_HALF) * jnp.abs(pre))
    poly = jnp.full_like(t, 0.5 * ERFC_C[-1])
    for coef in ERFC_C[-2::-1]:
        poly = poly * t + 0.5 * coef
    half_erfc = gauss * (t * poly)
    phi = jnp.where(pre < 0.0, half_erfc, 1.0 - half_erfc)
    return phi, gauss


def normalize(values):
    center = values - jnp.mean(values, axis=0, keepdims=True)
    inv_std = lax.rsqrt(jnp.mean(center * center, axis=0, keepdims=True) + EPSILON)
    return center * inv_std, inv_std


def norm_back(scaled, normed, inv_std):
    return inv_std * (
        scaled
        - jnp.mean(scaled, axis=0, keepdims=True)
        - normed * jnp.mean(scaled * normed, axis=0, keepdims=True)
    )


def load_rows(ref):
    pieces, _, sub, width = ref.shape
    return ref[...].reshape(pieces, sub, width).astype(F32).reshape(pieces * sub, width)


def store_rows(ref, rows):
    pieces, _, sub, width = ref.shape
    ref[...] = rows.reshape(pieces, 1, sub, width).astype(ref.dtype)


def fold_lanes(values):
    total = values[:, :128]
    for start in range(128, values.shape[1], 128):
        total = total + values[:, start : start + 128]
    return total


def begin(carried, acc_ref, grad_gain_ref):
    if carried:
        acc_ref[...] = carried[0][...]
        grad_gain_ref[...] = carried[1][...]
    else:
        acc_ref[...] = jnp.zeros_like(acc_ref)
        grad_gain_ref[...] = jnp.zeros_like(grad_gain_ref)


def finish(acc_ref, grads_ref, grad_gain_ref):
    rows = acc_ref.shape[0]
    grads_ref[:rows] = acc_ref[...].astype(grads_ref.dtype)
    if grads_ref.shape[0] > rows:
        gains = jnp.sum(grad_gain_ref[...].T, axis=0, keepdims=True)
        spare = grads_ref.shape[0] - rows
        first = lax.broadcasted_iota(jnp.int32, (spare, gains.shape[1]), 0) == 0
        grads_ref[rows:] = jnp.where(first, gains, 0.0).astype(grads_ref.dtype)


def attend_kernel(act_ref, gain_ref, joint_ref, flat_ref, triple_ref, mixed_ref):
    width = gain_ref.shape[0]
    head = width // HEADS
    factor = head ** (-0.5) * LOG2E
    flat = load_rows(act_ref).T
    flat_ref[0] = flat.astype(BF)
    normed, _ = normalize(flat)
    scaled = (normed * gain_ref[...]).astype(BF)
    triple_ref[0] = nn(joint_ref[...], scaled).astype(BF)
    for h in range(HEADS):
        rows = slice(h * head, (h + 1) * head)
        queries = triple_ref[0, h * head : (h + 1) * head]
        keys = triple_ref[0, width + h * head : width + (h + 1) * head]
        values = triple_ref[0, 2 * width + h * head : 2 * width + (h + 1) * head]
        scores = tn(keys, queries)
        weights = jnp.exp2((scores - jnp.max(scores, axis=0, keepdims=True)) * factor)
        weights = weights * (1.0 / jnp.sum(weights, axis=0, keepdims=True))
        mixed_ref[0, rows] = nn(values, weights.astype(BF)).astype(BF)


def mlp_kernel(
    flat_ref, mixed_ref, cot_ref, gain_ref, out_t_ref, up_t_ref, down_t_ref, down_ref, up_ref, out_w_ref,
    *rest,
):
    carried = rest[:-6]
    result_ref, grad_att_ref, grad_mixed_ref, grads_ref, grad_gain_ref, acc_ref = rest[-6:]
    step = pl.program_id(0)
    width = gain_ref.shape[0]
    hidden_dim = up_ref.shape[1]

    @pl.when(step == 0)
    def _():
        begin(carried, acc_ref, grad_gain_ref)

    cot_rows = load_rows(cot_ref)
    cot_b = cot_rows.astype(BF)
    cot_t = cot_rows.T
    cot_tb = cot_t.astype(BF)
    mixed = mixed_ref[0]
    attended = flat_ref[0].astype(F32) + nn(out_t_ref[...], mixed)
    normed, inv_std = normalize(attended)
    gain = gain_ref[...]
    scaled = (normed * gain).astype(BF)
    result = attended
    grad_scaled = jnp.zeros_like(attended)
    piece = width
    for start in range(0, hidden_dim, piece):
        part = slice(start, start + piece)
        pre = nn(up_t_ref[part], scaled)
        phi, gauss = gelu_parts(pre)
        hidden = (pre * phi).astype(BF)
        result = result + nn(down_t_ref[:, part], hidden)
        acc_ref[part] += nn(hidden, cot_b)
        grad_hidden = nn(down_ref[part], cot_tb).astype(BF).astype(F32)
        grad_pre = (grad_hidden * (phi + pre * gauss * INV_ROOT_TAU)).astype(BF)
        grad_scaled = grad_scaled + nn(up_ref[:, part], grad_pre)
        acc_ref[hidden_dim + start : hidden_dim + start + piece] += nt(grad_pre, scaled)
    store_rows(result_ref, result.T)
    grad_gain_ref[...] += fold_lanes(grad_scaled * normed)
    grad_att = cot_t + norm_back(grad_scaled * gain, normed, inv_std)
    grad_att_ref[0] = grad_att
    grad_att_b = grad_att.astype(BF)
    acc_ref[2 * hidden_dim :] += nt(mixed, grad_att_b)
    grad_mixed_ref[0] = nn(out_w_ref[...], grad_att_b).astype(BF)

    @pl.when(step == pl.num_programs(0) - 1)
    def _():
        finish(acc_ref, grads_ref, grad_gain_ref)


def back_kernel(
    flat_ref, triple_ref, grad_mixed_ref, grad_att_ref, gain_ref, joint_ref,
    *rest,
):
    carried = rest[:-5]
    grad_in_ref, grads_ref, grad_gain_ref, acc_ref, grad_triple_ref = rest[-5:]
    step = pl.program_id(0)
    width = gain_ref.shape[0]
    head = width // HEADS
    scale = head ** (-0.5)

    @pl.when(step == 0)
    def _():
        begin(carried, acc_ref, grad_gain_ref)

    for h in range(HEADS):
        queries = triple_ref[0, h * head : (h + 1) * head]
        keys = triple_ref[0, width + h * head : width + (h + 1) * head]
        values = triple_ref[0, 2 * width + h * head : 2 * width + (h + 1) * head]
        grad_heads = grad_mixed_ref[0, h * head : (h + 1) * head]
        scores = tn(keys, queries)
        weights = jnp.exp2((scores - jnp.max(scores, axis=0, keepdims=True)) * (scale * LOG2E))
        weights = weights * (1.0 / jnp.sum(weights, axis=0, keepdims=True))
        grad_weights = tn(values, grad_heads)
        inner = jnp.sum(weights * grad_weights, axis=0, keepdims=True)
        grad_scores = (weights * (grad_weights - inner) * scale).astype(BF)
        grad_triple_ref[h * head : (h + 1) * head] = nn(keys, grad_scores).astype(BF)
        grad_triple_ref[width + h * head : width + (h + 1) * head] = nt(queries, grad_scores).astype(BF)
        grad_triple_ref[2 * width + h * head : 2 * width + (h + 1) * head] = nt(
            grad_heads, weights.astype(BF)
        ).astype(BF)
    normed, inv_std = normalize(flat_ref[0].astype(F32))
    gain = gain_ref[...]
    scaled = (normed * gain).astype(BF)
    acc_ref[...] += nt(grad_triple_ref[...], scaled)
    grad_scaled = nn(joint_ref[...], grad_triple_ref[...])
    grad_gain_ref[...] += fold_lanes(grad_scaled * normed)
    grad_in = grad_att_ref[0] + norm_back(grad_scaled * gain, normed, inv_std)
    store_rows(grad_in_ref, grad_in.T)

    @pl.when(step == pl.num_programs(0) - 1)
    def _():
        finish(acc_ref, grads_ref, grad_gain_ref)


def pack_kernel(tile_ref, sends_ref, rows_ref):
    lines, _, chunk_rows, columns, width = tile_ref.shape
    cols, groups, share, _ = sends_ref.shape
    for line in range(lines):
        for row in range(chunk_rows):
            for block in range(columns // cols):
                near, part = block // (columns // cols // (share // lines)), block % (groups // chunk_rows)
                start = (row * (groups // chunk_rows) + part) * share + line * (share // lines) + near
                values = tile_ref[line, 0, row, block * cols : (block + 1) * cols].astype(F32)
                for lane in range(width // 128):
                    rows_ref[lane, pl.ds(start, cols, stride=groups * share)] = values[
                        :, lane * 128 : (lane + 1) * 128
                    ]
    for lane in range(width // 128):
        sends_ref[:, :, :, lane * 128 : (lane + 1) * 128] = (
            rows_ref[lane].reshape(cols, groups, share, 128).astype(BF)
        )


def unpack_kernel(*refs):
    *arrived, tile_ref, rows_ref = refs
    lines, _, all_rows, columns, width = tile_ref.shape
    cols, groups, share, _ = arrived[0].shape
    chunk_rows = all_rows // len(arrived)
    parts = groups // chunk_rows
    for chunk, part_ref in enumerate(arrived):
        for lane in range(width // 128):
            piece = part_ref[:, :, :, lane * 128 : (lane + 1) * 128].astype(F32)
            rows_ref[lane] = piece.reshape(cols * groups * share, 128)
        for line in range(lines):
            for row in range(chunk_rows):
                for block in range(columns // cols):
                    near, part = block // parts, block % parts
                    start = (row * parts + part) * share + line * (share // lines) + near
                    values = jnp.concatenate(
                        [
                            rows_ref[lane, pl.ds(start, cols, stride=groups * share)]
                            for lane in range(width // 128)
                        ],
                        axis=1,
                    )
                    tile_ref[line, 0, chunk * chunk_rows + row, block * cols : (block + 1) * cols] = (
                        values.astype(BF)
                    )


def pack_call(tile, chunk, chunk_rows, row_devs, cols, parts):
    lines, _, _, columns, width = tile.shape
    groups, share = chunk_rows * parts, lines * columns // (cols * parts)
    return pl.pallas_call(
        pack_kernel,
        grid=(row_devs,),
        in_specs=[
            pl.BlockSpec((lines, 1, chunk_rows, columns, width), lambda r: (0, r, chunk, 0, 0))
        ],
        out_specs=pl.BlockSpec((cols, groups, share, width), lambda r: (r, 0, 0, 0)),
        out_shape=jax.ShapeDtypeStruct((row_devs * cols, groups, share, width), BF),
        scratch_shapes=[pltpu.VMEM((width // 128, cols * groups * share, 128), F32)],
        compiler_params=params(),
        cost_estimate=cost(1e6, 4 * row_devs * cols * groups * share * width, 0),
    )(tile)


def unpack_call(arrived, lines, all_rows, columns, row_devs):
    devices, groups, share, width = arrived[0].shape
    cols = devices // row_devs
    piece = pl.BlockSpec((cols, groups, share, width), lambda r: (r, 0, 0, 0))
    return pl.pallas_call(
        unpack_kernel,
        grid=(row_devs,),
        in_specs=[piece] * len(arrived),
        out_specs=pl.BlockSpec((lines, 1, all_rows, columns, width), lambda r: (0, r, 0, 0, 0)),
        out_shape=jax.ShapeDtypeStruct((lines, row_devs, all_rows, columns, width), BF),
        scratch_shapes=[pltpu.VMEM((width // 128, cols * groups * share, 128), F32)],
        compiler_params=params(),
        cost_estimate=cost(1e6, 4 * lines * row_devs * all_rows * columns * width, 0),
    )(*arrived)


def whole(array):
    return pl.BlockSpec(array.shape, lambda g: (0,) * array.ndim)


def per_group(shape):
    return pl.BlockSpec((1,) + shape, lambda g: (g, 0, 0))


def pieces_spec(array):
    pieces, _, sub, width = array.shape
    return pl.BlockSpec((pieces, 1, sub, width), lambda g: (0, g, 0, 0))


def params():
    return pltpu.CompilerParams(dimension_semantics=("arbitrary",), vmem_limit_bytes=60 << 20)


def cost(flops, bytes_moved, exps):
    return pl.CostEstimate(flops=int(flops), bytes_accessed=int(bytes_moved), transcendentals=int(exps))


def attend_call(act, gain, joint_t):
    pieces, groups, sub, width = act.shape
    tokens = pieces * sub
    return pl.pallas_call(
        attend_kernel,
        grid=(groups,),
        in_specs=[pieces_spec(act), whole(gain), whole(joint_t)],
        out_specs=[per_group((width, tokens)), per_group((3 * width, tokens)), per_group((width, tokens))],
        out_shape=[
            jax.ShapeDtypeStruct((groups, width, tokens), BF),
            jax.ShapeDtypeStruct((groups, 3 * width, tokens), BF),
            jax.ShapeDtypeStruct((groups, width, tokens), BF),
        ],
        compiler_params=params(),
        cost_estimate=cost(3e9 * groups, 12 * groups * tokens * width, 0),
    )(act, gain, joint_t)


def mlp_call(flat, mixed, cot, gain, weights, carried, spare):
    pieces, groups, sub, width = cot.shape
    tokens = pieces * sub
    hidden_dim = weights[1].shape[0]
    rows = 2 * hidden_dim + width
    return pl.pallas_call(
        mlp_kernel,
        grid=(groups,),
        in_specs=[per_group((width, tokens)), per_group((width, tokens)), pieces_spec(cot), whole(gain)]
        + [whole(w) for w in weights + carried],
        out_specs=[
            pieces_spec(cot),
            per_group((width, tokens)),
            per_group((width, tokens)),
            pl.BlockSpec((rows + spare, width), lambda g: (0, 0)),
            pl.BlockSpec((width, 128), lambda g: (0, 0)),
        ],
        out_shape=[
            jax.ShapeDtypeStruct(cot.shape, BF),
            jax.ShapeDtypeStruct((groups, width, tokens), F32),
            jax.ShapeDtypeStruct((groups, width, tokens), BF),
            jax.ShapeDtypeStruct((rows + spare, width), BF if spare else F32),
            jax.ShapeDtypeStruct((width, 128), F32),
        ],
        scratch_shapes=[pltpu.VMEM((rows, width), F32)],
        compiler_params=params(),
        cost_estimate=cost(4e9 * groups, 14 * groups * tokens * width, 0),
    )(flat, mixed, cot, gain, *weights, *carried)


def back_call(flat, triple, grad_mixed, grad_att, gain, joint, like, carried, spare):
    rows = joint.shape[1]
    pieces, groups, sub, width = like.shape
    tokens = pieces * sub
    return pl.pallas_call(
        back_kernel,
        grid=(groups,),
        in_specs=[
            per_group((width, tokens)),
            per_group((3 * width, tokens)),
            per_group((width, tokens)),
            per_group((width, tokens)),
            whole(gain),
            whole(joint),
        ]
        + [whole(w) for w in carried],
        out_specs=[
            pieces_spec(like),
            pl.BlockSpec((rows + spare, width), lambda g: (0, 0)),
            pl.BlockSpec((width, 128), lambda g: (0, 0)),
        ],
        out_shape=[
            jax.ShapeDtypeStruct(like.shape, BF),
            jax.ShapeDtypeStruct((rows + spare, width), BF if spare else F32),
            jax.ShapeDtypeStruct((width, 128), F32),
        ],
        scratch_shapes=[pltpu.VMEM((3 * width, width), F32), pltpu.VMEM((3 * width, tokens), BF)],
        compiler_params=params(),
        cost_estimate=cost(6e9 * groups, 18 * groups * tokens * width, 0),
    )(flat, triple, grad_mixed, grad_att, gain, joint, *carried)


def tie(value, *after):
    return lax.optimization_barrier((value,) + after)[0]


def peers(axis, low, high):
    return lax.axis_index(axis) // (1 << low) % (1 << (high - low)), 1 << (high - low)


def swap(values, axis, offset):
    return lax.ppermute(values, axis, [(i, i ^ offset) for i in range(lax.axis_size(axis))])


def scatter_sum(values, axis, low, high):
    mine, count = peers(axis, low, high)
    parts = values.reshape((count, values.shape[0] // count) + values.shape[1:])
    total = lax.dynamic_index_in_dim(parts, mine, 0, keepdims=False).astype(F32)
    for other in range(1, count):
        part = lax.dynamic_index_in_dim(parts, mine ^ other, 0, keepdims=False)
        total = total + swap(part, axis, other << low).astype(F32)
    return total.astype(BF)


def collect(values, axis, low, high):
    mine, count = peers(axis, low, high)
    got = jnp.stack([values] + [swap(values, axis, other << low) for other in range(1, count)])
    return jnp.concatenate(
        [lax.dynamic_index_in_dim(got, slot ^ mine, 0, keepdims=False) for slot in range(count)]
    )


def stages():
    row_bits = lax.axis_size("row").bit_length() - 1
    col_bits = lax.axis_size("col").bit_length() - 1
    return (("col", 0, 1), ("col", 1, col_bits), ("row", 0, row_bits))


def shards(
    activations,
    cotangent,
    first_gain,
    joint_weight,
    output_weight,
    second_gain,
    expand_weight,
    reduce_weight,
):
    row_devs = lax.axis_size("row")
    col_devs = lax.axis_size("col")
    devices = row_devs * col_devs
    both = ("row", "col")
    tile_rows, tile_cols, channels = activations.shape
    local_rows = GRID // row_devs
    local_cols = GRID // col_devs
    stride_rows = tile_rows // local_rows
    stride_cols = tile_cols // local_cols
    part_rows = stride_rows // row_devs
    part_cols = stride_cols // col_devs
    share = local_rows * local_cols
    tokens = GRID * GRID
    factor = float(tile_rows * tile_cols * devices) ** (-0.5)

    chunks = 2
    chunk_rows = part_rows // chunks
    chunk_groups = chunk_rows * part_cols

    kernels_pack = share % SUB == 0 and col_devs == SUB

    def pack(tile, chunk):
        if kernels_pack:
            tile = tile.reshape(local_rows, row_devs, part_rows, tile_cols, channels)
            return pack_call(tile, chunk, chunk_rows, row_devs, col_devs, part_cols)
        sends = tile.reshape(
            local_rows, row_devs, part_rows, local_cols, part_cols, col_devs, channels
        )[:, :, chunk * chunk_rows : (chunk + 1) * chunk_rows]
        return sends.transpose(1, 5, 2, 4, 0, 3, 6).reshape(devices, chunk_groups, share, channels)

    def send(sends, *after):
        got = lax.all_to_all(tie(sends, *after), both, split_axis=0, concat_axis=0, tiled=True)
        if share % SUB:
            got = got.transpose(0, 2, 1, 3).reshape(tokens // SUB, SUB, chunk_groups, channels)
            got = got.transpose(0, 2, 1, 3)
        return got.reshape(tokens // SUB, chunk_groups, SUB, channels)

    def give_back(pieces, *after):
        if share % SUB:
            pieces = pieces.transpose(0, 2, 1, 3).reshape(devices, share, chunk_groups, channels)
            pieces = pieces.transpose(0, 2, 1, 3)
        pieces = tie(pieces.reshape(devices, chunk_groups, share, channels), *after)
        return lax.all_to_all(pieces, both, split_axis=0, concat_axis=0, tiled=True)

    def to_tile(arrived):
        if kernels_pack:
            tile = unpack_call(arrived, local_rows, part_rows, tile_cols, row_devs)
            return tile.reshape(tile_rows, tile_cols, channels)
        arrived = [
            part.reshape(row_devs, col_devs, chunk_rows, part_cols, local_rows, local_cols, channels)
            for part in arrived
        ]
        return jnp.concatenate(arrived, axis=2).transpose(4, 0, 2, 5, 3, 1, 6).reshape(
            tile_rows, tile_cols, channels
        )

    def spread(gain):
        return jnp.broadcast_to(gain[:, None], (channels, tokens))

    arrived = []
    for k, tile in enumerate([activations] * chunks + [cotangent] * chunks):
        sends = pack(tile, k % chunks)
        arrived.append(send(sends, *arrived[-1:]))
    act, cot = arrived[:chunks], arrived[chunks:]
    gain_one, gain_two = spread(first_gain), spread(second_gain)
    joint_t = joint_weight.T
    weights = (
        output_weight.T, expand_weight.T, reduce_weight.T, reduce_weight, expand_weight, output_weight
    )
    hidden_dim = expand_weight.shape[1]
    tail_rows, head_rows = 2 * hidden_dim + channels, 3 * channels
    unit = SUB * devices
    fronts = []
    for k in range(chunks):
        fronts.append(attend_call(act[k], gain_one, joint_t))
    tails, out_parts, carried = [], [], ()
    before = cot[-1:]
    for k in range(chunks):
        flat, _, mixed = fronts[k]
        spare = unit - tail_rows % unit if k == chunks - 1 else 0
        tails.append(mlp_call(flat, mixed, cot[k], gain_two, weights, carried, spare))
        carried = tails[-1][3:]
        out_parts.append(give_back(tails[-1][0], *before))
        before = out_parts[-1:]
    steps = stages()
    tail_sum = carried[0]
    heads, in_parts, carried = [], [], ()
    for k in range(chunks):
        flat, triple, _ = fronts[k]
        _, grad_att, grad_mixed = tails[k][:3]
        spare = unit - head_rows % unit if k == chunks - 1 else 0
        grad_mixed = tie(grad_mixed, out_parts[k], *((tail_sum,) if k else ()))
        heads.append(
            back_call(flat, triple, grad_mixed, grad_att, gain_one, joint_weight, cot[k], carried, spare)
        )
        carried = heads[-1][1:]
        in_parts.append(give_back(heads[-1][0], *before))
        before = in_parts[-1:]
        if k < len(steps):
            tail_sum = scatter_sum(tail_sum, *steps[k])
    head_sum = tie(carried[0], tail_sum)
    for stage in steps[:-1]:
        head_sum = scatter_sum(head_sum, *stage)
    rows_left = lax.axis_size("row")
    split = head_sum.shape[0] // rows_left
    both_sums = jnp.concatenate(
        [part.reshape(rows_left, -1, channels) for part in (head_sum, tail_sum)], axis=1
    )
    width_all = both_sums.shape[1]
    both_sums = scatter_sum(both_sums.reshape(-1, channels), *steps[-1])
    for stage in steps[::-1]:
        both_sums = collect(both_sums, *stage)
    both_sums = both_sums.reshape(devices, width_all, channels)
    head_sum = both_sums[:, :split].reshape(-1, channels).astype(F32) * factor
    tail_sum = both_sums[:, split:].reshape(-1, channels).astype(F32) * factor
    block_out = to_tile(out_parts)
    grad_input = to_tile(in_parts)
    return (
        block_out,
        grad_input,
        head_sum[:head_rows].T,
        tail_sum[2 * hidden_dim : tail_rows],
        tail_sum[hidden_dim : 2 * hidden_dim].T,
        tail_sum[:hidden_dim],
        head_sum[head_rows],
        tail_sum[tail_rows],
    )


def solution(mesh):
    placed = (P("row", "col", None), P("row", "col", None), P(), P(), P(), P(), P(), P())
    return jax.shard_map(shards, mesh=mesh, in_specs=placed, out_specs=placed, check_vma=False)
```

```python
import jax
import jax.numpy as jnp
from jax import lax
from jax.experimental import pallas as pl
from jax.experimental.pallas import tpu as pltpu
from jax.sharding import PartitionSpec as P


HEADS = 12
GRID = 16
SUB = 8
PIECE = 512
EPSILON = 1e-05
INV_ROOT_TAU = 0.3989422804014327
SQRT_HALF = 0.7071067811865476
LOG2E = 1.4426950408889634
BF = jnp.bfloat16
F32 = jnp.float32

ERFC_P = 0.4
ERFC_C = (
    0.2256758624069583,
    0.22566957331484927,
    0.20784305752189558,
    0.16853970978283367,
    0.1414388899580775,
    -0.005621196233437842,
    0.16909944767289115,
    -0.18290897174728507,
    0.05026375199644912,
)


def nn(a, b):
    return lax.dot_general(a, b, (((1,), (0,)), ((), ())), preferred_element_type=F32)


def nt(a, b):
    return lax.dot_general(a, b, (((1,), (1,)), ((), ())), preferred_element_type=F32)


def tn(a, b):
    return lax.dot_general(a, b, (((0,), (0,)), ((), ())), preferred_element_type=F32)


def gelu_parts(pre):
    gauss = jnp.exp2(pre * pre * (-0.5 * LOG2E))
    t = 1.0 / (1.0 + (ERFC_P * SQRT_HALF) * jnp.abs(pre))
    poly = jnp.full_like(t, 0.5 * ERFC_C[-1])
    for coef in ERFC_C[-2::-1]:
        poly = poly * t + 0.5 * coef
    half_erfc = gauss * (t * poly)
    phi = jnp.where(pre < 0.0, half_erfc, 1.0 - half_erfc)
    return phi, gauss


def normalize(values):
    center = values - jnp.mean(values, axis=0, keepdims=True)
    inv_std = lax.rsqrt(jnp.mean(center * center, axis=0, keepdims=True) + EPSILON)
    return center * inv_std, inv_std


def norm_back(scaled, normed, inv_std):
    return inv_std * (
        scaled
        - jnp.mean(scaled, axis=0, keepdims=True)
        - normed * jnp.mean(scaled * normed, axis=0, keepdims=True)
    )


def load_rows(ref):
    pieces, _, sub, width = ref.shape
    return ref[...].reshape(pieces, sub, width).astype(F32).reshape(pieces * sub, width)


def store_rows(ref, rows):
    pieces, _, sub, width = ref.shape
    ref[...] = rows.reshape(pieces, 1, sub, width).astype(ref.dtype)


def fold_lanes(values):
    total = values[:, :128]
    for start in range(128, values.shape[1], 128):
        total = total + values[:, start : start + 128]
    return total


def begin(carried, acc_ref, grad_gain_ref):
    if carried:
        acc_ref[...] = carried[0][...]
        grad_gain_ref[...] = carried[1][...]
    else:
        acc_ref[...] = jnp.zeros_like(acc_ref)
        grad_gain_ref[...] = jnp.zeros_like(grad_gain_ref)


def finish(acc_ref, grads_ref, grad_gain_ref):
    rows = acc_ref.shape[0]
    grads_ref[:rows] = acc_ref[...].astype(grads_ref.dtype)
    if grads_ref.shape[0] > rows:
        gains = jnp.sum(grad_gain_ref[...].T, axis=0, keepdims=True)
        spare = grads_ref.shape[0] - rows
        first = lax.broadcasted_iota(jnp.int32, (spare, gains.shape[1]), 0) == 0
        grads_ref[rows:] = jnp.where(first, gains, 0.0).astype(grads_ref.dtype)


def lane_halves(count):
    return [slice(start, start + 128) for start in range(0, count, 128)]


def attend_kernel(act_ref, gain_ref, joint_ref, flat_ref, triple_ref, mixed_ref, stat_ref, score_ref):
    width, tokens = gain_ref.shape
    head = width // HEADS
    factor = head ** (-0.5) * LOG2E
    flat = load_rows(act_ref).T
    flat_ref[0] = flat.astype(BF)
    normed, _ = normalize(flat)
    scaled = (normed * gain_ref[...]).astype(BF)
    triple_ref[0] = nn(joint_ref[...], scaled).astype(BF)

    def score(h):
        queries = triple_ref[0, h * head : (h + 1) * head]
        keys = triple_ref[0, width + h * head : width + (h + 1) * head]
        score_ref[h % 2] = tn(keys, queries)

    score(0)
    for h in range(HEADS):
        if h + 1 < HEADS:
            score(h + 1)
        values = triple_ref[0, 2 * width + h * head : 2 * width + (h + 1) * head]
        for lanes in lane_halves(tokens):
            scores = score_ref[h % 2, :, lanes]
            top = jnp.max(scores, axis=0, keepdims=True)
            weights = jnp.exp2((scores - top) * factor)
            total = jnp.sum(weights, axis=0, keepdims=True)
            stat_ref[0, h : h + 1, lanes] = top * factor + jnp.log2(total)
            weights = (weights * (1.0 / total)).astype(BF)
            mixed_ref[0, h * head : (h + 1) * head, lanes] = nn(values, weights).astype(BF)


def mlp_kernel(
    flat_ref, mixed_ref, cot_ref, gain_ref, out_t_ref, up_t_ref, down_t_ref, down_ref, up_ref, out_w_ref,
    *rest,
):
    carried = rest[:-13]
    result_ref, grad_att_ref, grad_mixed_ref, grads_ref, grad_gain_ref, acc_ref = rest[-13:-7]
    scaled_ref, cot_b_ref, cot_tb_ref, pre_ref, grad_hidden_ref, hidden_ref, grad_pre_ref = rest[-7:]
    step = pl.program_id(0)
    hidden_dim = up_ref.shape[1]

    @pl.when(step == 0)
    def _():
        begin(carried, acc_ref, grad_gain_ref)

    cot_rows = load_rows(cot_ref)
    cot_b = cot_rows.astype(BF)
    cot_t = cot_rows.T
    cot_tb = cot_t.astype(BF)
    mixed = mixed_ref[0]
    attended = flat_ref[0].astype(F32) + nn(out_t_ref[...], mixed)
    normed, inv_std = normalize(attended)
    gain = gain_ref[...]
    scaled = (normed * gain).astype(BF)
    scaled_ref[...] = scaled
    cot_b_ref[...] = cot_b
    cot_tb_ref[...] = cot_tb

    def products(n):
        part = slice(n * PIECE, (n + 1) * PIECE)
        pre_ref[n % 2] = nn(up_t_ref[part], scaled_ref[...])
        grad_hidden_ref[n % 2] = nn(down_ref[part], cot_tb_ref[...]).astype(BF)

    def activate(n):
        for start in range(0, PIECE, 32):
            some = slice(start, start + 32)
            here = slice(n * PIECE + start, n * PIECE + start + 32)
            pre = pre_ref[n % 2, some]
            phi, gauss = gelu_parts(pre)
            hidden_ref[here] = (pre * phi).astype(BF)
            slope = phi + pre * gauss * INV_ROOT_TAU
            grad_pre_ref[here] = (grad_hidden_ref[n % 2, some].astype(F32) * slope).astype(BF)

    def gather(n):
        part = slice(n * PIECE, (n + 1) * PIECE)
        acc_ref[part] += nn(hidden_ref[part], cot_b_ref[...])
        there = slice(hidden_dim + n * PIECE, hidden_dim + (n + 1) * PIECE)
        acc_ref[there] += nt(grad_pre_ref[part], scaled_ref[...])

    pieces = hidden_dim // PIECE
    products(0)
    for n in range(pieces):
        if n + 1 < pieces:
            products(n + 1)
        activate(n)
        if n:
            gather(n - 1)
    gather(pieces - 1)
    grad_scaled = nn(up_ref[...], grad_pre_ref[...])
    result = attended + nn(down_t_ref[...], hidden_ref[...])
    store_rows(result_ref, result.T)
    grad_gain_ref[...] += fold_lanes(grad_scaled * normed)
    grad_att = cot_t + norm_back(grad_scaled * gain, normed, inv_std)
    grad_att_ref[0] = grad_att
    grad_att_b = grad_att.astype(BF)
    acc_ref[2 * hidden_dim :] += nt(mixed, grad_att_b)
    grad_mixed_ref[0] = nn(out_w_ref[...], grad_att_b).astype(BF)

    @pl.when(step == pl.num_programs(0) - 1)
    def _():
        finish(acc_ref, grads_ref, grad_gain_ref)


def back_kernel(
    flat_ref, triple_ref, stat_ref, grad_mixed_ref, grad_att_ref, gain_ref, joint_ref,
    *rest,
):
    carried = rest[:-9]
    grad_in_ref, grads_ref, grad_gain_ref, acc_ref, grad_triple_ref = rest[-9:-4]
    score_ref, slope_ref, grad_score_ref, weight_ref = rest[-4:]
    step = pl.program_id(0)
    width = gain_ref.shape[0]
    head = width // HEADS
    scale = head ** (-0.5)

    @pl.when(step == 0)
    def _():
        begin(carried, acc_ref, grad_gain_ref)

    tokens = gain_ref.shape[1]

    def rows(part, h):
        return slice(part * width + h * head, part * width + (h + 1) * head)

    def products(h):
        score_ref[h % 2] = tn(triple_ref[0, rows(1, h)], triple_ref[0, rows(0, h)])
        slope_ref[h % 2] = tn(triple_ref[0, rows(2, h)], grad_mixed_ref[0, rows(0, h)])

    def weigh(h):
        for lanes in lane_halves(tokens):
            weights = jnp.exp2(score_ref[h % 2, :, lanes] * (scale * LOG2E) - stat_ref[0, h : h + 1, lanes])
            grad_weights = slope_ref[h % 2, :, lanes]
            inner = jnp.sum(weights * grad_weights, axis=0, keepdims=True)
            grad_score_ref[h % 2, :, lanes] = (weights * (grad_weights - inner) * scale).astype(BF)
            weight_ref[h % 2, :, lanes] = weights.astype(BF)

    def back(h):
        grad_scores = grad_score_ref[h % 2]
        grad_triple_ref[rows(0, h)] = nn(triple_ref[0, rows(1, h)], grad_scores).astype(BF)
        grad_triple_ref[rows(1, h)] = nt(triple_ref[0, rows(0, h)], grad_scores).astype(BF)
        grad_triple_ref[rows(2, h)] = nt(grad_mixed_ref[0, rows(0, h)], weight_ref[h % 2]).astype(BF)

    products(0)
    for h in range(HEADS):
        if h + 1 < HEADS:
            products(h + 1)
        weigh(h)
        if h:
            back(h - 1)
    back(HEADS - 1)
    normed, inv_std = normalize(flat_ref[0].astype(F32))
    gain = gain_ref[...]
    scaled = (normed * gain).astype(BF)
    acc_ref[...] += nt(grad_triple_ref[...], scaled)
    grad_scaled = nn(joint_ref[...], grad_triple_ref[...])
    grad_gain_ref[...] += fold_lanes(grad_scaled * normed)
    grad_in = grad_att_ref[0] + norm_back(grad_scaled * gain, normed, inv_std)
    store_rows(grad_in_ref, grad_in.T)

    @pl.when(step == pl.num_programs(0) - 1)
    def _():
        finish(acc_ref, grads_ref, grad_gain_ref)


def pack_kernel(tile_ref, sends_ref, rows_ref):
    lines, _, chunk_rows, columns, width = tile_ref.shape
    cols, groups, share, _ = sends_ref.shape
    for line in range(lines):
        for row in range(chunk_rows):
            for block in range(columns // cols):
                near, part = block // (columns // cols // (share // lines)), block % (groups // chunk_rows)
                start = (row * (groups // chunk_rows) + part) * share + line * (share // lines) + near
                values = tile_ref[line, 0, row, block * cols : (block + 1) * cols].astype(F32)
                for lane in range(width // 128):
                    rows_ref[lane, pl.ds(start, cols, stride=groups * share)] = values[
                        :, lane * 128 : (lane + 1) * 128
                    ]
    for lane in range(width // 128):
        sends_ref[:, :, :, lane * 128 : (lane + 1) * 128] = (
            rows_ref[lane].reshape(cols, groups, share, 128).astype(BF)
        )


def unpack_kernel(*refs):
    *arrived, tile_ref, rows_ref = refs
    lines, _, all_rows, columns, width = tile_ref.shape
    cols, groups, share, _ = arrived[0].shape
    chunk_rows = all_rows // len(arrived)
    parts = groups // chunk_rows
    for chunk, part_ref in enumerate(arrived):
        for lane in range(width // 128):
            piece = part_ref[:, :, :, lane * 128 : (lane + 1) * 128].astype(F32)
            rows_ref[lane] = piece.reshape(cols * groups * share, 128)
        for line in range(lines):
            for row in range(chunk_rows):
                for block in range(columns // cols):
                    near, part = block // parts, block % parts
                    start = (row * parts + part) * share + line * (share // lines) + near
                    values = jnp.concatenate(
                        [
                            rows_ref[lane, pl.ds(start, cols, stride=groups * share)]
                            for lane in range(width // 128)
                        ],
                        axis=1,
                    )
                    tile_ref[line, 0, chunk * chunk_rows + row, block * cols : (block + 1) * cols] = (
                        values.astype(BF)
                    )


def pack_call(tile, chunk, chunk_rows, row_devs, cols, parts):
    lines, _, _, columns, width = tile.shape
    groups, share = chunk_rows * parts, lines * columns // (cols * parts)
    return pl.pallas_call(
        pack_kernel,
        grid=(row_devs,),
        in_specs=[
            pl.BlockSpec((lines, 1, chunk_rows, columns, width), lambda r: (0, r, chunk, 0, 0))
        ],
        out_specs=pl.BlockSpec((cols, groups, share, width), lambda r: (r, 0, 0, 0)),
        out_shape=jax.ShapeDtypeStruct((row_devs * cols, groups, share, width), BF),
        scratch_shapes=[pltpu.VMEM((width // 128, cols * groups * share, 128), F32)],
        compiler_params=params(),
        cost_estimate=cost(1e6, 4 * row_devs * cols * groups * share * width, 0),
    )(tile)


def unpack_call(arrived, lines, all_rows, columns, row_devs):
    devices, groups, share, width = arrived[0].shape
    cols = devices // row_devs
    piece = pl.BlockSpec((cols, groups, share, width), lambda r: (r, 0, 0, 0))
    return pl.pallas_call(
        unpack_kernel,
        grid=(row_devs,),
        in_specs=[piece] * len(arrived),
        out_specs=pl.BlockSpec((lines, 1, all_rows, columns, width), lambda r: (0, r, 0, 0, 0)),
        out_shape=jax.ShapeDtypeStruct((lines, row_devs, all_rows, columns, width), BF),
        scratch_shapes=[pltpu.VMEM((width // 128, cols * groups * share, 128), F32)],
        compiler_params=params(),
        cost_estimate=cost(1e6, 4 * lines * row_devs * all_rows * columns * width, 0),
    )(*arrived)


def whole(array):
    return pl.BlockSpec(array.shape, lambda g: (0,) * array.ndim)


def per_group(shape):
    return pl.BlockSpec((1,) + shape, lambda g: (g, 0, 0))


def pieces_spec(array):
    pieces, _, sub, width = array.shape
    return pl.BlockSpec((pieces, 1, sub, width), lambda g: (0, g, 0, 0))


def params():
    return pltpu.CompilerParams(dimension_semantics=("arbitrary",), vmem_limit_bytes=60 << 20)


def cost(flops, bytes_moved, exps):
    return pl.CostEstimate(flops=int(flops), bytes_accessed=int(bytes_moved), transcendentals=int(exps))


def attend_call(act, gain, joint_t):
    pieces, groups, sub, width = act.shape
    tokens = pieces * sub
    return pl.pallas_call(
        attend_kernel,
        grid=(groups,),
        in_specs=[pieces_spec(act), whole(gain), whole(joint_t)],
        out_specs=[
            per_group((width, tokens)),
            per_group((3 * width, tokens)),
            per_group((width, tokens)),
            per_group((16, tokens)),
        ],
        out_shape=[
            jax.ShapeDtypeStruct((groups, width, tokens), BF),
            jax.ShapeDtypeStruct((groups, 3 * width, tokens), BF),
            jax.ShapeDtypeStruct((groups, width, tokens), BF),
            jax.ShapeDtypeStruct((groups, 16, tokens), F32),
        ],
        scratch_shapes=[pltpu.VMEM((2, tokens, tokens), F32)],
        compiler_params=params(),
        cost_estimate=cost(3e9 * groups, 12 * groups * tokens * width, 0),
    )(act, gain, joint_t)


def mlp_call(flat, mixed, cot, gain, weights, carried, spare):
    pieces, groups, sub, width = cot.shape
    tokens = pieces * sub
    hidden_dim = weights[1].shape[0]
    rows = 2 * hidden_dim + width
    return pl.pallas_call(
        mlp_kernel,
        grid=(groups,),
        in_specs=[per_group((width, tokens)), per_group((width, tokens)), pieces_spec(cot), whole(gain)]
        + [whole(w) for w in weights + carried],
        out_specs=[
            pieces_spec(cot),
            per_group((width, tokens)),
            per_group((width, tokens)),
            pl.BlockSpec((rows + spare, width), lambda g: (0, 0)),
            pl.BlockSpec((width, 128), lambda g: (0, 0)),
        ],
        out_shape=[
            jax.ShapeDtypeStruct(cot.shape, BF),
            jax.ShapeDtypeStruct((groups, width, tokens), F32),
            jax.ShapeDtypeStruct((groups, width, tokens), BF),
            jax.ShapeDtypeStruct((rows + spare, width), BF if spare else F32),
            jax.ShapeDtypeStruct((width, 128), F32),
        ],
        scratch_shapes=[
            pltpu.VMEM((rows, width), F32),
            pltpu.VMEM((width, tokens), BF),
            pltpu.VMEM((tokens, width), BF),
            pltpu.VMEM((width, tokens), BF),
            pltpu.VMEM((2, PIECE, tokens), F32),
            pltpu.VMEM((2, PIECE, tokens), BF),
            pltpu.VMEM((hidden_dim, tokens), BF),
            pltpu.VMEM((hidden_dim, tokens), BF),
        ],
        compiler_params=params(),
        cost_estimate=cost(4e9 * groups, 14 * groups * tokens * width, 0),
    )(flat, mixed, cot, gain, *weights, *carried)


def back_call(flat, triple, stat, grad_mixed, grad_att, gain, joint, like, carried, spare):
    rows = joint.shape[1]
    pieces, groups, sub, width = like.shape
    tokens = pieces * sub
    return pl.pallas_call(
        back_kernel,
        grid=(groups,),
        in_specs=[
            per_group((width, tokens)),
            per_group((3 * width, tokens)),
            per_group((16, tokens)),
            per_group((width, tokens)),
            per_group((width, tokens)),
            whole(gain),
            whole(joint),
        ]
        + [whole(w) for w in carried],
        out_specs=[
            pieces_spec(like),
            pl.BlockSpec((rows + spare, width), lambda g: (0, 0)),
            pl.BlockSpec((width, 128), lambda g: (0, 0)),
        ],
        out_shape=[
            jax.ShapeDtypeStruct(like.shape, BF),
            jax.ShapeDtypeStruct((rows + spare, width), BF if spare else F32),
            jax.ShapeDtypeStruct((width, 128), F32),
        ],
        scratch_shapes=[
            pltpu.VMEM((3 * width, width), F32),
            pltpu.VMEM((3 * width, tokens), BF),
            pltpu.VMEM((2, tokens, tokens), F32),
            pltpu.VMEM((2, tokens, tokens), F32),
            pltpu.VMEM((2, tokens, tokens), BF),
            pltpu.VMEM((2, tokens, tokens), BF),
        ],
        compiler_params=params(),
        cost_estimate=cost(6e9 * groups, 18 * groups * tokens * width, 0),
    )(flat, triple, stat, grad_mixed, grad_att, gain, joint, *carried)


def tie(value, *after):
    return lax.optimization_barrier((value,) + after)[0]


def peers(axis, low, high):
    return lax.axis_index(axis) // (1 << low) % (1 << (high - low)), 1 << (high - low)


def swap(values, axis, offset):
    return lax.ppermute(values, axis, [(i, i ^ offset) for i in range(lax.axis_size(axis))])


def scatter_sum(values, axis, low, high):
    mine, count = peers(axis, low, high)
    parts = values.reshape((count, values.shape[0] // count) + values.shape[1:])
    total = lax.dynamic_index_in_dim(parts, mine, 0, keepdims=False).astype(F32)
    for other in range(1, count):
        part = lax.dynamic_index_in_dim(parts, mine ^ other, 0, keepdims=False)
        total = total + swap(part, axis, other << low).astype(F32)
    return total.astype(BF)


def share_sum(values, axis, low, high):
    _, count = peers(axis, low, high)
    total = values.astype(F32)
    for other in range(1, count):
        total = total + swap(values, axis, other << low).astype(F32)
    return total.astype(BF)


def collect(values, axis, low, high):
    mine, count = peers(axis, low, high)
    got = jnp.stack([values] + [swap(values, axis, other << low) for other in range(1, count)])
    return jnp.concatenate(
        [lax.dynamic_index_in_dim(got, slot ^ mine, 0, keepdims=False) for slot in range(count)]
    )


def stages():
    row_bits = lax.axis_size("row").bit_length() - 1
    col_bits = lax.axis_size("col").bit_length() - 1
    return (("col", 0, 1), ("col", 1, col_bits), ("row", 0, row_bits))


def shards(
    activations,
    cotangent,
    first_gain,
    joint_weight,
    output_weight,
    second_gain,
    expand_weight,
    reduce_weight,
):
    row_devs = lax.axis_size("row")
    col_devs = lax.axis_size("col")
    devices = row_devs * col_devs
    both = ("row", "col")
    tile_rows, tile_cols, channels = activations.shape
    local_rows = GRID // row_devs
    local_cols = GRID // col_devs
    stride_rows = tile_rows // local_rows
    stride_cols = tile_cols // local_cols
    part_rows = stride_rows // row_devs
    part_cols = stride_cols // col_devs
    share = local_rows * local_cols
    tokens = GRID * GRID
    factor = float(tile_rows * tile_cols * devices) ** (-0.5)

    chunks = 2
    chunk_rows = part_rows // chunks
    chunk_groups = chunk_rows * part_cols

    kernels_pack = share % SUB == 0 and col_devs == SUB

    def pack(tile, chunk):
        if kernels_pack:
            tile = tile.reshape(local_rows, row_devs, part_rows, tile_cols, channels)
            return pack_call(tile, chunk, chunk_rows, row_devs, col_devs, part_cols)
        sends = tile.reshape(
            local_rows, row_devs, part_rows, local_cols, part_cols, col_devs, channels
        )[:, :, chunk * chunk_rows : (chunk + 1) * chunk_rows]
        return sends.transpose(1, 5, 2, 4, 0, 3, 6).reshape(devices, chunk_groups, share, channels)

    def send(sends, *after):
        got = lax.all_to_all(tie(sends, *after), both, split_axis=0, concat_axis=0, tiled=True)
        if share % SUB:
            got = got.transpose(0, 2, 1, 3).reshape(tokens // SUB, SUB, chunk_groups, channels)
            got = got.transpose(0, 2, 1, 3)
        return got.reshape(tokens // SUB, chunk_groups, SUB, channels)

    def give_back(pieces, *after):
        if share % SUB:
            pieces = pieces.transpose(0, 2, 1, 3).reshape(devices, share, chunk_groups, channels)
            pieces = pieces.transpose(0, 2, 1, 3)
        pieces = tie(pieces.reshape(devices, chunk_groups, share, channels), *after)
        return lax.all_to_all(pieces, both, split_axis=0, concat_axis=0, tiled=True)

    def to_tile(arrived):
        if kernels_pack:
            tile = unpack_call(arrived, local_rows, part_rows, tile_cols, row_devs)
            return tile.reshape(tile_rows, tile_cols, channels)
        arrived = [
            part.reshape(row_devs, col_devs, chunk_rows, part_cols, local_rows, local_cols, channels)
            for part in arrived
        ]
        return jnp.concatenate(arrived, axis=2).transpose(4, 0, 2, 5, 3, 1, 6).reshape(
            tile_rows, tile_cols, channels
        )

    def spread(gain):
        return jnp.broadcast_to(gain[:, None], (channels, tokens))

    arrived = []
    for k, tile in enumerate([activations] * chunks + [cotangent] * chunks):
        sends = pack(tile, k % chunks)
        arrived.append(send(sends, *arrived[-1:]))
    act, cot = arrived[:chunks], arrived[chunks:]
    gain_one, gain_two = spread(first_gain), spread(second_gain)
    joint_t = joint_weight.T
    weights = (
        output_weight.T, expand_weight.T, reduce_weight.T, reduce_weight, expand_weight, output_weight
    )
    hidden_dim = expand_weight.shape[1]
    tail_rows, head_rows = 2 * hidden_dim + channels, 3 * channels
    unit = SUB * devices
    fronts = []
    for k in range(chunks):
        fronts.append(attend_call(act[k], gain_one, joint_t))
    tails, out_parts, carried = [], [], ()
    before = cot[-1:]
    for k in range(chunks):
        flat, _, mixed, _ = fronts[k]
        spare = unit - tail_rows % unit if k == chunks - 1 else 0
        tails.append(mlp_call(flat, mixed, cot[k], gain_two, weights, carried, spare))
        carried = tails[-1][3:]
        out_parts.append(give_back(tails[-1][0], *before))
        before = out_parts[-1:]
    steps = stages()
    tail_sum = carried[0]
    heads, in_parts, carried = [], [], ()
    for k in range(chunks):
        flat, triple, _, stat = fronts[k]
        _, grad_att, grad_mixed = tails[k][:3]
        spare = unit - head_rows % unit if k == chunks - 1 else 0
        grad_mixed = tie(grad_mixed, out_parts[k], *((tail_sum,) if k else ()))
        heads.append(
            back_call(flat, triple, stat, grad_mixed, grad_att, gain_one, joint_weight, cot[k], carried, spare)
        )
        carried = heads[-1][1:]
        in_parts.append(give_back(heads[-1][0], *before))
        before = in_parts[-1:]
        if k < len(steps):
            tail_sum = scatter_sum(tail_sum, *steps[k])
    head_sum = carried[0]
    near, cols, rows = steps
    head_sum = scatter_sum(head_sum, *near)
    tail_sum = scatter_sum(tail_sum, *rows)
    head_sum = scatter_sum(head_sum, *cols)
    tail_sum = collect(tail_sum, *rows)
    head_sum = share_sum(head_sum, *rows)
    tail_sum = collect(tail_sum, *cols)
    head_sum = collect(head_sum, *cols)
    tail_sum = collect(tail_sum, *near)
    head_sum = collect(head_sum, *near)
    head_sum = head_sum.astype(F32) * factor
    tail_sum = tail_sum.astype(F32) * factor
    block_out = to_tile(out_parts)
    grad_input = to_tile(in_parts)
    return (
        block_out,
        grad_input,
        head_sum[:head_rows].T,
        tail_sum[2 * hidden_dim : tail_rows],
        tail_sum[hidden_dim : 2 * hidden_dim].T,
        tail_sum[:hidden_dim],
        head_sum[head_rows],
        tail_sum[tail_rows],
    )


def solution(mesh):
    placed = (P("row", "col", None), P("row", "col", None), P(), P(), P(), P(), P(), P())
    return jax.shard_map(shards, mesh=mesh, in_specs=placed, out_specs=placed, check_vma=False)
```

```python
import jax
import jax.numpy as jnp
from jax import lax
from jax.experimental import pallas as pl
from jax.experimental.pallas import tpu as pltpu
from jax.sharding import PartitionSpec as P


HEADS = 12
GRID = 16
SUB = 8
PIECE = 512
EPSILON = 1e-05
INV_ROOT_TAU = 0.3989422804014327
SQRT_HALF = 0.7071067811865476
LOG2E = 1.4426950408889634
BF = jnp.bfloat16
F32 = jnp.float32

ERFC_P = 0.4
ERFC_C = (
    0.2256758624069583,
    0.22566957331484927,
    0.20784305752189558,
    0.16853970978283367,
    0.1414388899580775,
    -0.005621196233437842,
    0.16909944767289115,
    -0.18290897174728507,
    0.05026375199644912,
)


def nn(a, b):
    return lax.dot_general(a, b, (((1,), (0,)), ((), ())), preferred_element_type=F32)


def nt(a, b):
    return lax.dot_general(a, b, (((1,), (1,)), ((), ())), preferred_element_type=F32)


def tn(a, b):
    return lax.dot_general(a, b, (((0,), (0,)), ((), ())), preferred_element_type=F32)


def gelu_parts(pre):
    gauss = jnp.exp2(pre * pre * (-0.5 * LOG2E))
    t = 1.0 / (1.0 + (ERFC_P * SQRT_HALF) * jnp.abs(pre))
    poly = jnp.full_like(t, 0.5 * ERFC_C[-1])
    for coef in ERFC_C[-2::-1]:
        poly = poly * t + 0.5 * coef
    half_erfc = gauss * (t * poly)
    phi = jnp.where(pre < 0.0, half_erfc, 1.0 - half_erfc)
    return phi, gauss


def normalize(values):
    center = values - jnp.mean(values, axis=0, keepdims=True)
    inv_std = lax.rsqrt(jnp.mean(center * center, axis=0, keepdims=True) + EPSILON)
    return center * inv_std, inv_std


def norm_back(scaled, normed, inv_std):
    return inv_std * (
        scaled
        - jnp.mean(scaled, axis=0, keepdims=True)
        - normed * jnp.mean(scaled * normed, axis=0, keepdims=True)
    )


def load_rows(ref):
    pieces, _, sub, width = ref.shape
    return ref[...].reshape(pieces, sub, width).astype(F32).reshape(pieces * sub, width)


def store_rows(ref, rows):
    pieces, _, sub, width = ref.shape
    ref[...] = rows.reshape(pieces, 1, sub, width).astype(ref.dtype)


def fold_lanes(values):
    total = values[:, :128]
    for start in range(128, values.shape[1], 128):
        total = total + values[:, start : start + 128]
    return total


def begin(carried, acc_ref, grad_gain_ref):
    if carried:
        acc_ref[...] = carried[0][...]
        grad_gain_ref[...] = carried[1][...]
    else:
        acc_ref[...] = jnp.zeros_like(acc_ref)
        grad_gain_ref[...] = jnp.zeros_like(grad_gain_ref)


def finish(acc_ref, grads_ref, grad_gain_ref):
    rows = acc_ref.shape[0]
    grads_ref[:rows] = acc_ref[...].astype(grads_ref.dtype)
    if grads_ref.shape[0] > rows:
        gains = jnp.sum(grad_gain_ref[...].T, axis=0, keepdims=True)
        spare = grads_ref.shape[0] - rows
        first = lax.broadcasted_iota(jnp.int32, (spare, gains.shape[1]), 0) == 0
        grads_ref[rows:] = jnp.where(first, gains, 0.0).astype(grads_ref.dtype)


def lane_halves(count):
    return [slice(start, start + 128) for start in range(0, count, 128)]


def attend_kernel(act_ref, gain_ref, joint_ref, flat_ref, triple_ref, mixed_ref, stat_ref, score_ref):
    width, tokens = gain_ref.shape
    head = width // HEADS
    factor = head ** (-0.5) * LOG2E
    flat = load_rows(act_ref).T
    flat_ref[0] = flat.astype(BF)
    normed, _ = normalize(flat)
    scaled = (normed * gain_ref[...]).astype(BF)
    triple_ref[0] = nn(joint_ref[...], scaled).astype(BF)

    def score(h):
        queries = triple_ref[0, h * head : (h + 1) * head]
        keys = triple_ref[0, width + h * head : width + (h + 1) * head]
        score_ref[h % 2] = tn(keys, queries)

    score(0)
    for h in range(HEADS):
        if h + 1 < HEADS:
            score(h + 1)
        values = triple_ref[0, 2 * width + h * head : 2 * width + (h + 1) * head]
        for lanes in lane_halves(tokens):
            scores = score_ref[h % 2, :, lanes]
            top = jnp.max(scores, axis=0, keepdims=True)
            weights = jnp.exp2((scores - top) * factor)
            total = jnp.sum(weights, axis=0, keepdims=True)
            stat_ref[0, h : h + 1, lanes] = top * factor + jnp.log2(total)
            weights = (weights * (1.0 / total)).astype(BF)
            mixed_ref[0, h * head : (h + 1) * head, lanes] = nn(values, weights).astype(BF)


def mlp_kernel(
    flat_ref, mixed_ref, cot_ref, gain_ref, out_t_ref, up_t_ref, down_t_ref, down_ref, up_ref, out_w_ref,
    *rest,
):
    carried = rest[:-13]
    result_ref, grad_att_ref, grad_mixed_ref, grads_ref, grad_gain_ref, acc_ref = rest[-13:-7]
    scaled_ref, cot_b_ref, cot_tb_ref, pre_ref, grad_hidden_ref, hidden_ref, grad_pre_ref = rest[-7:]
    step = pl.program_id(0)
    hidden_dim = up_ref.shape[1]

    @pl.when(step == 0)
    def _():
        begin(carried, acc_ref, grad_gain_ref)

    cot_rows = load_rows(cot_ref)
    cot_b = cot_rows.astype(BF)
    cot_t = cot_rows.T
    cot_tb = cot_t.astype(BF)
    mixed = mixed_ref[0]
    attended = flat_ref[0].astype(F32) + nn(out_t_ref[...], mixed)
    normed, inv_std = normalize(attended)
    gain = gain_ref[...]
    scaled = (normed * gain).astype(BF)
    scaled_ref[...] = scaled
    cot_b_ref[...] = cot_b
    cot_tb_ref[...] = cot_tb

    def products(n):
        part = slice(n * PIECE, (n + 1) * PIECE)
        pre_ref[n % 2] = nn(up_t_ref[part], scaled_ref[...])
        grad_hidden_ref[n % 2] = nn(down_ref[part], cot_tb_ref[...]).astype(BF)

    def activate(n):
        for start in range(0, PIECE, 32):
            some = slice(start, start + 32)
            here = slice(n * PIECE + start, n * PIECE + start + 32)
            pre = pre_ref[n % 2, some]
            phi, gauss = gelu_parts(pre)
            hidden_ref[here] = (pre * phi).astype(BF)
            slope = phi + pre * gauss * INV_ROOT_TAU
            grad_pre_ref[here] = (grad_hidden_ref[n % 2, some].astype(F32) * slope).astype(BF)

    def gather(n):
        part = slice(n * PIECE, (n + 1) * PIECE)
        acc_ref[part] += nn(hidden_ref[part], cot_b_ref[...])
        there = slice(hidden_dim + n * PIECE, hidden_dim + (n + 1) * PIECE)
        acc_ref[there] += nt(grad_pre_ref[part], scaled_ref[...])

    pieces = hidden_dim // PIECE
    products(0)
    for n in range(pieces):
        if n + 1 < pieces:
            products(n + 1)
        activate(n)
        if n:
            gather(n - 1)
    gather(pieces - 1)
    grad_scaled = nn(up_ref[...], grad_pre_ref[...])
    result = attended + nn(down_t_ref[...], hidden_ref[...])
    store_rows(result_ref, result.T)
    grad_gain_ref[...] += fold_lanes(grad_scaled * normed)
    grad_att = cot_t + norm_back(grad_scaled * gain, normed, inv_std)
    grad_att_ref[0] = grad_att
    grad_att_b = grad_att.astype(BF)
    acc_ref[2 * hidden_dim :] += nt(mixed, grad_att_b)
    grad_mixed_ref[0] = nn(out_w_ref[...], grad_att_b).astype(BF)

    @pl.when(step == pl.num_programs(0) - 1)
    def _():
        finish(acc_ref, grads_ref, grad_gain_ref)


def back_kernel(
    flat_ref, triple_ref, stat_ref, grad_mixed_ref, grad_att_ref, gain_ref, joint_ref,
    *rest,
):
    carried = rest[:-9]
    grad_in_ref, grads_ref, grad_gain_ref, acc_ref, grad_triple_ref = rest[-9:-4]
    score_ref, slope_ref, grad_score_ref, weight_ref = rest[-4:]
    step = pl.program_id(0)
    width = gain_ref.shape[0]
    head = width // HEADS
    scale = head ** (-0.5)

    @pl.when(step == 0)
    def _():
        begin(carried, acc_ref, grad_gain_ref)

    tokens = gain_ref.shape[1]

    def rows(part, h):
        return slice(part * width + h * head, part * width + (h + 1) * head)

    def products(h):
        score_ref[h % 2] = tn(triple_ref[0, rows(1, h)], triple_ref[0, rows(0, h)])
        slope_ref[h % 2] = tn(triple_ref[0, rows(2, h)], grad_mixed_ref[0, rows(0, h)])

    def weigh(h):
        for lanes in lane_halves(tokens):
            weights = jnp.exp2(score_ref[h % 2, :, lanes] * (scale * LOG2E) - stat_ref[0, h : h + 1, lanes])
            grad_weights = slope_ref[h % 2, :, lanes]
            inner = jnp.sum(weights * grad_weights, axis=0, keepdims=True)
            grad_score_ref[h % 2, :, lanes] = (weights * (grad_weights - inner) * scale).astype(BF)
            weight_ref[h % 2, :, lanes] = weights.astype(BF)

    def back(h):
        grad_scores = grad_score_ref[h % 2]
        grad_triple_ref[rows(0, h)] = nn(triple_ref[0, rows(1, h)], grad_scores).astype(BF)
        grad_triple_ref[rows(1, h)] = nt(triple_ref[0, rows(0, h)], grad_scores).astype(BF)
        grad_triple_ref[rows(2, h)] = nt(grad_mixed_ref[0, rows(0, h)], weight_ref[h % 2]).astype(BF)

    products(0)
    for h in range(HEADS):
        if h + 1 < HEADS:
            products(h + 1)
        weigh(h)
        if h:
            back(h - 1)
    back(HEADS - 1)
    normed, inv_std = normalize(flat_ref[0].astype(F32))
    gain = gain_ref[...]
    scaled = (normed * gain).astype(BF)
    acc_ref[...] += nt(grad_triple_ref[...], scaled)
    grad_scaled = nn(joint_ref[...], grad_triple_ref[...])
    grad_gain_ref[...] += fold_lanes(grad_scaled * normed)
    grad_in = grad_att_ref[0] + norm_back(grad_scaled * gain, normed, inv_std)
    store_rows(grad_in_ref, grad_in.T)

    @pl.when(step == pl.num_programs(0) - 1)
    def _():
        finish(acc_ref, grads_ref, grad_gain_ref)


def prepare_kernel(
    gain_one_ref, gain_two_ref, joint_ref, out_w_ref, up_ref, down_ref,
    wide_one_ref, wide_two_ref, joint_t_ref, out_t_ref, up_t_ref, down_t_ref,
):
    tokens = wide_one_ref.shape[1]
    for gain_ref, wide_ref in ((gain_one_ref, wide_one_ref), (gain_two_ref, wide_two_ref)):
        wide_ref[...] = jnp.broadcast_to(gain_ref[...], (tokens, gain_ref.shape[1])).T
    for weight_ref, turned_ref in (
        (joint_ref, joint_t_ref),
        (out_w_ref, out_t_ref),
        (up_ref, up_t_ref),
        (down_ref, down_t_ref),
    ):
        turned_ref[...] = weight_ref[...].T


def prepare_call(gain_one, gain_two, joint, out_w, up, down, tokens):
    width = gain_one.shape[0]
    turned = [jax.ShapeDtypeStruct(w.shape[::-1], w.dtype) for w in (joint, out_w, up, down)]
    wide = jax.ShapeDtypeStruct((width, tokens), F32)
    return pl.pallas_call(
        prepare_kernel,
        out_shape=[wide, wide] + turned,
        compiler_params=pltpu.CompilerParams(vmem_limit_bytes=60 << 20),
        cost_estimate=cost(1e6, 16e6, 0),
    )(gain_one.reshape(1, width), gain_two.reshape(1, width), joint, out_w, up, down)


def pack_kernel(tile_ref, sends_ref, rows_ref):
    lines, _, chunk_rows, columns, width = tile_ref.shape
    cols, groups, share, _ = sends_ref.shape
    for line in range(lines):
        for row in range(chunk_rows):
            for block in range(columns // cols):
                near, part = block // (columns // cols // (share // lines)), block % (groups // chunk_rows)
                start = (row * (groups // chunk_rows) + part) * share + line * (share // lines) + near
                values = tile_ref[line, 0, row, block * cols : (block + 1) * cols].astype(F32)
                for lane in range(width // 128):
                    rows_ref[lane, pl.ds(start, cols, stride=groups * share)] = values[
                        :, lane * 128 : (lane + 1) * 128
                    ]
    for lane in range(width // 128):
        sends_ref[:, :, :, lane * 128 : (lane + 1) * 128] = (
            rows_ref[lane].reshape(cols, groups, share, 128).astype(BF)
        )


def unpack_kernel(*refs):
    *arrived, tile_ref, rows_ref = refs
    lines, _, all_rows, columns, width = tile_ref.shape
    cols, groups, share, _ = arrived[0].shape
    chunk_rows = all_rows // len(arrived)
    parts = groups // chunk_rows
    for chunk, part_ref in enumerate(arrived):
        for lane in range(width // 128):
            piece = part_ref[:, :, :, lane * 128 : (lane + 1) * 128].astype(F32)
            rows_ref[lane] = piece.reshape(cols * groups * share, 128)
        for line in range(lines):
            for row in range(chunk_rows):
                for block in range(columns // cols):
                    near, part = block // parts, block % parts
                    start = (row * parts + part) * share + line * (share // lines) + near
                    values = jnp.concatenate(
                        [
                            rows_ref[lane, pl.ds(start, cols, stride=groups * share)]
                            for lane in range(width // 128)
                        ],
                        axis=1,
                    )
                    tile_ref[line, 0, chunk * chunk_rows + row, block * cols : (block + 1) * cols] = (
                        values.astype(BF)
                    )


def pack_call(tile, chunk, chunk_rows, row_devs, cols, parts):
    lines, _, _, columns, width = tile.shape
    groups, share = chunk_rows * parts, lines * columns // (cols * parts)
    return pl.pallas_call(
        pack_kernel,
        grid=(row_devs,),
        in_specs=[
            pl.BlockSpec((lines, 1, chunk_rows, columns, width), lambda r: (0, r, chunk, 0, 0))
        ],
        out_specs=pl.BlockSpec((cols, groups, share, width), lambda r: (r, 0, 0, 0)),
        out_shape=jax.ShapeDtypeStruct((row_devs * cols, groups, share, width), BF),
        scratch_shapes=[pltpu.VMEM((width // 128, cols * groups * share, 128), F32)],
        compiler_params=params(),
        cost_estimate=cost(1e6, 4 * row_devs * cols * groups * share * width, 0),
    )(tile)


def unpack_call(arrived, lines, all_rows, columns, row_devs):
    devices, groups, share, width = arrived[0].shape
    cols = devices // row_devs
    piece = pl.BlockSpec((cols, groups, share, width), lambda r: (r, 0, 0, 0))
    return pl.pallas_call(
        unpack_kernel,
        grid=(row_devs,),
        in_specs=[piece] * len(arrived),
        out_specs=pl.BlockSpec((lines, 1, all_rows, columns, width), lambda r: (0, r, 0, 0, 0)),
        out_shape=jax.ShapeDtypeStruct((lines, row_devs, all_rows, columns, width), BF),
        scratch_shapes=[pltpu.VMEM((width // 128, cols * groups * share, 128), F32)],
        compiler_params=params(),
        cost_estimate=cost(1e6, 4 * lines * row_devs * all_rows * columns * width, 0),
    )(*arrived)


def whole(array):
    return pl.BlockSpec(array.shape, lambda g: (0,) * array.ndim)


def per_group(shape):
    return pl.BlockSpec((1,) + shape, lambda g: (g, 0, 0))


def pieces_spec(array):
    pieces, _, sub, width = array.shape
    return pl.BlockSpec((pieces, 1, sub, width), lambda g: (0, g, 0, 0))


def params():
    return pltpu.CompilerParams(dimension_semantics=("arbitrary",), vmem_limit_bytes=60 << 20)


def cost(flops, bytes_moved, exps):
    return pl.CostEstimate(flops=int(flops), bytes_accessed=int(bytes_moved), transcendentals=int(exps))


def attend_call(act, gain, joint_t):
    pieces, groups, sub, width = act.shape
    tokens = pieces * sub
    return pl.pallas_call(
        attend_kernel,
        grid=(groups,),
        in_specs=[pieces_spec(act), whole(gain), whole(joint_t)],
        out_specs=[
            per_group((width, tokens)),
            per_group((3 * width, tokens)),
            per_group((width, tokens)),
            per_group((16, tokens)),
        ],
        out_shape=[
            jax.ShapeDtypeStruct((groups, width, tokens), BF),
            jax.ShapeDtypeStruct((groups, 3 * width, tokens), BF),
            jax.ShapeDtypeStruct((groups, width, tokens), BF),
            jax.ShapeDtypeStruct((groups, 16, tokens), F32),
        ],
        scratch_shapes=[pltpu.VMEM((2, tokens, tokens), F32)],
        compiler_params=params(),
        cost_estimate=cost(3e9 * groups, 12 * groups * tokens * width, 0),
    )(act, gain, joint_t)


def mlp_call(flat, mixed, cot, gain, weights, carried, spare):
    pieces, groups, sub, width = cot.shape
    tokens = pieces * sub
    hidden_dim = weights[1].shape[0]
    rows = 2 * hidden_dim + width
    return pl.pallas_call(
        mlp_kernel,
        grid=(groups,),
        in_specs=[per_group((width, tokens)), per_group((width, tokens)), pieces_spec(cot), whole(gain)]
        + [whole(w) for w in weights + carried],
        out_specs=[
            pieces_spec(cot),
            per_group((width, tokens)),
            per_group((width, tokens)),
            pl.BlockSpec((rows + spare, width), lambda g: (0, 0)),
            pl.BlockSpec((width, 128), lambda g: (0, 0)),
        ],
        out_shape=[
            jax.ShapeDtypeStruct(cot.shape, BF),
            jax.ShapeDtypeStruct((groups, width, tokens), F32),
            jax.ShapeDtypeStruct((groups, width, tokens), BF),
            jax.ShapeDtypeStruct((rows + spare, width), BF if spare else F32),
            jax.ShapeDtypeStruct((width, 128), F32),
        ],
        scratch_shapes=[
            pltpu.VMEM((rows, width), F32),
            pltpu.VMEM((width, tokens), BF),
            pltpu.VMEM((tokens, width), BF),
            pltpu.VMEM((width, tokens), BF),
            pltpu.VMEM((2, PIECE, tokens), F32),
            pltpu.VMEM((2, PIECE, tokens), BF),
            pltpu.VMEM((hidden_dim, tokens), BF),
            pltpu.VMEM((hidden_dim, tokens), BF),
        ],
        compiler_params=params(),
        cost_estimate=cost(4e9 * groups, 14 * groups * tokens * width, 0),
    )(flat, mixed, cot, gain, *weights, *carried)


def back_call(flat, triple, stat, grad_mixed, grad_att, gain, joint, like, carried, spare):
    rows = joint.shape[1]
    pieces, groups, sub, width = like.shape
    tokens = pieces * sub
    return pl.pallas_call(
        back_kernel,
        grid=(groups,),
        in_specs=[
            per_group((width, tokens)),
            per_group((3 * width, tokens)),
            per_group((16, tokens)),
            per_group((width, tokens)),
            per_group((width, tokens)),
            whole(gain),
            whole(joint),
        ]
        + [whole(w) for w in carried],
        out_specs=[
            pieces_spec(like),
            pl.BlockSpec((rows + spare, width), lambda g: (0, 0)),
            pl.BlockSpec((width, 128), lambda g: (0, 0)),
        ],
        out_shape=[
            jax.ShapeDtypeStruct(like.shape, BF),
            jax.ShapeDtypeStruct((rows + spare, width), BF if spare else F32),
            jax.ShapeDtypeStruct((width, 128), F32),
        ],
        scratch_shapes=[
            pltpu.VMEM((3 * width, width), F32),
            pltpu.VMEM((3 * width, tokens), BF),
            pltpu.VMEM((2, tokens, tokens), F32),
            pltpu.VMEM((2, tokens, tokens), F32),
            pltpu.VMEM((2, tokens, tokens), BF),
            pltpu.VMEM((2, tokens, tokens), BF),
        ],
        compiler_params=params(),
        cost_estimate=cost(6e9 * groups, 18 * groups * tokens * width, 0),
    )(flat, triple, stat, grad_mixed, grad_att, gain, joint, *carried)


def tie(value, *after):
    return lax.optimization_barrier((value,) + after)[0]


def peers(axis, low, high):
    return lax.axis_index(axis) // (1 << low) % (1 << (high - low)), 1 << (high - low)


def swap(values, axis, offset):
    return lax.ppermute(values, axis, [(i, i ^ offset) for i in range(lax.axis_size(axis))])


def scatter_sum(values, axis, low, high):
    mine, count = peers(axis, low, high)
    parts = values.reshape((count, values.shape[0] // count) + values.shape[1:])
    total = lax.dynamic_index_in_dim(parts, mine, 0, keepdims=False).astype(F32)
    for other in range(1, count):
        part = lax.dynamic_index_in_dim(parts, mine ^ other, 0, keepdims=False)
        total = total + swap(part, axis, other << low).astype(F32)
    return total.astype(BF)


def share_sum(values, axis, low, high):
    _, count = peers(axis, low, high)
    total = values.astype(F32)
    for other in range(1, count):
        total = total + swap(values, axis, other << low).astype(F32)
    return total.astype(BF)


def collect(values, axis, low, high):
    mine, count = peers(axis, low, high)
    got = jnp.stack([values] + [swap(values, axis, other << low) for other in range(1, count)])
    return jnp.concatenate(
        [lax.dynamic_index_in_dim(got, slot ^ mine, 0, keepdims=False) for slot in range(count)]
    )


def stages():
    row_bits = lax.axis_size("row").bit_length() - 1
    col_bits = lax.axis_size("col").bit_length() - 1
    return (("col", 0, 1), ("col", 1, col_bits), ("row", 0, row_bits))


def shards(
    activations,
    cotangent,
    first_gain,
    joint_weight,
    output_weight,
    second_gain,
    expand_weight,
    reduce_weight,
):
    row_devs = lax.axis_size("row")
    col_devs = lax.axis_size("col")
    devices = row_devs * col_devs
    both = ("row", "col")
    tile_rows, tile_cols, channels = activations.shape
    local_rows = GRID // row_devs
    local_cols = GRID // col_devs
    stride_rows = tile_rows // local_rows
    stride_cols = tile_cols // local_cols
    part_rows = stride_rows // row_devs
    part_cols = stride_cols // col_devs
    share = local_rows * local_cols
    tokens = GRID * GRID
    factor = float(tile_rows * tile_cols * devices) ** (-0.5)

    chunks = 2
    chunk_rows = part_rows // chunks
    chunk_groups = chunk_rows * part_cols

    kernels_pack = share % SUB == 0 and col_devs == SUB

    def pack(tile, chunk):
        if kernels_pack:
            tile = tile.reshape(local_rows, row_devs, part_rows, tile_cols, channels)
            return pack_call(tile, chunk, chunk_rows, row_devs, col_devs, part_cols)
        sends = tile.reshape(
            local_rows, row_devs, part_rows, local_cols, part_cols, col_devs, channels
        )[:, :, chunk * chunk_rows : (chunk + 1) * chunk_rows]
        return sends.transpose(1, 5, 2, 4, 0, 3, 6).reshape(devices, chunk_groups, share, channels)

    def send(sends, *after):
        got = lax.all_to_all(tie(sends, *after), both, split_axis=0, concat_axis=0, tiled=True)
        if share % SUB:
            got = got.transpose(0, 2, 1, 3).reshape(tokens // SUB, SUB, chunk_groups, channels)
            got = got.transpose(0, 2, 1, 3)
        return got.reshape(tokens // SUB, chunk_groups, SUB, channels)

    def give_back(pieces, *after):
        if share % SUB:
            pieces = pieces.transpose(0, 2, 1, 3).reshape(devices, share, chunk_groups, channels)
            pieces = pieces.transpose(0, 2, 1, 3)
        pieces = tie(pieces.reshape(devices, chunk_groups, share, channels), *after)
        return lax.all_to_all(pieces, both, split_axis=0, concat_axis=0, tiled=True)

    def to_tile(arrived):
        if kernels_pack:
            tile = unpack_call(arrived, local_rows, part_rows, tile_cols, row_devs)
            return tile.reshape(tile_rows, tile_cols, channels)
        arrived = [
            part.reshape(row_devs, col_devs, chunk_rows, part_cols, local_rows, local_cols, channels)
            for part in arrived
        ]
        return jnp.concatenate(arrived, axis=2).transpose(4, 0, 2, 5, 3, 1, 6).reshape(
            tile_rows, tile_cols, channels
        )

    arrived = []
    for k, tile in enumerate([activations] * chunks + [cotangent] * chunks):
        sends = pack(tile, k % chunks)
        arrived.append(send(sends, *arrived[-1:]))
    act, cot = arrived[:chunks], arrived[chunks:]
    gain_one, gain_two, joint_t, out_t, up_t, down_t = prepare_call(
        first_gain, second_gain, joint_weight, output_weight, expand_weight, reduce_weight, tokens
    )
    weights = (out_t, up_t, down_t, reduce_weight, expand_weight, output_weight)
    hidden_dim = expand_weight.shape[1]
    tail_rows, head_rows = 2 * hidden_dim + channels, 3 * channels
    unit = SUB * devices
    fronts = []
    for k in range(chunks):
        fronts.append(attend_call(act[k], gain_one, joint_t))
    tails, out_parts, carried = [], [], ()
    before = cot[-1:]
    for k in range(chunks):
        flat, _, mixed, _ = fronts[k]
        spare = unit - tail_rows % unit if k == chunks - 1 else 0
        tails.append(mlp_call(flat, mixed, cot[k], gain_two, weights, carried, spare))
        carried = tails[-1][3:]
        out_parts.append(give_back(tails[-1][0], *before))
        before = out_parts[-1:]
    steps = stages()
    tail_sum = scatter_sum(carried[0], *steps[0])
    heads, in_parts, carried = [], [], ()
    for k in range(chunks):
        flat, triple, _, stat = fronts[k]
        _, grad_att, grad_mixed = tails[k][:3]
        spare = unit - head_rows % unit if k == chunks - 1 else 0
        grad_mixed = tie(grad_mixed, out_parts[k])
        heads.append(
            back_call(flat, triple, stat, grad_mixed, grad_att, gain_one, joint_weight, cot[k], carried, spare)
        )
        carried = heads[-1][1:]
        in_parts.append(give_back(heads[-1][0], *before))
        before = in_parts[-1:]
        tail_sum = scatter_sum(tail_sum, *steps[k + 1])
    head_sum = carried[0]
    near, cols, rows = steps
    head_sum = scatter_sum(head_sum, *near)
    head_sum = scatter_sum(head_sum, *cols)
    tail_sum = collect(tail_sum, *rows)
    head_sum = share_sum(head_sum, *rows)
    tail_sum = collect(tail_sum, *cols)
    head_sum = collect(head_sum, *cols)
    tail_sum = collect(tail_sum, *near)
    head_sum = collect(head_sum, *near)
    head_sum = head_sum.astype(F32) * factor
    tail_sum = tail_sum.astype(F32) * factor
    block_out = to_tile(out_parts)
    grad_input = to_tile(in_parts)
    return (
        block_out,
        grad_input,
        head_sum[:head_rows].T,
        tail_sum[2 * hidden_dim : tail_rows],
        tail_sum[hidden_dim : 2 * hidden_dim].T,
        tail_sum[:hidden_dim],
        head_sum[head_rows],
        tail_sum[tail_rows],
    )


def solution(mesh):
    placed = (P("row", "col", None), P("row", "col", None), P(), P(), P(), P(), P(), P())
    return jax.shard_map(shards, mesh=mesh, in_specs=placed, out_specs=placed, check_vma=False)
```

```python
import jax
import jax.numpy as jnp
from jax import lax
from jax.experimental import pallas as pl
from jax.experimental.pallas import tpu as pltpu
from jax.sharding import PartitionSpec as P


HEADS = 12
GRID = 16
SUB = 8
PIECE = 512
EPSILON = 1e-05
INV_ROOT_TAU = 0.3989422804014327
SQRT_HALF = 0.7071067811865476
LOG2E = 1.4426950408889634
BF = jnp.bfloat16
F32 = jnp.float32

ERFC_P = 0.4
ERFC_C = (
    0.2256758624069583,
    0.22566957331484927,
    0.20784305752189558,
    0.16853970978283367,
    0.1414388899580775,
    -0.005621196233437842,
    0.16909944767289115,
    -0.18290897174728507,
    0.05026375199644912,
)


def nn(a, b):
    return lax.dot_general(a, b, (((1,), (0,)), ((), ())), preferred_element_type=F32)


def nt(a, b):
    return lax.dot_general(a, b, (((1,), (1,)), ((), ())), preferred_element_type=F32)


def tn(a, b):
    return lax.dot_general(a, b, (((0,), (0,)), ((), ())), preferred_element_type=F32)


def gelu_parts(pre):
    gauss = jnp.exp2(pre * pre * (-0.5 * LOG2E))
    t = 1.0 / (1.0 + (ERFC_P * SQRT_HALF) * jnp.abs(pre))
    poly = jnp.full_like(t, 0.5 * ERFC_C[-1])
    for coef in ERFC_C[-2::-1]:
        poly = poly * t + 0.5 * coef
    half_erfc = gauss * (t * poly)
    phi = jnp.where(pre < 0.0, half_erfc, 1.0 - half_erfc)
    return phi, gauss


def normalize(values):
    center = values - jnp.mean(values, axis=0, keepdims=True)
    inv_std = lax.rsqrt(jnp.mean(center * center, axis=0, keepdims=True) + EPSILON)
    return center * inv_std, inv_std


def norm_back(scaled, normed, inv_std):
    return inv_std * (
        scaled
        - jnp.mean(scaled, axis=0, keepdims=True)
        - normed * jnp.mean(scaled * normed, axis=0, keepdims=True)
    )


def load_rows(ref):
    pieces, _, sub, width = ref.shape
    return ref[...].reshape(pieces, sub, width).astype(F32).reshape(pieces * sub, width)


def store_rows(ref, rows):
    pieces, _, sub, width = ref.shape
    ref[...] = rows.reshape(pieces, 1, sub, width).astype(ref.dtype)


def fold_lanes(values):
    total = values[:, :128]
    for start in range(128, values.shape[1], 128):
        total = total + values[:, start : start + 128]
    return total


def begin(carried, acc_ref, grad_gain_ref):
    if carried:
        acc_ref[...] = carried[0][...]
        grad_gain_ref[...] = carried[1][...]
    else:
        acc_ref[...] = jnp.zeros_like(acc_ref)
        grad_gain_ref[...] = jnp.zeros_like(grad_gain_ref)


def finish(acc_ref, grads_ref, grad_gain_ref):
    rows = acc_ref.shape[0]
    grads_ref[:rows] = acc_ref[...].astype(grads_ref.dtype)
    if grads_ref.shape[0] > rows:
        gains = jnp.sum(grad_gain_ref[...].T, axis=0, keepdims=True)
        spare = grads_ref.shape[0] - rows
        first = lax.broadcasted_iota(jnp.int32, (spare, gains.shape[1]), 0) == 0
        grads_ref[rows:] = jnp.where(first, gains, 0.0).astype(grads_ref.dtype)


def lane_halves(count):
    return [slice(start, start + 128) for start in range(0, count, 128)]


def attend_kernel(
    act_ref, gain_ref, joint_ref, out_t_ref,
    flat_ref, triple_ref, mixed_ref, stat_ref, attended_ref, score_ref,
):
    width, tokens = gain_ref.shape
    head = width // HEADS
    factor = head ** (-0.5) * LOG2E
    flat = load_rows(act_ref).T
    flat_ref[0] = flat.astype(BF)
    normed, _ = normalize(flat)
    scaled = (normed * gain_ref[...]).astype(BF)
    triple_ref[0] = nn(joint_ref[...], scaled).astype(BF)

    def score(h):
        queries = triple_ref[0, h * head : (h + 1) * head]
        keys = triple_ref[0, width + h * head : width + (h + 1) * head]
        score_ref[h % 2] = tn(keys, queries)

    score(0)
    for h in range(HEADS):
        if h + 1 < HEADS:
            score(h + 1)
        values = triple_ref[0, 2 * width + h * head : 2 * width + (h + 1) * head]
        for lanes in lane_halves(tokens):
            scores = score_ref[h % 2, :, lanes]
            top = jnp.max(scores, axis=0, keepdims=True)
            weights = jnp.exp2((scores - top) * factor)
            total = jnp.sum(weights, axis=0, keepdims=True)
            stat_ref[0, h : h + 1, lanes] = top * factor + jnp.log2(total)
            weights = (weights * (1.0 / total)).astype(BF)
            mixed_ref[0, h * head : (h + 1) * head, lanes] = nn(values, weights).astype(BF)
    attended_ref[0] = flat_ref[0].astype(F32) + nn(out_t_ref[...], mixed_ref[0])


def mlp_kernel(
    attended_ref, mixed_ref, cot_ref, gain_ref, up_t_ref, down_t_ref, down_ref, up_ref, out_w_ref,
    *rest,
):
    carried = rest[:-13]
    result_ref, grad_att_ref, grad_mixed_ref, grads_ref, grad_gain_ref, acc_ref = rest[-13:-7]
    scaled_ref, cot_b_ref, cot_tb_ref, pre_ref, grad_hidden_ref, hidden_ref, grad_pre_ref = rest[-7:]
    step = pl.program_id(0)
    hidden_dim = up_ref.shape[1]

    @pl.when(step == 0)
    def _():
        begin(carried, acc_ref, grad_gain_ref)

    cot_rows = load_rows(cot_ref)
    cot_b = cot_rows.astype(BF)
    cot_t = cot_rows.T
    cot_tb = cot_t.astype(BF)
    mixed = mixed_ref[0]
    attended = attended_ref[0]
    normed, inv_std = normalize(attended)
    gain = gain_ref[...]
    scaled = (normed * gain).astype(BF)
    scaled_ref[...] = scaled
    cot_b_ref[...] = cot_b
    cot_tb_ref[...] = cot_tb

    def products(n):
        part = slice(n * PIECE, (n + 1) * PIECE)
        pre_ref[n % 2] = nn(up_t_ref[part], scaled_ref[...])
        grad_hidden_ref[n % 2] = nn(down_ref[part], cot_tb_ref[...]).astype(BF)

    def activate(n):
        for start in range(0, PIECE, 32):
            some = slice(start, start + 32)
            here = slice(n * PIECE + start, n * PIECE + start + 32)
            pre = pre_ref[n % 2, some]
            phi, gauss = gelu_parts(pre)
            hidden_ref[here] = (pre * phi).astype(BF)
            slope = phi + pre * gauss * INV_ROOT_TAU
            grad_pre_ref[here] = (grad_hidden_ref[n % 2, some].astype(F32) * slope).astype(BF)

    def gather(n):
        part = slice(n * PIECE, (n + 1) * PIECE)
        acc_ref[part] += nn(hidden_ref[part], cot_b_ref[...])
        there = slice(hidden_dim + n * PIECE, hidden_dim + (n + 1) * PIECE)
        acc_ref[there] += nt(grad_pre_ref[part], scaled_ref[...])

    pieces = hidden_dim // PIECE
    products(0)
    for n in range(pieces):
        if n + 1 < pieces:
            products(n + 1)
        activate(n)
        if n:
            gather(n - 1)
    gather(pieces - 1)
    grad_scaled = nn(up_ref[...], grad_pre_ref[...])
    result = attended + nn(down_t_ref[...], hidden_ref[...])
    store_rows(result_ref, result.T)
    grad_gain_ref[...] += fold_lanes(grad_scaled * normed)
    grad_att = cot_t + norm_back(grad_scaled * gain, normed, inv_std)
    grad_att_ref[0] = grad_att
    grad_att_b = grad_att.astype(BF)
    acc_ref[2 * hidden_dim :] += nt(mixed, grad_att_b)
    grad_mixed_ref[0] = nn(out_w_ref[...], grad_att_b).astype(BF)

    @pl.when(step == pl.num_programs(0) - 1)
    def _():
        finish(acc_ref, grads_ref, grad_gain_ref)


def back_kernel(
    flat_ref, triple_ref, stat_ref, grad_mixed_ref, grad_att_ref, gain_ref, joint_ref,
    *rest,
):
    carried = rest[:-9]
    grad_in_ref, grads_ref, grad_gain_ref, acc_ref, grad_triple_ref = rest[-9:-4]
    score_ref, slope_ref, grad_score_ref, weight_ref = rest[-4:]
    step = pl.program_id(0)
    width = gain_ref.shape[0]
    head = width // HEADS
    scale = head ** (-0.5)

    @pl.when(step == 0)
    def _():
        begin(carried, acc_ref, grad_gain_ref)

    tokens = gain_ref.shape[1]

    def rows(part, h):
        return slice(part * width + h * head, part * width + (h + 1) * head)

    def products(h):
        score_ref[h % 2] = tn(triple_ref[0, rows(1, h)], triple_ref[0, rows(0, h)])
        slope_ref[h % 2] = tn(triple_ref[0, rows(2, h)], grad_mixed_ref[0, rows(0, h)])

    def weigh(h):
        for lanes in lane_halves(tokens):
            weights = jnp.exp2(score_ref[h % 2, :, lanes] * (scale * LOG2E) - stat_ref[0, h : h + 1, lanes])
            grad_weights = slope_ref[h % 2, :, lanes]
            inner = jnp.sum(weights * grad_weights, axis=0, keepdims=True)
            grad_score_ref[h % 2, :, lanes] = (weights * (grad_weights - inner) * scale).astype(BF)
            weight_ref[h % 2, :, lanes] = weights.astype(BF)

    def back(h):
        grad_scores = grad_score_ref[h % 2]
        grad_triple_ref[rows(0, h)] = nn(triple_ref[0, rows(1, h)], grad_scores).astype(BF)
        grad_triple_ref[rows(1, h)] = nt(triple_ref[0, rows(0, h)], grad_scores).astype(BF)
        grad_triple_ref[rows(2, h)] = nt(grad_mixed_ref[0, rows(0, h)], weight_ref[h % 2]).astype(BF)

    products(0)
    for h in range(HEADS):
        if h + 1 < HEADS:
            products(h + 1)
        weigh(h)
        if h:
            back(h - 1)
    back(HEADS - 1)
    normed, inv_std = normalize(flat_ref[0].astype(F32))
    gain = gain_ref[...]
    scaled = (normed * gain).astype(BF)
    acc_ref[...] += nt(grad_triple_ref[...], scaled)
    grad_scaled = nn(joint_ref[...], grad_triple_ref[...])
    grad_gain_ref[...] += fold_lanes(grad_scaled * normed)
    grad_in = grad_att_ref[0] + norm_back(grad_scaled * gain, normed, inv_std)
    store_rows(grad_in_ref, grad_in.T)

    @pl.when(step == pl.num_programs(0) - 1)
    def _():
        finish(acc_ref, grads_ref, grad_gain_ref)


def prepare_kernel(
    gain_one_ref, gain_two_ref, joint_ref, out_w_ref, up_ref, down_ref,
    wide_one_ref, wide_two_ref, joint_t_ref, out_t_ref, up_t_ref, down_t_ref,
):
    tokens = wide_one_ref.shape[1]
    for gain_ref, wide_ref in ((gain_one_ref, wide_one_ref), (gain_two_ref, wide_two_ref)):
        wide_ref[...] = jnp.broadcast_to(gain_ref[...], (tokens, gain_ref.shape[1])).T
    for weight_ref, turned_ref in (
        (joint_ref, joint_t_ref),
        (out_w_ref, out_t_ref),
        (up_ref, up_t_ref),
        (down_ref, down_t_ref),
    ):
        turned_ref[...] = weight_ref[...].T


def prepare_call(gain_one, gain_two, joint, out_w, up, down, tokens):
    width = gain_one.shape[0]
    turned = [jax.ShapeDtypeStruct(w.shape[::-1], w.dtype) for w in (joint, out_w, up, down)]
    wide = jax.ShapeDtypeStruct((width, tokens), F32)
    return pl.pallas_call(
        prepare_kernel,
        out_shape=[wide, wide] + turned,
        compiler_params=pltpu.CompilerParams(vmem_limit_bytes=60 << 20),
        cost_estimate=cost(1e6, 16e6, 0),
    )(gain_one.reshape(1, width), gain_two.reshape(1, width), joint, out_w, up, down)


def pack_kernel(tile_ref, sends_ref, rows_ref):
    lines, _, chunk_rows, columns, width = tile_ref.shape
    cols, groups, share, _ = sends_ref.shape
    for line in range(lines):
        for row in range(chunk_rows):
            for block in range(columns // cols):
                near, part = block // (columns // cols // (share // lines)), block % (groups // chunk_rows)
                start = (row * (groups // chunk_rows) + part) * share + line * (share // lines) + near
                values = tile_ref[line, 0, row, block * cols : (block + 1) * cols].astype(F32)
                for lane in range(width // 128):
                    rows_ref[lane, pl.ds(start, cols, stride=groups * share)] = values[
                        :, lane * 128 : (lane + 1) * 128
                    ]
    for lane in range(width // 128):
        sends_ref[:, :, :, lane * 128 : (lane + 1) * 128] = (
            rows_ref[lane].reshape(cols, groups, share, 128).astype(BF)
        )


def unpack_kernel(*refs):
    *arrived, tile_ref, rows_ref = refs
    lines, _, all_rows, columns, width = tile_ref.shape
    cols, groups, share, _ = arrived[0].shape
    chunk_rows = all_rows // len(arrived)
    parts = groups // chunk_rows
    for chunk, part_ref in enumerate(arrived):
        for lane in range(width // 128):
            piece = part_ref[:, :, :, lane * 128 : (lane + 1) * 128].astype(F32)
            rows_ref[lane] = piece.reshape(cols * groups * share, 128)
        for line in range(lines):
            for row in range(chunk_rows):
                for block in range(columns // cols):
                    near, part = block // parts, block % parts
                    start = (row * parts + part) * share + line * (share // lines) + near
                    values = jnp.concatenate(
                        [
                            rows_ref[lane, pl.ds(start, cols, stride=groups * share)]
                            for lane in range(width // 128)
                        ],
                        axis=1,
                    )
                    tile_ref[line, 0, chunk * chunk_rows + row, block * cols : (block + 1) * cols] = (
                        values.astype(BF)
                    )


def pack_call(tile, chunk, chunk_rows, row_devs, cols, parts):
    lines, _, _, columns, width = tile.shape
    groups, share = chunk_rows * parts, lines * columns // (cols * parts)
    return pl.pallas_call(
        pack_kernel,
        grid=(row_devs,),
        in_specs=[
            pl.BlockSpec((lines, 1, chunk_rows, columns, width), lambda r: (0, r, chunk, 0, 0))
        ],
        out_specs=pl.BlockSpec((cols, groups, share, width), lambda r: (r, 0, 0, 0)),
        out_shape=jax.ShapeDtypeStruct((row_devs * cols, groups, share, width), BF),
        scratch_shapes=[pltpu.VMEM((width // 128, cols * groups * share, 128), F32)],
        compiler_params=params(),
        cost_estimate=cost(1e6, 4 * row_devs * cols * groups * share * width, 0),
    )(tile)


def unpack_call(arrived, lines, all_rows, columns, row_devs):
    devices, groups, share, width = arrived[0].shape
    cols = devices // row_devs
    piece = pl.BlockSpec((cols, groups, share, width), lambda r: (r, 0, 0, 0))
    return pl.pallas_call(
        unpack_kernel,
        grid=(row_devs,),
        in_specs=[piece] * len(arrived),
        out_specs=pl.BlockSpec((lines, 1, all_rows, columns, width), lambda r: (0, r, 0, 0, 0)),
        out_shape=jax.ShapeDtypeStruct((lines, row_devs, all_rows, columns, width), BF),
        scratch_shapes=[pltpu.VMEM((width // 128, cols * groups * share, 128), F32)],
        compiler_params=params(),
        cost_estimate=cost(1e6, 4 * lines * row_devs * all_rows * columns * width, 0),
    )(*arrived)


def whole(array):
    return pl.BlockSpec(array.shape, lambda g: (0,) * array.ndim)


def per_group(shape):
    return pl.BlockSpec((1,) + shape, lambda g: (g, 0, 0))


def pieces_spec(array):
    pieces, _, sub, width = array.shape
    return pl.BlockSpec((pieces, 1, sub, width), lambda g: (0, g, 0, 0))


def params():
    return pltpu.CompilerParams(dimension_semantics=("arbitrary",), vmem_limit_bytes=60 << 20)


def cost(flops, bytes_moved, exps):
    return pl.CostEstimate(flops=int(flops), bytes_accessed=int(bytes_moved), transcendentals=int(exps))


def attend_call(act, gain, joint_t, out_t):
    pieces, groups, sub, width = act.shape
    tokens = pieces * sub
    return pl.pallas_call(
        attend_kernel,
        grid=(groups,),
        in_specs=[pieces_spec(act), whole(gain), whole(joint_t), whole(out_t)],
        out_specs=[
            per_group((width, tokens)),
            per_group((3 * width, tokens)),
            per_group((width, tokens)),
            per_group((16, tokens)),
            per_group((width, tokens)),
        ],
        out_shape=[
            jax.ShapeDtypeStruct((groups, width, tokens), BF),
            jax.ShapeDtypeStruct((groups, 3 * width, tokens), BF),
            jax.ShapeDtypeStruct((groups, width, tokens), BF),
            jax.ShapeDtypeStruct((groups, 16, tokens), F32),
            jax.ShapeDtypeStruct((groups, width, tokens), F32),
        ],
        scratch_shapes=[pltpu.VMEM((2, tokens, tokens), F32)],
        compiler_params=params(),
        cost_estimate=cost(3e9 * groups, 12 * groups * tokens * width, 0),
    )(act, gain, joint_t, out_t)


def mlp_call(attended, mixed, cot, gain, weights, carried, spare):
    pieces, groups, sub, width = cot.shape
    tokens = pieces * sub
    hidden_dim = weights[0].shape[0]
    rows = 2 * hidden_dim + width
    return pl.pallas_call(
        mlp_kernel,
        grid=(groups,),
        in_specs=[per_group((width, tokens)), per_group((width, tokens)), pieces_spec(cot), whole(gain)]
        + [whole(w) for w in weights + carried],
        out_specs=[
            pieces_spec(cot),
            per_group((width, tokens)),
            per_group((width, tokens)),
            pl.BlockSpec((rows + spare, width), lambda g: (0, 0)),
            pl.BlockSpec((width, 128), lambda g: (0, 0)),
        ],
        out_shape=[
            jax.ShapeDtypeStruct(cot.shape, BF),
            jax.ShapeDtypeStruct((groups, width, tokens), F32),
            jax.ShapeDtypeStruct((groups, width, tokens), BF),
            jax.ShapeDtypeStruct((rows + spare, width), BF if spare else F32),
            jax.ShapeDtypeStruct((width, 128), F32),
        ],
        scratch_shapes=[
            pltpu.VMEM((rows, width), F32),
            pltpu.VMEM((width, tokens), BF),
            pltpu.VMEM((tokens, width), BF),
            pltpu.VMEM((width, tokens), BF),
            pltpu.VMEM((2, PIECE, tokens), F32),
            pltpu.VMEM((2, PIECE, tokens), BF),
            pltpu.VMEM((hidden_dim, tokens), BF),
            pltpu.VMEM((hidden_dim, tokens), BF),
        ],
        compiler_params=params(),
        cost_estimate=cost(4e9 * groups, 14 * groups * tokens * width, 0),
    )(attended, mixed, cot, gain, *weights, *carried)


def back_call(flat, triple, stat, grad_mixed, grad_att, gain, joint, like, carried, spare):
    rows = joint.shape[1]
    pieces, groups, sub, width = like.shape
    tokens = pieces * sub
    return pl.pallas_call(
        back_kernel,
        grid=(groups,),
        in_specs=[
            per_group((width, tokens)),
            per_group((3 * width, tokens)),
            per_group((16, tokens)),
            per_group((width, tokens)),
            per_group((width, tokens)),
            whole(gain),
            whole(joint),
        ]
        + [whole(w) for w in carried],
        out_specs=[
            pieces_spec(like),
            pl.BlockSpec((rows + spare, width), lambda g: (0, 0)),
            pl.BlockSpec((width, 128), lambda g: (0, 0)),
        ],
        out_shape=[
            jax.ShapeDtypeStruct(like.shape, BF),
            jax.ShapeDtypeStruct((rows + spare, width), BF if spare else F32),
            jax.ShapeDtypeStruct((width, 128), F32),
        ],
        scratch_shapes=[
            pltpu.VMEM((3 * width, width), F32),
            pltpu.VMEM((3 * width, tokens), BF),
            pltpu.VMEM((2, tokens, tokens), F32),
            pltpu.VMEM((2, tokens, tokens), F32),
            pltpu.VMEM((2, tokens, tokens), BF),
            pltpu.VMEM((2, tokens, tokens), BF),
        ],
        compiler_params=params(),
        cost_estimate=cost(6e9 * groups, 18 * groups * tokens * width, 0),
    )(flat, triple, stat, grad_mixed, grad_att, gain, joint, *carried)


def tie(value, *after):
    return lax.optimization_barrier((value,) + after)[0]


def peers(axis, low, high):
    return lax.axis_index(axis) // (1 << low) % (1 << (high - low)), 1 << (high - low)


def swap(values, axis, offset):
    return lax.ppermute(values, axis, [(i, i ^ offset) for i in range(lax.axis_size(axis))])


def scatter_sum(values, axis, low, high):
    mine, count = peers(axis, low, high)
    parts = values.reshape((count, values.shape[0] // count) + values.shape[1:])
    total = lax.dynamic_index_in_dim(parts, mine, 0, keepdims=False).astype(F32)
    for other in range(1, count):
        part = lax.dynamic_index_in_dim(parts, mine ^ other, 0, keepdims=False)
        total = total + swap(part, axis, other << low).astype(F32)
    return total.astype(BF)


def share_sum(values, axis, low, high):
    _, count = peers(axis, low, high)
    total = values.astype(F32)
    for other in range(1, count):
        total = total + swap(values, axis, other << low).astype(F32)
    return total.astype(BF)


def collect(values, axis, low, high):
    mine, count = peers(axis, low, high)
    got = jnp.stack([values] + [swap(values, axis, other << low) for other in range(1, count)])
    return jnp.concatenate(
        [lax.dynamic_index_in_dim(got, slot ^ mine, 0, keepdims=False) for slot in range(count)]
    )


def stages():
    row_bits = lax.axis_size("row").bit_length() - 1
    col_bits = lax.axis_size("col").bit_length() - 1
    return (("col", 0, 1), ("col", 1, col_bits), ("row", 0, row_bits))


def shards(
    activations,
    cotangent,
    first_gain,
    joint_weight,
    output_weight,
    second_gain,
    expand_weight,
    reduce_weight,
):
    row_devs = lax.axis_size("row")
    col_devs = lax.axis_size("col")
    devices = row_devs * col_devs
    both = ("row", "col")
    tile_rows, tile_cols, channels = activations.shape
    local_rows = GRID // row_devs
    local_cols = GRID // col_devs
    stride_rows = tile_rows // local_rows
    stride_cols = tile_cols // local_cols
    part_rows = stride_rows // row_devs
    part_cols = stride_cols // col_devs
    share = local_rows * local_cols
    tokens = GRID * GRID
    factor = float(tile_rows * tile_cols * devices) ** (-0.5)

    chunks = 2
    chunk_rows = part_rows // chunks
    chunk_groups = chunk_rows * part_cols

    kernels_pack = share % SUB == 0 and col_devs == SUB

    def pack(tile, chunk):
        if kernels_pack:
            tile = tile.reshape(local_rows, row_devs, part_rows, tile_cols, channels)
            return pack_call(tile, chunk, chunk_rows, row_devs, col_devs, part_cols)
        sends = tile.reshape(
            local_rows, row_devs, part_rows, local_cols, part_cols, col_devs, channels
        )[:, :, chunk * chunk_rows : (chunk + 1) * chunk_rows]
        return sends.transpose(1, 5, 2, 4, 0, 3, 6).reshape(devices, chunk_groups, share, channels)

    def send(sends, *after):
        got = lax.all_to_all(tie(sends, *after), both, split_axis=0, concat_axis=0, tiled=True)
        if share % SUB:
            got = got.transpose(0, 2, 1, 3).reshape(tokens // SUB, SUB, chunk_groups, channels)
            got = got.transpose(0, 2, 1, 3)
        return got.reshape(tokens // SUB, chunk_groups, SUB, channels)

    def give_back(pieces, *after):
        if share % SUB:
            pieces = pieces.transpose(0, 2, 1, 3).reshape(devices, share, chunk_groups, channels)
            pieces = pieces.transpose(0, 2, 1, 3)
        pieces = tie(pieces.reshape(devices, chunk_groups, share, channels), *after)
        return lax.all_to_all(pieces, both, split_axis=0, concat_axis=0, tiled=True)

    def to_tile(arrived):
        if kernels_pack:
            tile = unpack_call(arrived, local_rows, part_rows, tile_cols, row_devs)
            return tile.reshape(tile_rows, tile_cols, channels)
        arrived = [
            part.reshape(row_devs, col_devs, chunk_rows, part_cols, local_rows, local_cols, channels)
            for part in arrived
        ]
        return jnp.concatenate(arrived, axis=2).transpose(4, 0, 2, 5, 3, 1, 6).reshape(
            tile_rows, tile_cols, channels
        )

    arrived = []
    for k, tile in enumerate([activations] * chunks + [cotangent] * chunks):
        sends = pack(tile, k % chunks)
        arrived.append(send(sends, *arrived[-1:]))
    act, cot = arrived[:chunks], arrived[chunks:]
    gain_one, gain_two, joint_t, out_t, up_t, down_t = prepare_call(
        first_gain, second_gain, joint_weight, output_weight, expand_weight, reduce_weight, tokens
    )
    weights = (up_t, down_t, reduce_weight, expand_weight, output_weight)
    hidden_dim = expand_weight.shape[1]
    tail_rows, head_rows = 2 * hidden_dim + channels, 3 * channels
    unit = SUB * devices
    fronts = []
    for k in range(chunks):
        fronts.append(attend_call(act[k], gain_one, joint_t, out_t))
    tails, out_parts, carried = [], [], ()
    before = cot[-1:]
    for k in range(chunks):
        _, _, mixed, _, attended = fronts[k]
        spare = unit - tail_rows % unit if k == chunks - 1 else 0
        tails.append(mlp_call(attended, mixed, cot[k], gain_two, weights, carried, spare))
        carried = tails[-1][3:]
        out_parts.append(give_back(tails[-1][0], *before))
        before = out_parts[-1:]
    steps = stages()
    tail_sum = scatter_sum(carried[0], *steps[0])
    heads, in_parts, carried = [], [], ()
    for k in range(chunks):
        flat, triple, _, stat, _ = fronts[k]
        _, grad_att, grad_mixed = tails[k][:3]
        spare = unit - head_rows % unit if k == chunks - 1 else 0
        grad_mixed = tie(grad_mixed, out_parts[k])
        heads.append(
            back_call(flat, triple, stat, grad_mixed, grad_att, gain_one, joint_weight, cot[k], carried, spare)
        )
        carried = heads[-1][1:]
        in_parts.append(give_back(heads[-1][0], *before))
        before = in_parts[-1:]
        tail_sum = scatter_sum(tail_sum, *steps[k + 1])
    head_sum = carried[0]
    near, cols, rows = steps
    head_sum = scatter_sum(head_sum, *near)
    head_sum = scatter_sum(head_sum, *cols)
    tail_sum = collect(tail_sum, *rows)
    head_sum = share_sum(head_sum, *rows)
    tail_sum = collect(tail_sum, *cols)
    head_sum = collect(head_sum, *cols)
    tail_sum = collect(tail_sum, *near)
    head_sum = collect(head_sum, *near)
    head_sum = head_sum.astype(F32) * factor
    tail_sum = tail_sum.astype(F32) * factor
    block_out = to_tile(out_parts)
    grad_input = to_tile(in_parts)
    return (
        block_out,
        grad_input,
        head_sum[:head_rows].T,
        tail_sum[2 * hidden_dim : tail_rows],
        tail_sum[hidden_dim : 2 * hidden_dim].T,
        tail_sum[:hidden_dim],
        head_sum[head_rows],
        tail_sum[tail_rows],
    )


def solution(mesh):
    placed = (P("row", "col", None), P("row", "col", None), P(), P(), P(), P(), P(), P())
    return jax.shard_map(shards, mesh=mesh, in_specs=placed, out_specs=placed, check_vma=False)
```

```python
import jax
import jax.numpy as jnp
from jax import lax
from jax.experimental import pallas as pl
from jax.experimental.pallas import tpu as pltpu
from jax.sharding import PartitionSpec as P


HEADS = 12
GRID = 16
SUB = 8
PIECE = 512
EPSILON = 1e-05
INV_ROOT_TAU = 0.3989422804014327
SQRT_HALF = 0.7071067811865476
LOG2E = 1.4426950408889634
BF = jnp.bfloat16
F32 = jnp.float32

ERFC_P = 0.4
ERFC_C = (
    0.2256758624069583,
    0.22566957331484927,
    0.20784305752189558,
    0.16853970978283367,
    0.1414388899580775,
    -0.005621196233437842,
    0.16909944767289115,
    -0.18290897174728507,
    0.05026375199644912,
)


def nn(a, b):
    return lax.dot_general(a, b, (((1,), (0,)), ((), ())), preferred_element_type=F32)


def nt(a, b):
    return lax.dot_general(a, b, (((1,), (1,)), ((), ())), preferred_element_type=F32)


def tn(a, b):
    return lax.dot_general(a, b, (((0,), (0,)), ((), ())), preferred_element_type=F32)


def gelu_parts(pre):
    gauss = jnp.exp2(pre * pre * (-0.5 * LOG2E))
    t = 1.0 / (1.0 + (ERFC_P * SQRT_HALF) * jnp.abs(pre))
    poly = jnp.full_like(t, 0.5 * ERFC_C[-1])
    for coef in ERFC_C[-2::-1]:
        poly = poly * t + 0.5 * coef
    half_erfc = gauss * (t * poly)
    phi = jnp.where(pre < 0.0, half_erfc, 1.0 - half_erfc)
    return phi, gauss


def normalize(values):
    center = values - jnp.mean(values, axis=0, keepdims=True)
    inv_std = lax.rsqrt(jnp.mean(center * center, axis=0, keepdims=True) + EPSILON)
    return center * inv_std, inv_std


def norm_back(scaled, normed, inv_std):
    return inv_std * (
        scaled
        - jnp.mean(scaled, axis=0, keepdims=True)
        - normed * jnp.mean(scaled * normed, axis=0, keepdims=True)
    )


def load_rows(ref):
    pieces, _, sub, width = ref.shape
    return ref[...].reshape(pieces, sub, width).astype(F32).reshape(pieces * sub, width)


def store_rows(ref, rows):
    pieces, _, sub, width = ref.shape
    ref[...] = rows.reshape(pieces, 1, sub, width).astype(ref.dtype)


def fold_lanes(values):
    total = values[:, :128]
    for start in range(128, values.shape[1], 128):
        total = total + values[:, start : start + 128]
    return total


def by_rows(rows, body):
    def step(n, _):
        body(pl.ds(pl.multiple_of(n * 128, 128), 128))
        return 0

    lax.fori_loop(0, rows // 128, step, 0)


def begin(carried, acc_ref, grad_gain_ref):
    def fill(part):
        if carried:
            acc_ref[part] = carried[0][part]
        else:
            acc_ref[part] = jnp.zeros((128, acc_ref.shape[1]), F32)

    by_rows(acc_ref.shape[0], fill)
    if carried:
        grad_gain_ref[...] = carried[1][...]
    else:
        grad_gain_ref[...] = jnp.zeros_like(grad_gain_ref)


def finish(acc_ref, grads_ref, grad_gain_ref):
    rows = acc_ref.shape[0]

    def cast(part):
        grads_ref[part] = acc_ref[part].astype(grads_ref.dtype)

    by_rows(rows, cast)
    if grads_ref.shape[0] > rows:
        gains = jnp.sum(grad_gain_ref[...].T, axis=0, keepdims=True)
        spare = grads_ref.shape[0] - rows
        first = lax.broadcasted_iota(jnp.int32, (spare, gains.shape[1]), 0) == 0
        grads_ref[rows:] = jnp.where(first, gains, 0.0).astype(grads_ref.dtype)


def lane_halves(count):
    return [slice(start, start + 128) for start in range(0, count, 128)]


def attend_kernel(
    act_ref, gain_ref, joint_ref, out_t_ref,
    flat_ref, triple_ref, mixed_ref, stat_ref, attended_ref, score_ref,
):
    width, tokens = gain_ref.shape
    head = width // HEADS
    factor = head ** (-0.5) * LOG2E
    flat = load_rows(act_ref).T
    flat_ref[0] = flat.astype(BF)
    normed, _ = normalize(flat)
    scaled = (normed * gain_ref[...]).astype(BF)
    triple_ref[0] = nn(joint_ref[...], scaled).astype(BF)

    def score(h):
        queries = triple_ref[0, h * head : (h + 1) * head]
        keys = triple_ref[0, width + h * head : width + (h + 1) * head]
        score_ref[h % 2] = tn(keys, queries)

    score(0)
    for h in range(HEADS):
        if h + 1 < HEADS:
            score(h + 1)
        values = triple_ref[0, 2 * width + h * head : 2 * width + (h + 1) * head]
        for lanes in lane_halves(tokens):
            scores = score_ref[h % 2, :, lanes]
            top = jnp.max(scores, axis=0, keepdims=True)
            weights = jnp.exp2((scores - top) * factor)
            total = jnp.sum(weights, axis=0, keepdims=True)
            stat_ref[0, h : h + 1, lanes] = top * factor + jnp.log2(total)
            weights = (weights * (1.0 / total)).astype(BF)
            mixed_ref[0, h * head : (h + 1) * head, lanes] = nn(values, weights).astype(BF)
    attended_ref[0] = flat_ref[0].astype(F32) + nn(out_t_ref[...], mixed_ref[0])


def mlp_kernel(
    attended_ref, mixed_ref, cot_ref, gain_ref, up_t_ref, down_t_ref, down_ref, up_ref, out_w_ref,
    *rest,
):
    carried = rest[:-13]
    result_ref, grad_att_ref, grad_mixed_ref, grads_ref, grad_gain_ref, acc_ref = rest[-13:-7]
    scaled_ref, cot_b_ref, cot_tb_ref, pre_ref, grad_hidden_ref, hidden_ref, grad_pre_ref = rest[-7:]
    step = pl.program_id(0)
    hidden_dim = up_ref.shape[1]

    @pl.when(step == 0)
    def _():
        begin(carried, acc_ref, grad_gain_ref)

    cot_rows = load_rows(cot_ref)
    cot_b = cot_rows.astype(BF)
    cot_t = cot_rows.T
    cot_tb = cot_t.astype(BF)
    mixed = mixed_ref[0]
    attended = attended_ref[0]
    normed, inv_std = normalize(attended)
    gain = gain_ref[...]
    scaled = (normed * gain).astype(BF)
    scaled_ref[...] = scaled
    cot_b_ref[...] = cot_b
    cot_tb_ref[...] = cot_tb

    def products(n):
        part = slice(n * PIECE, (n + 1) * PIECE)
        pre_ref[n % 2] = nn(up_t_ref[part], scaled_ref[...])
        grad_hidden_ref[n % 2] = nn(down_ref[part], cot_tb_ref[...]).astype(BF)

    def activate(n):
        for start in range(0, PIECE, 32):
            some = slice(start, start + 32)
            here = slice(n * PIECE + start, n * PIECE + start + 32)
            pre = pre_ref[n % 2, some]
            phi, gauss = gelu_parts(pre)
            hidden_ref[here] = (pre * phi).astype(BF)
            slope = phi + pre * gauss * INV_ROOT_TAU
            grad_pre_ref[here] = (grad_hidden_ref[n % 2, some].astype(F32) * slope).astype(BF)

    def gather(n):
        part = slice(n * PIECE, (n + 1) * PIECE)
        acc_ref[part] += nn(hidden_ref[part], cot_b_ref[...])
        there = slice(hidden_dim + n * PIECE, hidden_dim + (n + 1) * PIECE)
        acc_ref[there] += nt(grad_pre_ref[part], scaled_ref[...])

    pieces = hidden_dim // PIECE
    products(0)
    for n in range(pieces):
        if n + 1 < pieces:
            products(n + 1)
        activate(n)
        if n:
            gather(n - 1)
    gather(pieces - 1)
    grad_scaled = nn(up_ref[...], grad_pre_ref[...])
    result = attended + nn(down_t_ref[...], hidden_ref[...])
    store_rows(result_ref, result.T)
    grad_gain_ref[...] += fold_lanes(grad_scaled * normed)
    grad_att = cot_t + norm_back(grad_scaled * gain, normed, inv_std)
    grad_att_ref[0] = grad_att
    grad_att_b = grad_att.astype(BF)
    acc_ref[2 * hidden_dim :] += nt(mixed, grad_att_b)
    grad_mixed_ref[0] = nn(out_w_ref[...], grad_att_b).astype(BF)

    @pl.when(step == pl.num_programs(0) - 1)
    def _():
        finish(acc_ref, grads_ref, grad_gain_ref)


def back_kernel(
    flat_ref, triple_ref, stat_ref, grad_mixed_ref, grad_att_ref, gain_ref, joint_ref,
    *rest,
):
    carried = rest[:-9]
    grad_in_ref, grads_ref, grad_gain_ref, acc_ref, grad_triple_ref = rest[-9:-4]
    score_ref, slope_ref, grad_score_ref, weight_ref = rest[-4:]
    step = pl.program_id(0)
    width = gain_ref.shape[0]
    head = width // HEADS
    scale = head ** (-0.5)

    @pl.when(step == 0)
    def _():
        begin(carried, acc_ref, grad_gain_ref)

    tokens = gain_ref.shape[1]

    def rows(part, h):
        return slice(part * width + h * head, part * width + (h + 1) * head)

    def products(h):
        score_ref[h % 2] = tn(triple_ref[0, rows(1, h)], triple_ref[0, rows(0, h)])
        slope_ref[h % 2] = tn(triple_ref[0, rows(2, h)], grad_mixed_ref[0, rows(0, h)])

    def weigh(h):
        for lanes in lane_halves(tokens):
            weights = jnp.exp2(score_ref[h % 2, :, lanes] * (scale * LOG2E) - stat_ref[0, h : h + 1, lanes])
            grad_weights = slope_ref[h % 2, :, lanes]
            inner = jnp.sum(weights * grad_weights, axis=0, keepdims=True)
            grad_score_ref[h % 2, :, lanes] = (weights * (grad_weights - inner) * scale).astype(BF)
            weight_ref[h % 2, :, lanes] = weights.astype(BF)

    def back(h):
        grad_scores = grad_score_ref[h % 2]
        grad_triple_ref[rows(0, h)] = nn(triple_ref[0, rows(1, h)], grad_scores).astype(BF)
        grad_triple_ref[rows(1, h)] = nt(triple_ref[0, rows(0, h)], grad_scores).astype(BF)
        grad_triple_ref[rows(2, h)] = nt(grad_mixed_ref[0, rows(0, h)], weight_ref[h % 2]).astype(BF)

    products(0)
    for h in range(HEADS):
        if h + 1 < HEADS:
            products(h + 1)
        weigh(h)
        if h:
            back(h - 1)
    back(HEADS - 1)
    normed, inv_std = normalize(flat_ref[0].astype(F32))
    gain = gain_ref[...]
    scaled = (normed * gain).astype(BF)
    acc_ref[...] += nt(grad_triple_ref[...], scaled)
    grad_scaled = nn(joint_ref[...], grad_triple_ref[...])
    grad_gain_ref[...] += fold_lanes(grad_scaled * normed)
    grad_in = grad_att_ref[0] + norm_back(grad_scaled * gain, normed, inv_std)
    store_rows(grad_in_ref, grad_in.T)

    @pl.when(step == pl.num_programs(0) - 1)
    def _():
        finish(acc_ref, grads_ref, grad_gain_ref)


def prepare_kernel(
    gain_one_ref, gain_two_ref, joint_ref, out_w_ref, up_ref, down_ref,
    wide_one_ref, wide_two_ref, joint_t_ref, out_t_ref, up_t_ref, down_t_ref,
):
    tokens = wide_one_ref.shape[1]
    for gain_ref, wide_ref in ((gain_one_ref, wide_one_ref), (gain_two_ref, wide_two_ref)):
        wide_ref[...] = jnp.broadcast_to(gain_ref[...], (tokens, gain_ref.shape[1])).T
    for weight_ref, turned_ref in (
        (joint_ref, joint_t_ref),
        (out_w_ref, out_t_ref),
        (up_ref, up_t_ref),
        (down_ref, down_t_ref),
    ):
        turned_ref[...] = weight_ref[...].T


def prepare_call(gain_one, gain_two, joint, out_w, up, down, tokens):
    width = gain_one.shape[0]
    turned = [jax.ShapeDtypeStruct(w.shape[::-1], w.dtype) for w in (joint, out_w, up, down)]
    wide = jax.ShapeDtypeStruct((width, tokens), F32)
    return pl.pallas_call(
        prepare_kernel,
        out_shape=[wide, wide] + turned,
        compiler_params=pltpu.CompilerParams(vmem_limit_bytes=60 << 20),
        cost_estimate=cost(1e6, 16e6, 0),
    )(gain_one.reshape(1, width), gain_two.reshape(1, width), joint, out_w, up, down)


def pack_kernel(tile_ref, sends_ref, rows_ref):
    lines, _, chunk_rows, columns, width = tile_ref.shape
    cols, groups, share, _ = sends_ref.shape
    for line in range(lines):
        for row in range(chunk_rows):
            for block in range(columns // cols):
                near, part = block // (columns // cols // (share // lines)), block % (groups // chunk_rows)
                start = (row * (groups // chunk_rows) + part) * share + line * (share // lines) + near
                values = tile_ref[line, 0, row, block * cols : (block + 1) * cols].astype(F32)
                for lane in range(width // 128):
                    rows_ref[lane, pl.ds(start, cols, stride=groups * share)] = values[
                        :, lane * 128 : (lane + 1) * 128
                    ]
    for lane in range(width // 128):
        sends_ref[:, :, :, lane * 128 : (lane + 1) * 128] = (
            rows_ref[lane].reshape(cols, groups, share, 128).astype(BF)
        )


def unpack_kernel(*refs):
    *arrived, tile_ref, rows_ref = refs
    lines, _, all_rows, columns, width = tile_ref.shape
    cols, groups, share, _ = arrived[0].shape
    chunk_rows = all_rows // len(arrived)
    parts = groups // chunk_rows
    for chunk, part_ref in enumerate(arrived):
        for lane in range(width // 128):
            piece = part_ref[:, :, :, lane * 128 : (lane + 1) * 128].astype(F32)
            rows_ref[lane] = piece.reshape(cols * groups * share, 128)
        for line in range(lines):
            for row in range(chunk_rows):
                for block in range(columns // cols):
                    near, part = block // parts, block % parts
                    start = (row * parts + part) * share + line * (share // lines) + near
                    values = jnp.concatenate(
                        [
                            rows_ref[lane, pl.ds(start, cols, stride=groups * share)]
                            for lane in range(width // 128)
                        ],
                        axis=1,
                    )
                    tile_ref[line, 0, chunk * chunk_rows + row, block * cols : (block + 1) * cols] = (
                        values.astype(BF)
                    )


def pack_call(tile, chunk, chunk_rows, row_devs, cols, parts):
    lines, _, _, columns, width = tile.shape
    groups, share = chunk_rows * parts, lines * columns // (cols * parts)
    return pl.pallas_call(
        pack_kernel,
        grid=(row_devs,),
        in_specs=[
            pl.BlockSpec((lines, 1, chunk_rows, columns, width), lambda r: (0, r, chunk, 0, 0))
        ],
        out_specs=pl.BlockSpec((cols, groups, share, width), lambda r: (r, 0, 0, 0)),
        out_shape=jax.ShapeDtypeStruct((row_devs * cols, groups, share, width), BF),
        scratch_shapes=[pltpu.VMEM((width // 128, cols * groups * share, 128), F32)],
        compiler_params=params(),
        cost_estimate=cost(1e6, 4 * row_devs * cols * groups * share * width, 0),
    )(tile)


def unpack_call(arrived, lines, all_rows, columns, row_devs):
    devices, groups, share, width = arrived[0].shape
    cols = devices // row_devs
    piece = pl.BlockSpec((cols, groups, share, width), lambda r: (r, 0, 0, 0))
    return pl.pallas_call(
        unpack_kernel,
        grid=(row_devs,),
        in_specs=[piece] * len(arrived),
        out_specs=pl.BlockSpec((lines, 1, all_rows, columns, width), lambda r: (0, r, 0, 0, 0)),
        out_shape=jax.ShapeDtypeStruct((lines, row_devs, all_rows, columns, width), BF),
        scratch_shapes=[pltpu.VMEM((width // 128, cols * groups * share, 128), F32)],
        compiler_params=params(),
        cost_estimate=cost(1e6, 4 * lines * row_devs * all_rows * columns * width, 0),
    )(*arrived)


def whole(array):
    return pl.BlockSpec(array.shape, lambda g: (0,) * array.ndim)


def per_group(shape):
    return pl.BlockSpec((1,) + shape, lambda g: (g, 0, 0))


def pieces_spec(array):
    pieces, _, sub, width = array.shape
    return pl.BlockSpec((pieces, 1, sub, width), lambda g: (0, g, 0, 0))


def params():
    return pltpu.CompilerParams(dimension_semantics=("arbitrary",), vmem_limit_bytes=60 << 20)


def cost(flops, bytes_moved, exps):
    return pl.CostEstimate(flops=int(flops), bytes_accessed=int(bytes_moved), transcendentals=int(exps))


def attend_call(act, gain, joint_t, out_t):
    pieces, groups, sub, width = act.shape
    tokens = pieces * sub
    return pl.pallas_call(
        attend_kernel,
        grid=(groups,),
        in_specs=[pieces_spec(act), whole(gain), whole(joint_t), whole(out_t)],
        out_specs=[
            per_group((width, tokens)),
            per_group((3 * width, tokens)),
            per_group((width, tokens)),
            per_group((16, tokens)),
            per_group((width, tokens)),
        ],
        out_shape=[
            jax.ShapeDtypeStruct((groups, width, tokens), BF),
            jax.ShapeDtypeStruct((groups, 3 * width, tokens), BF),
            jax.ShapeDtypeStruct((groups, width, tokens), BF),
            jax.ShapeDtypeStruct((groups, 16, tokens), F32),
            jax.ShapeDtypeStruct((groups, width, tokens), F32),
        ],
        scratch_shapes=[pltpu.VMEM((2, tokens, tokens), F32)],
        compiler_params=params(),
        cost_estimate=cost(3e9 * groups, 12 * groups * tokens * width, 0),
    )(act, gain, joint_t, out_t)


def mlp_call(attended, mixed, cot, gain, weights, carried, spare):
    pieces, groups, sub, width = cot.shape
    tokens = pieces * sub
    hidden_dim = weights[0].shape[0]
    rows = 2 * hidden_dim + width
    return pl.pallas_call(
        mlp_kernel,
        grid=(groups,),
        in_specs=[per_group((width, tokens)), per_group((width, tokens)), pieces_spec(cot), whole(gain)]
        + [whole(w) for w in weights + carried],
        out_specs=[
            pieces_spec(cot),
            per_group((width, tokens)),
            per_group((width, tokens)),
            pl.BlockSpec((rows + spare, width), lambda g: (0, 0)),
            pl.BlockSpec((width, 128), lambda g: (0, 0)),
        ],
        out_shape=[
            jax.ShapeDtypeStruct(cot.shape, BF),
            jax.ShapeDtypeStruct((groups, width, tokens), F32),
            jax.ShapeDtypeStruct((groups, width, tokens), BF),
            jax.ShapeDtypeStruct((rows + spare, width), BF if spare else F32),
            jax.ShapeDtypeStruct((width, 128), F32),
        ],
        scratch_shapes=[
            pltpu.VMEM((rows, width), F32),
            pltpu.VMEM((width, tokens), BF),
            pltpu.VMEM((tokens, width), BF),
            pltpu.VMEM((width, tokens), BF),
            pltpu.VMEM((2, PIECE, tokens), F32),
            pltpu.VMEM((2, PIECE, tokens), BF),
            pltpu.VMEM((hidden_dim, tokens), BF),
            pltpu.VMEM((hidden_dim, tokens), BF),
        ],
        compiler_params=params(),
        cost_estimate=cost(4e9 * groups, 14 * groups * tokens * width, 0),
    )(attended, mixed, cot, gain, *weights, *carried)


def back_call(flat, triple, stat, grad_mixed, grad_att, gain, joint, like, carried, spare):
    rows = joint.shape[1]
    pieces, groups, sub, width = like.shape
    tokens = pieces * sub
    return pl.pallas_call(
        back_kernel,
        grid=(groups,),
        in_specs=[
            per_group((width, tokens)),
            per_group((3 * width, tokens)),
            per_group((16, tokens)),
            per_group((width, tokens)),
            per_group((width, tokens)),
            whole(gain),
            whole(joint),
        ]
        + [whole(w) for w in carried],
        out_specs=[
            pieces_spec(like),
            pl.BlockSpec((rows + spare, width), lambda g: (0, 0)),
            pl.BlockSpec((width, 128), lambda g: (0, 0)),
        ],
        out_shape=[
            jax.ShapeDtypeStruct(like.shape, BF),
            jax.ShapeDtypeStruct((rows + spare, width), BF if spare else F32),
            jax.ShapeDtypeStruct((width, 128), F32),
        ],
        scratch_shapes=[
            pltpu.VMEM((3 * width, width), F32),
            pltpu.VMEM((3 * width, tokens), BF),
            pltpu.VMEM((2, tokens, tokens), F32),
            pltpu.VMEM((2, tokens, tokens), F32),
            pltpu.VMEM((2, tokens, tokens), BF),
            pltpu.VMEM((2, tokens, tokens), BF),
        ],
        compiler_params=params(),
        cost_estimate=cost(6e9 * groups, 18 * groups * tokens * width, 0),
    )(flat, triple, stat, grad_mixed, grad_att, gain, joint, *carried)


def tie(value, *after):
    return lax.optimization_barrier((value,) + after)[0]


def peers(axis, low, high):
    return lax.axis_index(axis) // (1 << low) % (1 << (high - low)), 1 << (high - low)


def swap(values, axis, offset):
    return lax.ppermute(values, axis, [(i, i ^ offset) for i in range(lax.axis_size(axis))])


def scatter_sum(values, axis, low, high):
    mine, count = peers(axis, low, high)
    parts = values.reshape((count, values.shape[0] // count) + values.shape[1:])
    total = lax.dynamic_index_in_dim(parts, mine, 0, keepdims=False).astype(F32)
    for other in range(1, count):
        part = lax.dynamic_index_in_dim(parts, mine ^ other, 0, keepdims=False)
        total = total + swap(part, axis, other << low).astype(F32)
    return total.astype(BF)


def share_sum(values, axis, low, high):
    _, count = peers(axis, low, high)
    total = values.astype(F32)
    for other in range(1, count):
        total = total + swap(values, axis, other << low).astype(F32)
    return total.astype(BF)


def collect(values, axis, low, high):
    mine, count = peers(axis, low, high)
    got = jnp.stack([values] + [swap(values, axis, other << low) for other in range(1, count)])
    return jnp.concatenate(
        [lax.dynamic_index_in_dim(got, slot ^ mine, 0, keepdims=False) for slot in range(count)]
    )


def stages():
    row_bits = lax.axis_size("row").bit_length() - 1
    col_bits = lax.axis_size("col").bit_length() - 1
    return (("col", 0, 1), ("col", 1, col_bits), ("row", 0, row_bits))


def shards(
    activations,
    cotangent,
    first_gain,
    joint_weight,
    output_weight,
    second_gain,
    expand_weight,
    reduce_weight,
):
    row_devs = lax.axis_size("row")
    col_devs = lax.axis_size("col")
    devices = row_devs * col_devs
    both = ("row", "col")
    tile_rows, tile_cols, channels = activations.shape
    local_rows = GRID // row_devs
    local_cols = GRID // col_devs
    stride_rows = tile_rows // local_rows
    stride_cols = tile_cols // local_cols
    part_rows = stride_rows // row_devs
    part_cols = stride_cols // col_devs
    share = local_rows * local_cols
    tokens = GRID * GRID
    factor = float(tile_rows * tile_cols * devices) ** (-0.5)

    chunks = 2
    chunk_rows = part_rows // chunks
    chunk_groups = chunk_rows * part_cols

    kernels_pack = share % SUB == 0 and col_devs == SUB

    def pack(tile, chunk):
        if kernels_pack:
            tile = tile.reshape(local_rows, row_devs, part_rows, tile_cols, channels)
            return pack_call(tile, chunk, chunk_rows, row_devs, col_devs, part_cols)
        sends = tile.reshape(
            local_rows, row_devs, part_rows, local_cols, part_cols, col_devs, channels
        )[:, :, chunk * chunk_rows : (chunk + 1) * chunk_rows]
        return sends.transpose(1, 5, 2, 4, 0, 3, 6).reshape(devices, chunk_groups, share, channels)

    def send(sends, *after):
        got = lax.all_to_all(tie(sends, *after), both, split_axis=0, concat_axis=0, tiled=True)
        if share % SUB:
            got = got.transpose(0, 2, 1, 3).reshape(tokens // SUB, SUB, chunk_groups, channels)
            got = got.transpose(0, 2, 1, 3)
        return got.reshape(tokens // SUB, chunk_groups, SUB, channels)

    def give_back(pieces, *after):
        if share % SUB:
            pieces = pieces.transpose(0, 2, 1, 3).reshape(devices, share, chunk_groups, channels)
            pieces = pieces.transpose(0, 2, 1, 3)
        pieces = tie(pieces.reshape(devices, chunk_groups, share, channels), *after)
        return lax.all_to_all(pieces, both, split_axis=0, concat_axis=0, tiled=True)

    def to_tile(arrived):
        if kernels_pack:
            tile = unpack_call(arrived, local_rows, part_rows, tile_cols, row_devs)
            return tile.reshape(tile_rows, tile_cols, channels)
        arrived = [
            part.reshape(row_devs, col_devs, chunk_rows, part_cols, local_rows, local_cols, channels)
            for part in arrived
        ]
        return jnp.concatenate(arrived, axis=2).transpose(4, 0, 2, 5, 3, 1, 6).reshape(
            tile_rows, tile_cols, channels
        )

    arrived = []
    for k, tile in enumerate([activations] * chunks + [cotangent] * chunks):
        sends = pack(tile, k % chunks)
        arrived.append(send(sends, *arrived[-1:]))
    act, cot = arrived[:chunks], arrived[chunks:]
    gain_one, gain_two, joint_t, out_t, up_t, down_t = prepare_call(
        first_gain, second_gain, joint_weight, output_weight, expand_weight, reduce_weight, tokens
    )
    weights = (up_t, down_t, reduce_weight, expand_weight, output_weight)
    hidden_dim = expand_weight.shape[1]
    tail_rows, head_rows = 2 * hidden_dim + channels, 3 * channels
    unit = SUB * devices
    fronts = []
    for k in range(chunks):
        fronts.append(attend_call(act[k], gain_one, joint_t, out_t))
    tails, out_parts, carried = [], [], ()
    before = cot[-1:]
    for k in range(chunks):
        _, _, mixed, _, attended = fronts[k]
        spare = unit - tail_rows % unit if k == chunks - 1 else 0
        tails.append(mlp_call(attended, mixed, cot[k], gain_two, weights, carried, spare))
        carried = tails[-1][3:]
        out_parts.append(give_back(tails[-1][0], *before))
        before = out_parts[-1:]
    steps = stages()
    tail_sum = scatter_sum(carried[0], *steps[0])
    heads, in_parts, carried = [], [], ()
    for k in range(chunks):
        flat, triple, _, stat, _ = fronts[k]
        _, grad_att, grad_mixed = tails[k][:3]
        spare = unit - head_rows % unit if k == chunks - 1 else 0
        grad_mixed = tie(grad_mixed, out_parts[k])
        heads.append(
            back_call(flat, triple, stat, grad_mixed, grad_att, gain_one, joint_weight, cot[k], carried, spare)
        )
        carried = heads[-1][1:]
        in_parts.append(give_back(heads[-1][0], *before))
        before = in_parts[-1:]
        tail_sum = scatter_sum(tail_sum, *steps[k + 1])
    head_sum = carried[0]
    near, cols, rows = steps
    head_sum = scatter_sum(head_sum, *near)
    head_sum = scatter_sum(head_sum, *cols)
    tail_sum = collect(tail_sum, *rows)
    head_sum = share_sum(head_sum, *rows)
    tail_sum = collect(tail_sum, *cols)
    head_sum = collect(head_sum, *cols)
    tail_sum = collect(tail_sum, *near)
    head_sum = collect(head_sum, *near)
    head_sum = head_sum.astype(F32) * factor
    tail_sum = tail_sum.astype(F32) * factor
    block_out = to_tile(out_parts)
    grad_input = to_tile(in_parts)
    return (
        block_out,
        grad_input,
        head_sum[:head_rows].T,
        tail_sum[2 * hidden_dim : tail_rows],
        tail_sum[hidden_dim : 2 * hidden_dim].T,
        tail_sum[:hidden_dim],
        head_sum[head_rows],
        tail_sum[tail_rows],
    )


def solution(mesh):
    placed = (P("row", "col", None), P("row", "col", None), P(), P(), P(), P(), P(), P())
    return jax.shard_map(shards, mesh=mesh, in_specs=placed, out_specs=placed, check_vma=False)
```

```python
import jax
import jax.numpy as jnp
from jax import lax
from jax.experimental import pallas as pl
from jax.experimental.pallas import tpu as pltpu
from jax.sharding import PartitionSpec as P


HEADS = 12
GRID = 16
SUB = 8
PIECE = 512
EPSILON = 1e-05
INV_ROOT_TAU = 0.3989422804014327
SQRT_HALF = 0.7071067811865476
LOG2E = 1.4426950408889634
BF = jnp.bfloat16
F32 = jnp.float32

ERFC_P = 0.4
ERFC_C = (
    0.2256758624069583,
    0.22566957331484927,
    0.20784305752189558,
    0.16853970978283367,
    0.1414388899580775,
    -0.005621196233437842,
    0.16909944767289115,
    -0.18290897174728507,
    0.05026375199644912,
)


def nn(a, b):
    return lax.dot_general(a, b, (((1,), (0,)), ((), ())), preferred_element_type=F32)


def nt(a, b):
    return lax.dot_general(a, b, (((1,), (1,)), ((), ())), preferred_element_type=F32)


def tn(a, b):
    return lax.dot_general(a, b, (((0,), (0,)), ((), ())), preferred_element_type=F32)


def gelu_parts(pre):
    gauss = jnp.exp2(pre * pre * (-0.5 * LOG2E))
    t = 1.0 / (1.0 + (ERFC_P * SQRT_HALF) * jnp.abs(pre))
    poly = jnp.full_like(t, 0.5 * ERFC_C[-1])
    for coef in ERFC_C[-2::-1]:
        poly = poly * t + 0.5 * coef
    half_erfc = gauss * (t * poly)
    phi = jnp.where(pre < 0.0, half_erfc, 1.0 - half_erfc)
    return phi, gauss


def normalize(values):
    center = values - jnp.mean(values, axis=0, keepdims=True)
    inv_std = lax.rsqrt(jnp.mean(center * center, axis=0, keepdims=True) + EPSILON)
    return center * inv_std, inv_std


def norm_back(scaled, normed, inv_std):
    return inv_std * (
        scaled
        - jnp.mean(scaled, axis=0, keepdims=True)
        - normed * jnp.mean(scaled * normed, axis=0, keepdims=True)
    )


def load_rows(ref):
    pieces, _, sub, width = ref.shape
    return ref[...].reshape(pieces, sub, width).astype(F32).reshape(pieces * sub, width)


def store_rows(ref, rows):
    pieces, _, sub, width = ref.shape
    ref[...] = rows.reshape(pieces, 1, sub, width).astype(ref.dtype)


def fold_lanes(values):
    total = values[:, :128]
    for start in range(128, values.shape[1], 128):
        total = total + values[:, start : start + 128]
    return total


def by_rows(rows, body):
    def step(n, _):
        body(pl.ds(pl.multiple_of(n * 128, 128), 128))
        return 0

    lax.fori_loop(0, rows // 128, step, 0)


def begin(carried, acc_ref, grad_gain_ref):
    def fill(part):
        if carried:
            acc_ref[part] = carried[0][part]
        else:
            acc_ref[part] = jnp.zeros((128, acc_ref.shape[1]), F32)

    by_rows(acc_ref.shape[0], fill)
    if carried:
        grad_gain_ref[...] = carried[1][...]
    else:
        grad_gain_ref[...] = jnp.zeros_like(grad_gain_ref)


def finish(acc_ref, grads_ref, grad_gain_ref):
    rows = acc_ref.shape[0]

    def cast(part):
        grads_ref[part] = acc_ref[part].astype(grads_ref.dtype)

    by_rows(rows, cast)
    if grads_ref.shape[0] > rows:
        gains = jnp.sum(grad_gain_ref[...].T, axis=0, keepdims=True)
        spare = grads_ref.shape[0] - rows
        first = lax.broadcasted_iota(jnp.int32, (spare, gains.shape[1]), 0) == 0
        grads_ref[rows:] = jnp.where(first, gains, 0.0).astype(grads_ref.dtype)


def lane_halves(count):
    return [slice(start, start + 128) for start in range(0, count, 128)]


def attend_kernel(
    act_ref, gain_ref, joint_ref, out_t_ref,
    flat_ref, triple_ref, mixed_ref, stat_ref, attended_ref, score_ref,
):
    width, tokens = gain_ref.shape
    head = width // HEADS
    factor = head ** (-0.5) * LOG2E
    flat = load_rows(act_ref).T
    flat_ref[0] = flat.astype(BF)
    normed, _ = normalize(flat)
    scaled = (normed * gain_ref[...]).astype(BF)
    triple_ref[0] = nn(joint_ref[...], scaled).astype(BF)

    def score(h):
        queries = triple_ref[0, h * head : (h + 1) * head]
        keys = triple_ref[0, width + h * head : width + (h + 1) * head]
        score_ref[h % 2] = tn(keys, queries)

    score(0)
    for h in range(HEADS):
        if h + 1 < HEADS:
            score(h + 1)
        values = triple_ref[0, 2 * width + h * head : 2 * width + (h + 1) * head]
        for lanes in lane_halves(tokens):
            scores = score_ref[h % 2, :, lanes]
            top = jnp.max(scores, axis=0, keepdims=True)
            weights = jnp.exp2((scores - top) * factor)
            total = jnp.sum(weights, axis=0, keepdims=True)
            stat_ref[0, h : h + 1, lanes] = top * factor + jnp.log2(total)
            weights = (weights * (1.0 / total)).astype(BF)
            mixed_ref[0, h * head : (h + 1) * head, lanes] = nn(values, weights).astype(BF)
    attended_ref[0] = flat_ref[0].astype(F32) + nn(out_t_ref[...], mixed_ref[0])


def mlp_kernel(
    attended_ref, mixed_ref, cot_ref, gain_ref, up_t_ref, down_t_ref, down_ref, up_ref, out_w_ref,
    *rest,
):
    carried = rest[:-13]
    result_ref, grad_att_ref, grad_mixed_ref, grads_ref, grad_gain_ref, acc_ref = rest[-13:-7]
    scaled_ref, cot_b_ref, cot_tb_ref, pre_ref, grad_hidden_ref, hidden_ref, grad_pre_ref = rest[-7:]
    step = pl.program_id(0)
    hidden_dim = up_ref.shape[1]

    @pl.when(step == 0)
    def _():
        begin(carried, acc_ref, grad_gain_ref)

    cot_rows = load_rows(cot_ref)
    cot_b = cot_rows.astype(BF)
    cot_t = cot_rows.T
    cot_tb = cot_t.astype(BF)
    mixed = mixed_ref[0]
    attended = attended_ref[0]
    normed, inv_std = normalize(attended)
    gain = gain_ref[...]
    scaled = (normed * gain).astype(BF)
    scaled_ref[...] = scaled
    cot_b_ref[...] = cot_b
    cot_tb_ref[...] = cot_tb

    def products(n):
        part = slice(n * PIECE, (n + 1) * PIECE)
        pre_ref[n % 2] = nn(up_t_ref[part], scaled_ref[...])
        grad_hidden_ref[n % 2] = nn(down_ref[part], cot_tb_ref[...]).astype(BF)

    def activate(n):
        for start in range(0, PIECE, 32):
            some = slice(start, start + 32)
            here = slice(n * PIECE + start, n * PIECE + start + 32)
            pre = pre_ref[n % 2, some]
            phi, gauss = gelu_parts(pre)
            hidden_ref[here] = (pre * phi).astype(BF)
            slope = phi + pre * gauss * INV_ROOT_TAU
            grad_pre_ref[here] = (grad_hidden_ref[n % 2, some].astype(F32) * slope).astype(BF)

    def gather(n):
        part = slice(n * PIECE, (n + 1) * PIECE)
        acc_ref[part] += nn(hidden_ref[part], cot_b_ref[...])
        there = slice(hidden_dim + n * PIECE, hidden_dim + (n + 1) * PIECE)
        acc_ref[there] += nt(grad_pre_ref[part], scaled_ref[...])

    pieces = hidden_dim // PIECE
    products(0)
    for n in range(pieces):
        if n + 1 < pieces:
            products(n + 1)
        activate(n)
        if n:
            gather(n - 1)
    gather(pieces - 1)
    grad_scaled = nn(up_ref[...], grad_pre_ref[...])
    result = attended + nn(down_t_ref[...], hidden_ref[...])
    store_rows(result_ref, result.T)
    grad_gain_ref[...] += fold_lanes(grad_scaled * normed)
    grad_att = cot_t + norm_back(grad_scaled * gain, normed, inv_std)
    grad_att_ref[0] = grad_att
    grad_att_b = grad_att.astype(BF)
    acc_ref[2 * hidden_dim :] += nt(mixed, grad_att_b)
    grad_mixed_ref[0] = nn(out_w_ref[...], grad_att_b).astype(BF)

    @pl.when(step == pl.num_programs(0) - 1)
    def _():
        finish(acc_ref, grads_ref, grad_gain_ref)


def back_kernel(
    flat_ref, triple_ref, stat_ref, grad_mixed_ref, grad_att_ref, gain_ref, joint_ref,
    *rest,
):
    carried = rest[:-9]
    grad_in_ref, grads_ref, grad_gain_ref, acc_ref, grad_triple_ref = rest[-9:-4]
    score_ref, slope_ref, grad_score_ref, weight_ref = rest[-4:]
    step = pl.program_id(0)
    width = gain_ref.shape[0]
    head = width // HEADS
    scale = head ** (-0.5)

    @pl.when(step == 0)
    def _():
        begin(carried, acc_ref, grad_gain_ref)

    tokens = gain_ref.shape[1]

    def rows(part, h):
        return slice(part * width + h * head, part * width + (h + 1) * head)

    def products(h):
        score_ref[h % 2] = tn(triple_ref[0, rows(1, h)], triple_ref[0, rows(0, h)])
        slope_ref[h % 2] = tn(triple_ref[0, rows(2, h)], grad_mixed_ref[0, rows(0, h)])

    def weigh(h):
        for lanes in lane_halves(tokens):
            weights = jnp.exp2(score_ref[h % 2, :, lanes] * (scale * LOG2E) - stat_ref[0, h : h + 1, lanes])
            grad_weights = slope_ref[h % 2, :, lanes]
            inner = jnp.sum(weights * grad_weights, axis=0, keepdims=True)
            grad_score_ref[h % 2, :, lanes] = (weights * (grad_weights - inner) * scale).astype(BF)
            weight_ref[h % 2, :, lanes] = weights.astype(BF)

    def back(h):
        grad_scores = grad_score_ref[h % 2]
        grad_triple_ref[rows(0, h)] = nn(triple_ref[0, rows(1, h)], grad_scores).astype(BF)
        grad_triple_ref[rows(1, h)] = nt(triple_ref[0, rows(0, h)], grad_scores).astype(BF)
        grad_triple_ref[rows(2, h)] = nt(grad_mixed_ref[0, rows(0, h)], weight_ref[h % 2]).astype(BF)

    products(0)
    for h in range(HEADS):
        if h + 1 < HEADS:
            products(h + 1)
        weigh(h)
        if h:
            back(h - 1)
    back(HEADS - 1)
    normed, inv_std = normalize(flat_ref[0].astype(F32))
    gain = gain_ref[...]
    scaled = (normed * gain).astype(BF)
    acc_ref[...] += nt(grad_triple_ref[...], scaled)
    grad_scaled = nn(joint_ref[...], grad_triple_ref[...])
    grad_gain_ref[...] += fold_lanes(grad_scaled * normed)
    grad_in = grad_att_ref[0] + norm_back(grad_scaled * gain, normed, inv_std)
    store_rows(grad_in_ref, grad_in.T)

    @pl.when(step == pl.num_programs(0) - 1)
    def _():
        finish(acc_ref, grads_ref, grad_gain_ref)


def prepare_kernel(
    gain_one_ref, gain_two_ref, joint_ref, out_w_ref, up_ref, down_ref,
    wide_one_ref, wide_two_ref, joint_t_ref, out_t_ref, up_t_ref, down_t_ref,
):
    tokens = wide_one_ref.shape[1]
    for gain_ref, wide_ref in ((gain_one_ref, wide_one_ref), (gain_two_ref, wide_two_ref)):
        wide_ref[...] = jnp.broadcast_to(gain_ref[...], (tokens, gain_ref.shape[1])).T
    for weight_ref, turned_ref in (
        (joint_ref, joint_t_ref),
        (out_w_ref, out_t_ref),
        (up_ref, up_t_ref),
        (down_ref, down_t_ref),
    ):
        turned_ref[...] = weight_ref[...].T


def prepare_call(gain_one, gain_two, joint, out_w, up, down, tokens):
    width = gain_one.shape[0]
    turned = [jax.ShapeDtypeStruct(w.shape[::-1], w.dtype) for w in (joint, out_w, up, down)]
    wide = jax.ShapeDtypeStruct((width, tokens), F32)
    return pl.pallas_call(
        prepare_kernel,
        out_shape=[wide, wide] + turned,
        compiler_params=pltpu.CompilerParams(vmem_limit_bytes=60 << 20),
        cost_estimate=cost(1e6, 16e6, 0),
    )(gain_one.reshape(1, width), gain_two.reshape(1, width), joint, out_w, up, down)


def pack_kernel(tile_ref, sends_ref, rows_ref):
    lines, _, chunk_rows, columns, width = tile_ref.shape
    cols, groups, share, _ = sends_ref.shape
    for line in range(lines):
        for row in range(chunk_rows):
            for block in range(columns // cols):
                near, part = block // (columns // cols // (share // lines)), block % (groups // chunk_rows)
                start = (row * (groups // chunk_rows) + part) * share + line * (share // lines) + near
                values = tile_ref[line, 0, row, block * cols : (block + 1) * cols].astype(F32)
                for lane in range(width // 128):
                    rows_ref[lane, pl.ds(start, cols, stride=groups * share)] = values[
                        :, lane * 128 : (lane + 1) * 128
                    ]
    for lane in range(width // 128):
        sends_ref[:, :, :, lane * 128 : (lane + 1) * 128] = (
            rows_ref[lane].reshape(cols, groups, share, 128).astype(BF)
        )


def unpack_kernel(*refs):
    *arrived, tile_ref, rows_ref = refs
    lines, _, all_rows, columns, width = tile_ref.shape
    cols, groups, share, _ = arrived[0].shape
    chunk_rows = all_rows // len(arrived)
    parts = groups // chunk_rows
    for chunk, part_ref in enumerate(arrived):
        for lane in range(width // 128):
            piece = part_ref[:, :, :, lane * 128 : (lane + 1) * 128].astype(F32)
            rows_ref[lane] = piece.reshape(cols * groups * share, 128)
        for line in range(lines):
            for row in range(chunk_rows):
                for block in range(columns // cols):
                    near, part = block // parts, block % parts
                    start = (row * parts + part) * share + line * (share // lines) + near
                    values = jnp.concatenate(
                        [
                            rows_ref[lane, pl.ds(start, cols, stride=groups * share)]
                            for lane in range(width // 128)
                        ],
                        axis=1,
                    )
                    tile_ref[line, 0, chunk * chunk_rows + row, block * cols : (block + 1) * cols] = (
                        values.astype(BF)
                    )


def pack_call(tile, chunk, chunk_rows, row_devs, cols, parts):
    lines, _, _, columns, width = tile.shape
    groups, share = chunk_rows * parts, lines * columns // (cols * parts)
    return pl.pallas_call(
        pack_kernel,
        grid=(row_devs,),
        in_specs=[
            pl.BlockSpec((lines, 1, chunk_rows, columns, width), lambda r: (0, r, chunk, 0, 0))
        ],
        out_specs=pl.BlockSpec((cols, groups, share, width), lambda r: (r, 0, 0, 0)),
        out_shape=jax.ShapeDtypeStruct((row_devs * cols, groups, share, width), BF),
        scratch_shapes=[pltpu.VMEM((width // 128, cols * groups * share, 128), F32)],
        compiler_params=params(),
        cost_estimate=cost(1e6, 4 * row_devs * cols * groups * share * width, 0),
    )(tile)


def unpack_call(arrived, lines, all_rows, columns, row_devs):
    devices, groups, share, width = arrived[0].shape
    cols = devices // row_devs
    piece = pl.BlockSpec((cols, groups, share, width), lambda r: (r, 0, 0, 0))
    return pl.pallas_call(
        unpack_kernel,
        grid=(row_devs,),
        in_specs=[piece] * len(arrived),
        out_specs=pl.BlockSpec((lines, 1, all_rows, columns, width), lambda r: (0, r, 0, 0, 0)),
        out_shape=jax.ShapeDtypeStruct((lines, row_devs, all_rows, columns, width), BF),
        scratch_shapes=[pltpu.VMEM((width // 128, cols * groups * share, 128), F32)],
        compiler_params=params(),
        cost_estimate=cost(1e6, 4 * lines * row_devs * all_rows * columns * width, 0),
    )(*arrived)


def whole(array):
    return pl.BlockSpec(array.shape, lambda g: (0,) * array.ndim)


def per_group(shape):
    return pl.BlockSpec((1,) + shape, lambda g: (g, 0, 0))


def pieces_spec(array):
    pieces, _, sub, width = array.shape
    return pl.BlockSpec((pieces, 1, sub, width), lambda g: (0, g, 0, 0))


def params():
    return pltpu.CompilerParams(dimension_semantics=("arbitrary",), vmem_limit_bytes=60 << 20)


def cost(flops, bytes_moved, exps):
    return pl.CostEstimate(flops=int(flops), bytes_accessed=int(bytes_moved), transcendentals=int(exps))


def attend_call(act, gain, joint_t, out_t):
    pieces, groups, sub, width = act.shape
    tokens = pieces * sub
    return pl.pallas_call(
        attend_kernel,
        grid=(groups,),
        in_specs=[pieces_spec(act), whole(gain), whole(joint_t), whole(out_t)],
        out_specs=[
            per_group((width, tokens)),
            per_group((3 * width, tokens)),
            per_group((width, tokens)),
            per_group((16, tokens)),
            per_group((width, tokens)),
        ],
        out_shape=[
            jax.ShapeDtypeStruct((groups, width, tokens), BF),
            jax.ShapeDtypeStruct((groups, 3 * width, tokens), BF),
            jax.ShapeDtypeStruct((groups, width, tokens), BF),
            jax.ShapeDtypeStruct((groups, 16, tokens), F32),
            jax.ShapeDtypeStruct((groups, width, tokens), F32),
        ],
        scratch_shapes=[pltpu.VMEM((2, tokens, tokens), F32)],
        compiler_params=params(),
        cost_estimate=cost(3e9 * groups, 12 * groups * tokens * width, 0),
    )(act, gain, joint_t, out_t)


def mlp_call(attended, mixed, cot, gain, weights, carried, spare):
    pieces, groups, sub, width = cot.shape
    tokens = pieces * sub
    hidden_dim = weights[0].shape[0]
    rows = 2 * hidden_dim + width
    return pl.pallas_call(
        mlp_kernel,
        grid=(groups,),
        in_specs=[per_group((width, tokens)), per_group((width, tokens)), pieces_spec(cot), whole(gain)]
        + [whole(w) for w in weights + carried],
        out_specs=[
            pieces_spec(cot),
            per_group((width, tokens)),
            per_group((width, tokens)),
            pl.BlockSpec((rows + spare, width), lambda g: (0, 0)),
            pl.BlockSpec((width, 128), lambda g: (0, 0)),
        ],
        out_shape=[
            jax.ShapeDtypeStruct(cot.shape, BF),
            jax.ShapeDtypeStruct((groups, width, tokens), F32),
            jax.ShapeDtypeStruct((groups, width, tokens), BF),
            jax.ShapeDtypeStruct((rows + spare, width), BF if spare else F32),
            jax.ShapeDtypeStruct((width, 128), F32),
        ],
        scratch_shapes=[
            pltpu.VMEM((rows, width), F32),
            pltpu.VMEM((width, tokens), BF),
            pltpu.VMEM((tokens, width), BF),
            pltpu.VMEM((width, tokens), BF),
            pltpu.VMEM((2, PIECE, tokens), F32),
            pltpu.VMEM((2, PIECE, tokens), BF),
            pltpu.VMEM((hidden_dim, tokens), BF),
            pltpu.VMEM((hidden_dim, tokens), BF),
        ],
        compiler_params=params(),
        cost_estimate=cost(4e9 * groups, 14 * groups * tokens * width, 0),
    )(attended, mixed, cot, gain, *weights, *carried)


def back_call(flat, triple, stat, grad_mixed, grad_att, gain, joint, like, carried, spare):
    rows = joint.shape[1]
    pieces, groups, sub, width = like.shape
    tokens = pieces * sub
    return pl.pallas_call(
        back_kernel,
        grid=(groups,),
        in_specs=[
            per_group((width, tokens)),
            per_group((3 * width, tokens)),
            per_group((16, tokens)),
            per_group((width, tokens)),
            per_group((width, tokens)),
            whole(gain),
            whole(joint),
        ]
        + [whole(w) for w in carried],
        out_specs=[
            pieces_spec(like),
            pl.BlockSpec((rows + spare, width), lambda g: (0, 0)),
            pl.BlockSpec((width, 128), lambda g: (0, 0)),
        ],
        out_shape=[
            jax.ShapeDtypeStruct(like.shape, BF),
            jax.ShapeDtypeStruct((rows + spare, width), BF if spare else F32),
            jax.ShapeDtypeStruct((width, 128), F32),
        ],
        scratch_shapes=[
            pltpu.VMEM((3 * width, width), F32),
            pltpu.VMEM((3 * width, tokens), BF),
            pltpu.VMEM((2, tokens, tokens), F32),
            pltpu.VMEM((2, tokens, tokens), F32),
            pltpu.VMEM((2, tokens, tokens), BF),
            pltpu.VMEM((2, tokens, tokens), BF),
        ],
        compiler_params=params(),
        cost_estimate=cost(6e9 * groups, 18 * groups * tokens * width, 0),
    )(flat, triple, stat, grad_mixed, grad_att, gain, joint, *carried)


def tie(value, *after):
    return lax.optimization_barrier((value,) + after)[0]


def peers(axis, low, high):
    return lax.axis_index(axis) // (1 << low) % (1 << (high - low)), 1 << (high - low)


def swap(values, axis, offset):
    return lax.ppermute(values, axis, [(i, i ^ offset) for i in range(lax.axis_size(axis))])


def scatter_sum(values, axis, low, high):
    mine, count = peers(axis, low, high)
    parts = values.reshape((count, values.shape[0] // count) + values.shape[1:])
    total = lax.dynamic_index_in_dim(parts, mine, 0, keepdims=False).astype(F32)
    for other in range(1, count):
        part = lax.dynamic_index_in_dim(parts, mine ^ other, 0, keepdims=False)
        total = total + swap(part, axis, other << low).astype(F32)
    return total.astype(BF)


def share_sum(values, axis, low, high):
    _, count = peers(axis, low, high)
    total = values.astype(F32)
    for other in range(1, count):
        total = total + swap(values, axis, other << low).astype(F32)
    return total.astype(BF)


def collect(values, axis, low, high):
    mine, count = peers(axis, low, high)
    got = jnp.stack([values] + [swap(values, axis, other << low) for other in range(1, count)])
    return jnp.concatenate(
        [lax.dynamic_index_in_dim(got, slot ^ mine, 0, keepdims=False) for slot in range(count)]
    )


def stages():
    row_bits = lax.axis_size("row").bit_length() - 1
    col_bits = lax.axis_size("col").bit_length() - 1
    return (("col", 0, 1), ("col", 1, col_bits), ("row", 0, row_bits))


def shards(
    activations,
    cotangent,
    first_gain,
    joint_weight,
    output_weight,
    second_gain,
    expand_weight,
    reduce_weight,
):
    row_devs = lax.axis_size("row")
    col_devs = lax.axis_size("col")
    devices = row_devs * col_devs
    both = ("row", "col")
    tile_rows, tile_cols, channels = activations.shape
    local_rows = GRID // row_devs
    local_cols = GRID // col_devs
    stride_rows = tile_rows // local_rows
    stride_cols = tile_cols // local_cols
    part_rows = stride_rows // row_devs
    part_cols = stride_cols // col_devs
    share = local_rows * local_cols
    tokens = GRID * GRID
    factor = float(tile_rows * tile_cols * devices) ** (-0.5)

    chunks = 2
    chunk_rows = part_rows // chunks
    chunk_groups = chunk_rows * part_cols

    kernels_pack = share % SUB == 0 and col_devs == SUB

    def pack(tile, chunk):
        if kernels_pack:
            tile = tile.reshape(local_rows, row_devs, part_rows, tile_cols, channels)
            return pack_call(tile, chunk, chunk_rows, row_devs, col_devs, part_cols)
        sends = tile.reshape(
            local_rows, row_devs, part_rows, local_cols, part_cols, col_devs, channels
        )[:, :, chunk * chunk_rows : (chunk + 1) * chunk_rows]
        return sends.transpose(1, 5, 2, 4, 0, 3, 6).reshape(devices, chunk_groups, share, channels)

    def send(sends, *after):
        got = lax.all_to_all(tie(sends, *after), both, split_axis=0, concat_axis=0, tiled=True)
        if share % SUB:
            got = got.transpose(0, 2, 1, 3).reshape(tokens // SUB, SUB, chunk_groups, channels)
            got = got.transpose(0, 2, 1, 3)
        return got.reshape(tokens // SUB, chunk_groups, SUB, channels)

    def give_back(pieces, *after):
        if share % SUB:
            pieces = pieces.transpose(0, 2, 1, 3).reshape(devices, share, chunk_groups, channels)
            pieces = pieces.transpose(0, 2, 1, 3)
        pieces = tie(pieces.reshape(devices, chunk_groups, share, channels), *after)
        return lax.all_to_all(pieces, both, split_axis=0, concat_axis=0, tiled=True)

    def to_tile(arrived):
        if kernels_pack:
            tile = unpack_call(arrived, local_rows, part_rows, tile_cols, row_devs)
            return tile.reshape(tile_rows, tile_cols, channels)
        arrived = [
            part.reshape(row_devs, col_devs, chunk_rows, part_cols, local_rows, local_cols, channels)
            for part in arrived
        ]
        return jnp.concatenate(arrived, axis=2).transpose(4, 0, 2, 5, 3, 1, 6).reshape(
            tile_rows, tile_cols, channels
        )

    arrived = []
    for k, tile in enumerate([activations] * chunks + [cotangent] * chunks):
        sends = pack(tile, k % chunks)
        arrived.append(send(sends, *arrived[-1:]))
    act, cot = arrived[:chunks], arrived[chunks:]
    gain_one, gain_two, joint_t, out_t, up_t, down_t = prepare_call(
        first_gain, second_gain, joint_weight, output_weight, expand_weight, reduce_weight, tokens
    )
    weights = (up_t, down_t, reduce_weight, expand_weight, output_weight)
    hidden_dim = expand_weight.shape[1]
    tail_rows, head_rows = 2 * hidden_dim + channels, 3 * channels
    unit = SUB * devices
    fronts = []
    for k in range(chunks):
        fronts.append(attend_call(act[k], gain_one, joint_t, out_t))
    tails, out_parts, carried = [], [], ()
    before = cot[-1:]
    for k in range(chunks):
        _, _, mixed, _, attended = fronts[k]
        spare = unit - tail_rows % unit if k == chunks - 1 else 0
        tails.append(mlp_call(attended, mixed, cot[k], gain_two, weights, carried, spare))
        carried = tails[-1][3:]
        out_parts.append(give_back(tails[-1][0], *before))
        before = out_parts[-1:]
    steps = stages()
    tail_sum = scatter_sum(carried[0], *steps[0])
    heads, in_parts, carried = [], [], ()
    for k in range(chunks):
        flat, triple, _, stat, _ = fronts[k]
        _, grad_att, grad_mixed = tails[k][:3]
        spare = unit - head_rows % unit if k == chunks - 1 else 0
        grad_mixed = tie(grad_mixed, out_parts[k])
        heads.append(
            back_call(flat, triple, stat, grad_mixed, grad_att, gain_one, joint_weight, cot[k], carried, spare)
        )
        carried = heads[-1][1:]
        in_parts.append(give_back(heads[-1][0], *before))
        before = in_parts[-1:]
        tail_sum = scatter_sum(tail_sum, *steps[k + 1])
    head_sum = carried[0]
    near, cols, rows = steps
    head_sum = scatter_sum(head_sum, *near)
    head_sum = scatter_sum(head_sum, *cols)
    tail_sum = collect(tail_sum, *rows)
    head_sum = share_sum(head_sum, *rows)
    tail_sum = collect(tail_sum, *cols)
    head_sum = collect(head_sum, *cols)
    tail_sum = collect(tail_sum, *near)
    head_sum = collect(head_sum, *near)
    block_out = to_tile(out_parts)
    grad_input = to_tile(in_parts)
    return (
        block_out,
        grad_input,
        head_sum[:head_rows].T.astype(F32) * factor,
        tail_sum[2 * hidden_dim : tail_rows].astype(F32) * factor,
        tail_sum[hidden_dim : 2 * hidden_dim].T.astype(F32) * factor,
        tail_sum[:hidden_dim].astype(F32) * factor,
        head_sum[head_rows].astype(F32) * factor,
        tail_sum[tail_rows].astype(F32) * factor,
    )


def solution(mesh):
    placed = (P("row", "col", None), P("row", "col", None), P(), P(), P(), P(), P(), P())
    return jax.shard_map(shards, mesh=mesh, in_specs=placed, out_specs=placed, check_vma=False)
```
